32 devices in a mesh: seq: 2 (over core), grp: 16 (over z, y, x).
Axes of the slice: x: 2, y: 2, z: 4, core: 2. Of those that a mesh axis runs over, the one named last changes fastest.
Arguments:
- inputs: bfloat16 [2, 16, 1024, 768], P(None, 'grp', 'seq'), may hold values from -6 to 6
- cotangent: bfloat16 [2, 16, 1024, 768], P(None, 'grp', 'seq'), may hold values from -6 to 6
- query_weight: bfloat16 [768, 768], P(('seq', 'grp')), may hold values from -0.3125 to 0.3125
- query_bias: bfloat16 [768], P(('seq', 'grp')), may hold values from -1.5 to 1.5
- key_weight: bfloat16 [768, 768], P(('seq', 'grp')), may hold values from -0.3125 to 0.3125
- value_weight: bfloat16 [768, 768], P(('seq', 'grp')), may hold values from -0.21875 to 0.21875
- value_bias: bfloat16 [768], P(('seq', 'grp')), may hold values from -1.5 to 1.5
- output_weight: bfloat16 [768, 768], P(('seq', 'grp')), may hold values from -1.25 to 1.25
- output_bias: bfloat16 [768], P(('seq', 'grp')), may hold values from -1.5 to 1.5
- first_gain: bfloat16 [768], P(('seq', 'grp')), may hold values from 0.5 to 1.5
- first_shift: bfloat16 [768], P(('seq', 'grp')), may hold values from -1.5 to 1.5
- inner_weight: bfloat16 [768, 3072], P(('seq', 'grp')), may hold values from -0.21875 to 0.21875
- inner_bias: bfloat16 [3072], P(('seq', 'grp')), may hold values from -1.5 to 1.5
- outer_weight: bfloat16 [3072, 768], P(('seq', 'grp')), may hold values from -0.109375 to 0.109375
- outer_bias: bfloat16 [768], P(('seq', 'grp')), may hold values from -1.5 to 1.5
- second_gain: bfloat16 [768], P(('seq', 'grp')), may hold values from 0.5 to 1.5
- second_shift: bfloat16 [768], P(('seq', 'grp')), may hold values from -1.5 to 1.5
Outputs:
- layer_out: bfloat16 [2, 16, 1024, 768], P(None, 'grp', 'seq')
- input_gradient: bfloat16 [2, 16, 1024, 768], P(None, 'grp', 'seq')
- query_weight_gradient: float32 [768, 768], P(('seq', 'grp'))
- query_bias_gradient: float32 [768], P(('seq', 'grp'))
- key_weight_gradient: float32 [768, 768], P(('seq', 'grp'))
- value_weight_gradient: float32 [768, 768], P(('seq', 'grp'))
- value_bias_gradient: float32 [768], P(('seq', 'grp'))
- output_weight_gradient: float32 [768, 768], P(('seq', 'grp'))
- output_bias_gradient: float32 [768], P(('seq', 'grp'))
- first_gain_gradient: float32 [768], P(('seq', 'grp'))
- first_shift_gradient: float32 [768], P(('seq', 'grp'))
- inner_weight_gradient: float32 [768, 3072], P(('seq', 'grp'))
- inner_bias_gradient: float32 [3072], P(('seq', 'grp'))
- outer_weight_gradient: float32 [3072, 768], P(('seq', 'grp'))
- outer_bias_gradient: float32 [768], P(('seq', 'grp'))
- second_gain_gradient: float32 [768], P(('seq', 'grp'))
- second_shift_gradient: float32 [768], P(('seq', 'grp'))
The draws below stay inside these ranges and needn't reach their ends.
All inputs are finite; a program needn't handle non-finite values.
Results may differ from the reference program's by a relative error of at most 0.015.
The reference program's roundings to bfloat16 on the way count: a program that leaves them out, or rounds other values in their place, can miss the bound.
Values may be sent and summed in bfloat16 or wider, within the bound.
A program may use at most 192 MiB of HBM per device.

```python
import jax
import jax.numpy as jnp
from jax import lax

D = 768
HEADS = 12
HEAD_DIM = 64
FF = 3072
MICRO = 2
BLOCK = 512
LENGTH = 1024
SEQS = 16


def strengthened(drawn, rng, source, target, shards_of, factor):
    owner, partner = [(jnp.arange(drawn.shape[dim]) // (drawn.shape[dim] // shards_of)).reshape([-1 if axis == dim else 1 for axis in range(drawn.ndim)]) for dim in (source, target)]
    chosen = jax.random.permutation(rng, shards_of)[partner]
    strong = (owner == chosen) | (owner == (partner + shards_of // 2) % shards_of)
    return jnp.where(strong, factor * drawn, drawn)


def level_of(rng, shape, shards, least, top_value):
    factor_of = 1.0
    for axis_at, parts in shards:
        steps = jax.random.uniform(jax.random.fold_in(jax.random.fold_in(rng, 6), axis_at), (parts,), jnp.float32, least / len(shards), top_value / len(shards))
        factor_of = factor_of * jnp.repeat(jnp.exp(steps), shape[axis_at] // parts).reshape((-1,) + (1,) * (len(shape) - 1 - axis_at))
    return factor_of


def scatter_about(key, shape, deviation, most, cuts=(), dtype=jnp.bfloat16):
    factor_of = level_of(key, shape, cuts, -0.22, 0.18) if cuts else 1.0
    values = jax.random.normal(key, shape, jnp.float32) * deviation * factor_of
    return jnp.minimum(jnp.maximum(values, -most), most).astype(dtype)


def bell_draw_with(stream_key, extent, spread, reach, cuts, heavy, held_as=jnp.bfloat16):
    array = spread * jax.random.normal(stream_key, extent, jnp.float32)
    if cuts:
        array = array * level_of(stream_key, extent, cuts, -0.22, 0.18)
    return jnp.clip(strengthened(array, jax.random.fold_in(stream_key, 3), *heavy), -reach, reach).astype(held_as)


def setup_inputs(seed: int = 0) -> dict:
    arg_keys = jax.random.split(jax.random.key(seed), 18)
    return {
        "inputs": bell_draw_with(arg_keys[0], (MICRO, SEQS, LENGTH, D), 1.0, 6.0, ((1, 16), (2, 2)), (1, 3, 16, 2.0)),
        "cotangent": bell_draw_with(arg_keys[1], (MICRO, SEQS, LENGTH, D), 1.0, 6.0, ((1, 16), (2, 2)), (1, 3, 16, 2.0)),
        "query_weight": scatter_about(arg_keys[2], (D, D), (D // 2) ** -0.5, 0.3125, ((0, 32),)),
        "query_bias": scatter_about(arg_keys[3], (D,), 0.3, 1.5, ((0, 32),)),
        "key_weight": scatter_about(arg_keys[4], (D, D), (D // 2) ** -0.5, 0.3125, ((0, 32),)),
        "value_weight": scatter_about(arg_keys[5], (D, D), D ** -0.5, 0.21875, ((0, 32),)),
        "value_bias": scatter_about(arg_keys[6], (D,), 0.3, 1.5, ((0, 32),)),
        "output_weight": scatter_about(arg_keys[7], (D, D), (D // 32) ** -0.5, 1.25, ((0, 32),)),
        "output_bias": scatter_about(arg_keys[8], (D,), 0.3, 1.5, ((0, 32),)),
        "first_gain": jnp.clip(1.0 + 0.1 * jax.random.normal(arg_keys[9], (D,), jnp.float32), 0.5, 1.5).astype(jnp.bfloat16),
        "first_shift": scatter_about(arg_keys[10], (D,), 0.3, 1.5, ((0, 32),)),
        "inner_weight": scatter_about(arg_keys[11], (D, FF), D ** -0.5, 0.21875, ((0, 32),)),
        "inner_bias": scatter_about(arg_keys[12], (FF,), 0.3, 1.5, ((0, 32),)),
        "outer_weight": scatter_about(arg_keys[13], (FF, D), FF ** -0.5, 0.109375, ((0, 32),)),
        "outer_bias": scatter_about(arg_keys[14], (D,), 0.3, 1.5, ((0, 32),)),
        "second_gain": jnp.clip(1.0 + 0.1 * jax.random.normal(arg_keys[15], (D,), jnp.float32), 0.5, 1.5).astype(jnp.bfloat16),
        "second_shift": scatter_about(arg_keys[16], (D,), 0.3, 1.5, ((0, 32),)),
    }


@jax.custom_vjp
def low(v):
    return lax.optimization_barrier(v.astype(jnp.bfloat16)).astype(jnp.float32)

@jax.custom_vjp
def low_back(v):
    return v

def low_keep(v):
    return (low(v), None)

def low_pass(kept, grad):
    return (grad,)

def back_keep(v):
    return (v, None)

def back_low(kept, grad):
    return (low(grad),)
low.defvjp(low_keep, low_pass)
low_back.defvjp(back_keep, back_low)
HIGHEST = lax.Precision.HIGHEST

def norm_rows(rows, gain, shift):
    average = lax.optimization_barrier(jnp.mean(rows, axis=-1, keepdims=True))
    centred = rows - average
    variance = lax.optimization_barrier(jnp.mean(centred * centred, axis=-1, keepdims=True))
    return centred * lax.rsqrt(variance + 1e-05) * gain + shift

def attend_block(query_block, keys, values):
    scores = low_back(jnp.einsum('qhd,khd->hqk', query_block, keys, precision=HIGHEST) * 0.125)
    probs = low(jax.nn.softmax(scores, axis=-1))
    return jnp.einsum('hqk,khd->qhd', probs, values, precision=HIGHEST)

def layer(tokens, params):
    query_weight, query_bias, key_weight, value_weight, value_bias, output_weight, output_bias, first_gain, first_shift, inner_weight, inner_bias, outer_weight, outer_bias, second_gain, second_shift = params
    queries = low_back(low(jnp.dot(tokens, query_weight, precision=HIGHEST) + query_bias))
    keys = low_back(low(jnp.dot(tokens, key_weight, precision=HIGHEST)))
    values = low_back(low(jnp.dot(tokens, value_weight, precision=HIGHEST) + value_bias))
    queries = queries.reshape(LENGTH, HEADS, HEAD_DIM)
    keys = keys.reshape(LENGTH, HEADS, HEAD_DIM)
    values = values.reshape(LENGTH, HEADS, HEAD_DIM)
    blocks = queries.reshape(LENGTH // BLOCK, BLOCK, HEADS, HEAD_DIM)

    def attend(query_block):
        return attend_block(query_block, keys, values)
    mixed = lax.map(jax.checkpoint(attend), blocks)
    attended = low_back(low(mixed.reshape(LENGTH, D)))
    branch = low_back(jnp.dot(attended, output_weight, precision=HIGHEST) + output_bias)
    hidden = norm_rows(tokens + branch, first_gain, first_shift)
    hidden_low = low(hidden)
    inner = low_back(jnp.dot(hidden_low, inner_weight, precision=HIGHEST) + inner_bias)
    active = low(jax.nn.gelu(inner, approximate=True))
    feed = low_back(jnp.dot(active, outer_weight, precision=HIGHEST) + outer_bias)
    return norm_rows(hidden + feed, second_gain, second_shift)

def reference(inputs, cotangent, query_weight, query_bias, key_weight, value_weight, value_bias, output_weight, output_bias, first_gain, first_shift, inner_weight, inner_bias, outer_weight, outer_bias, second_gain, second_shift):
    params = tuple((piece.astype(jnp.float32) for piece in (query_weight, query_bias, key_weight, value_weight, value_bias, output_weight, output_bias, first_gain, first_shift, inner_weight, inner_bias, outer_weight, outer_bias, second_gain, second_shift)))
    flat = inputs.astype(jnp.float32).reshape(MICRO * SEQS, LENGTH, D)

    def forward(flat_in, weights):

        def one_sequence(sequence):
            return layer(sequence, weights)
        return lax.map(jax.checkpoint(one_sequence), flat_in)
    result, pullback = jax.vjp(forward, flat, params)
    input_part, grads = pullback(cotangent.astype(jnp.float32).reshape(MICRO * SEQS, LENGTH, D))
    return (result.reshape(inputs.shape).astype(jnp.bfloat16), input_part.reshape(inputs.shape).astype(jnp.bfloat16), grads[0], grads[1], grads[2], grads[3], grads[4], grads[5], grads[6], grads[7], grads[8], grads[9], grads[10], grads[11], grads[12], grads[13], grads[14])
```

```python
import functools

import jax
import jax.numpy as jnp
from jax import lax
from jax.experimental import pallas as pl
from jax.experimental.pallas import tpu as pltpu
from jax.sharding import PartitionSpec as P

HEADS = 12
SCALE = 0.125
EPS = 1e-05
PAIR = 128
ROWS = 256
CHUNK = 768
LANES = 128
VMEM_LIMIT = 64 * 1024 * 1024 - 65536
GELU_C = 0.7978845608028654
GELU_A = 0.044715
MESH = pl.DeviceIdType.MESH
F32 = jnp.float32
BF16 = jnp.bfloat16


def dot_nn(left, right):
    return lax.dot_general(left, right, (((1,), (0,)), ((), ())), preferred_element_type=F32)


def dot_nt(left, right):
    return lax.dot_general(left, right, (((1,), (1,)), ((), ())), preferred_element_type=F32)


def dot_tn(left, right):
    return lax.dot_general(left, right, (((0,), (0,)), ((), ())), preferred_element_type=F32)


def place():
    s = lax.axis_index("seq")
    g = lax.axis_index("grp")
    return s, g // 4, (g // 2) % 2, g % 2


def device(s, z, y, x):
    return (s, z * 4 + y * 2 + x)


def first_partner(s, z, y, x):
    return device(s, z, y * s + (1 - y) * (1 - s), x * (1 - s) + (1 - x) * s)


def second_partner(s, z, y, x):
    return device(s, z, y * (1 - s) + (1 - y) * s, x * s + (1 - x) * (1 - s))


def greet(s, z, y, x):
    barrier = pltpu.get_barrier_semaphore()
    partners = [device(1 - s, z, y, x), first_partner(s, z, y, x), second_partner(s, z, y, x)]
    partners += [device(s, (z + k) % 4, y, x) for k in (1, 2, 3)]
    for partner in partners:
        pl.semaphore_signal(barrier, inc=1, device_id=partner, device_id_type=MESH)
    pl.semaphore_wait(barrier, len(partners))


def remote(src, dst, send, recv, target):
    return pltpu.make_async_remote_copy(
        src_ref=src, dst_ref=dst, send_sem=send, recv_sem=recv, device_id=target, device_id_type=MESH
    )


def gather_kernel(count, *refs):
    shards = refs[:count]
    rows = refs[count]
    fulls = refs[count + 1 : 2 * count + 1]
    all_rows = refs[2 * count + 1]
    own_sem, send, recv, row_own, row_send, row_recv = refs[2 * count + 2 :]
    s, z, y, x = place()
    greet(s, z, y, x)

    def own(a):
        return pltpu.make_async_copy(shards[a], fulls[a].at[s, z, y, x], own_sem.at[a])

    def along_z(a, k):
        return remote(
            shards[a],
            fulls[a].at[s, z, y, x],
            send.at[a, k - 1],
            recv.at[a, k - 1],
            device(s, (z + k) % 4, y, x),
        )

    def first(a):
        part = fulls[a].at[s, :, y, x]
        return remote(part, part, send.at[a, 3], recv.at[a, 3], second_partner(s, z, y, x))

    def second(a, j):
        yy = y * (1 - s) + j * s
        xx = j * (1 - s) + x * s
        part = fulls[a].at[s, :, yy, xx]
        return remote(part, part, send.at[a, 4 + j], recv.at[a, 4 + j], first_partner(s, z, y, x))

    def across(a):
        part = fulls[a].at[s]
        return remote(part, part, send.at[a, 6], recv.at[a, 6], device(1 - s, z, y, x))

    row_copy = remote(rows, all_rows.at[s], row_send, row_recv, device(1 - s, z, y, x))
    row_local = pltpu.make_async_copy(rows, all_rows.at[s], row_own)

    def stage(t, a):
        if t == 0:
            for k in (1, 2, 3):
                along_z(a, k).start()
            own(a).start()
        elif t == 1:
            own(a).wait()
            for k in (1, 2, 3):
                along_z(a, k).wait_recv()
            first(a).start()
        elif t == 2:
            first(a).wait_recv()
            for j in (0, 1):
                second(a, j).start()
        elif t == 3:
            for j in (0, 1):
                second(a, j).wait_recv()
            across(a).start()

    for a in range(count):
        stage(0, a)
    row_copy.start()
    row_local.start()
    for i in range(1, count + 3):
        for t in (3, 2, 1):
            a = i - t
            if 0 <= a < count:
                stage(t, a)
    for a in range(count):
        across(a).wait_recv()
    row_local.wait()
    row_copy.wait()
    for a in range(count):
        for k in (1, 2, 3):
            along_z(a, k).wait_send()
        first(a).wait_send()
        for j in (0, 1):
            second(a, j).wait_send()
        across(a).wait_send()


def gather_box(shards, rows):
    count = len(shards)
    any_spec = pl.BlockSpec(memory_space=pl.ANY)
    vmem_spec = pl.BlockSpec(memory_space=pltpu.VMEM)
    outs = pl.pallas_call(
        functools.partial(gather_kernel, count),
        out_shape=[jax.ShapeDtypeStruct((2, 4, 2, 2) + a.shape, a.dtype) for a in shards]
        + [jax.ShapeDtypeStruct((2,) + rows.shape, rows.dtype)],
        in_specs=[vmem_spec] * (count + 1),
        out_specs=[any_spec] * (count + 1),
        scratch_shapes=[
            pltpu.SemaphoreType.DMA((count,)),
            pltpu.SemaphoreType.DMA((count, 7)),
            pltpu.SemaphoreType.DMA((count, 7)),
            pltpu.SemaphoreType.DMA,
            pltpu.SemaphoreType.DMA,
            pltpu.SemaphoreType.DMA,
        ],
        compiler_params=pltpu.CompilerParams(
            collective_id=1, has_side_effects=True, vmem_limit_bytes=VMEM_LIMIT
        ),
        name="gather_weights",
    )(*shards, rows)
    fulls = [full.reshape((-1, full.shape[-1])) for full in outs[:-1]]
    return fulls, outs[-1]


def scatter_kernel(count, *refs):
    terms = refs[:count]
    outs = refs[count : 2 * count]
    scratch = refs[2 * count :]
    held = scratch[:count]
    got1 = scratch[count : 2 * count]
    got2 = scratch[2 * count : 3 * count]
    got3 = scratch[3 * count : 4 * count]
    got4 = scratch[4 * count : 5 * count]
    load, send, recv = scratch[5 * count :]
    s, z, y, x = place()
    greet(s, z, y, x)
    y2 = y * (1 - s) + (1 - y) * s
    x2 = (1 - x) * (1 - s) + x * s

    def fetch(a):
        return pltpu.make_async_copy(terms[a].at[s], held[a], load.at[a])

    def across(a):
        return remote(
            terms[a].at[1 - s], got1[a], send.at[a, 0], recv.at[a, 0], device(1 - s, z, y, x)
        )

    def first(a, j):
        yy = (1 - y) * (1 - s) + j * s
        xx = j * (1 - s) + (1 - x) * s
        return remote(
            held[a].at[:, yy, xx],
            got2[a].at[:, j],
            send.at[a, 1 + j],
            recv.at[a, 1 + j],
            first_partner(s, z, y, x),
        )

    def second(a):
        return remote(
            held[a].at[:, y2, x2],
            got3[a],
            send.at[a, 3],
            recv.at[a, 3],
            second_partner(s, z, y, x),
        )

    def along_z(a, k):
        zt = (z + k) % 4
        return remote(
            held[a].at[zt, y, x],
            got4[a].at[k - 1],
            send.at[a, 3 + k],
            recv.at[a, 3 + k],
            device(s, zt, y, x),
        )

    def stage(t, a):
        if t == 0:
            across(a).start()
            fetch(a).start()
        elif t == 1:
            fetch(a).wait()
            across(a).wait_recv()

            def add1(i, unused):
                zz, yy, xx = i // 4, (i // 2) % 2, i % 2
                held[a][zz, yy, xx] = (
                    held[a][zz, yy, xx].astype(F32) + got1[a][zz, yy, xx].astype(F32)
                ).astype(BF16)
                return unused

            lax.fori_loop(0, 16, add1, 0)
            for j in (0, 1):
                first(a, j).start()
        elif t == 2:
            for j in (0, 1):
                first(a, j).wait_recv()

            def add2(i, unused):
                zz, j = i // 2, i % 2
                yy = y * (1 - s) + j * s
                xx = j * (1 - s) + x * s
                held[a][zz, yy, xx] = (
                    held[a][zz, yy, xx].astype(F32) + got2[a][zz, j].astype(F32)
                ).astype(BF16)
                return unused

            lax.fori_loop(0, 8, add2, 0)
            second(a).start()
        elif t == 3:
            second(a).wait_recv()

            def add3(zz, unused):
                held[a][zz, y, x] = (
                    held[a][zz, y, x].astype(F32) + got3[a][zz].astype(F32)
                ).astype(BF16)
                return unused

            lax.fori_loop(0, 4, add3, 0)
            for k in (1, 2, 3):
                along_z(a, k).start()
        elif t == 4:
            for k in (1, 2, 3):
                along_z(a, k).wait_recv()
            outs[a][...] = (
                held[a][z, y, x].astype(F32)
                + got4[a][0].astype(F32)
                + got4[a][1].astype(F32)
                + got4[a][2].astype(F32)
            )

    for i in range(count + 4):
        for t in (4, 3, 2, 1, 0):
            a = i - t
            if 0 <= a < count:
                stage(t, a)
    for a in range(count):
        across(a).wait_send()
        for j in (0, 1):
            first(a, j).wait_send()
        second(a).wait_send()
        for k in (1, 2, 3):
            along_z(a, k).wait_send()


def scatter_box(terms):
    count = len(terms)
    any_spec = pl.BlockSpec(memory_space=pl.ANY)
    vmem_spec = pl.BlockSpec(memory_space=pltpu.VMEM)
    sizes = [(term.shape[0] // 32, term.shape[1]) for term in terms]
    shaped = [term.reshape((2, 4, 2, 2) + size) for term, size in zip(terms, sizes)]
    scratch = []
    for lead in ((4, 2, 2), (4, 2, 2), (4, 2), (4,), (3,)):
        scratch += [pltpu.VMEM(lead + size, BF16) for size in sizes]
    scratch += [
        pltpu.SemaphoreType.DMA((count,)),
        pltpu.SemaphoreType.DMA((count, 7)),
        pltpu.SemaphoreType.DMA((count, 7)),
    ]
    return pl.pallas_call(
        functools.partial(scatter_kernel, count),
        out_shape=[jax.ShapeDtypeStruct(size, F32) for size in sizes],
        in_specs=[any_spec] * count,
        out_specs=[vmem_spec] * count,
        scratch_shapes=scratch,
        compiler_params=pltpu.CompilerParams(
            collective_id=2, has_side_effects=True, vmem_limit_bytes=VMEM_LIMIT
        ),
        name="scatter_gradients",
    )(*shaped)


def project_kernel(own_ref, all_ref, wq_ref, wk_ref, wv_ref, vec_ref, q_ref, kv_ref, bias):
    width = wq_ref.shape[1]
    micro = 2

    @pl.when(pl.program_id(0) == 0)
    def _():
        bias[...] = jnp.transpose(vec_ref[...].astype(F32))[:8]

    @pl.when(pl.program_id(0) < micro)
    def _():
        queries = dot_nn(own_ref[0], wq_ref[...]) + bias[0:1]
        q_ref[0] = (queries.astype(BF16).astype(F32) * SCALE).astype(BF16)

    rows = all_ref[0, 0]
    kv_ref[0, 0, :, :width] = dot_nn(rows, wk_ref[...]).astype(BF16)
    kv_ref[0, 0, :, width:] = (dot_nn(rows, wv_ref[...]) + bias[1:2]).astype(BF16)


def project(own, all_rows, wq, wk, wv, vec):
    micro, length, width = own.shape
    parts = all_rows.shape[0]
    whole = lambda a: pl.BlockSpec(a.shape, lambda i: (0,) * a.ndim)
    last = micro - 1
    return pl.pallas_call(
        project_kernel,
        grid=(parts * micro,),
        in_specs=[
            pl.BlockSpec((1, length, width), lambda i: (jnp.minimum(i, last), 0, 0)),
            pl.BlockSpec((1, 1, length, width), lambda i: (i // micro, i % micro, 0, 0)),
            whole(wq),
            whole(wk),
            whole(wv),
            whole(vec),
        ],
        out_specs=[
            pl.BlockSpec((1, length, width), lambda i: (jnp.minimum(i, last), 0, 0)),
            pl.BlockSpec((1, 1, length, 2 * width), lambda i: (i // micro, i % micro, 0, 0)),
        ],
        out_shape=[
            jax.ShapeDtypeStruct((micro, length, width), BF16),
            jax.ShapeDtypeStruct((parts, micro, length, 2 * width), BF16),
        ],
        scratch_shapes=[pltpu.VMEM((8, width), F32)],
        compiler_params=pltpu.CompilerParams(vmem_limit_bytes=VMEM_LIMIT),
        name="project",
    )(own, all_rows, wq, wk, wv, vec)


def head_of(shape):
    return lax.broadcasted_iota(jnp.int32, shape, len(shape) - 1) // 64


def pick(values, head):
    return jnp.where(head_of(values.shape) == head, values, jnp.zeros_like(values))


def attend_kernel(q_ref, k_ref, v_ref, o_ref, lse_ref):
    queries = q_ref[0]
    length = queries.shape[0]
    keys = k_ref[:, 0].reshape(-1, PAIR)
    values = v_ref[:, 0].reshape(-1, PAIR)
    mixed = []
    for head in (0, 1):
        scores = dot_nt(pick(queries, head), keys)
        top = jnp.max(scores, axis=1, keepdims=True)
        powers = jnp.exp(scores - top)
        total = jnp.sum(powers, axis=1, keepdims=True)
        mixed.append(dot_nn(powers.astype(BF16), values) * (1.0 / total))
        column = jnp.broadcast_to(top + jnp.log(total), (length, LANES))
        lse_ref[0, 0, head : head + 1, :] = jnp.transpose(column)[0:1]
    o_ref[0] = jnp.where(head_of(mixed[0].shape) == 0, mixed[0], mixed[1]).astype(BF16)


def attend(queries, kv):
    micro, length, width = queries.shape
    parts = kv.shape[0]
    pairs = width // PAIR
    return pl.pallas_call(
        attend_kernel,
        grid=(micro, pairs),
        in_specs=[
            pl.BlockSpec((1, length, PAIR), lambda m, p: (m, 0, p)),
            pl.BlockSpec((parts, 1, length, PAIR), lambda m, p: (0, m, 0, p)),
            pl.BlockSpec((parts, 1, length, PAIR), lambda m, p: (0, m, 0, pairs + p)),
        ],
        out_specs=[
            pl.BlockSpec((1, length, PAIR), lambda m, p: (m, 0, p)),
            pl.BlockSpec((1, 1, 2, length), lambda m, p: (m, p, 0, 0)),
        ],
        out_shape=[
            jax.ShapeDtypeStruct(queries.shape, BF16),
            jax.ShapeDtypeStruct((micro, pairs, 2, length), F32),
        ],
        compiler_params=pltpu.CompilerParams(vmem_limit_bytes=VMEM_LIMIT),
        name="attend",
    )(queries, kv, kv)


def attend_back_kernel(q_ref, k_ref, v_ref, o_ref, g_ref, lse_ref, dq_ref, dk_ref, dv_ref):
    parts = k_ref.shape[0]
    queries = q_ref[0]
    length = queries.shape[0]
    keys = k_ref[:, 0].reshape(-1, PAIR)
    values = v_ref[:, 0].reshape(-1, PAIR)
    grad = g_ref[0]
    keys_t = jnp.transpose(keys)
    products = jnp.transpose(grad.astype(F32) * o_ref[0].astype(F32))
    dk = jnp.zeros(keys.shape, F32)
    dv = jnp.zeros(keys.shape, F32)
    dq_t = []
    for head in (0, 1):
        offset = jnp.sum(products[64 * head : 64 * head + 64], axis=0, keepdims=True)
        q_head = pick(queries, head)
        g_head = pick(grad, head)
        scores_t = dot_nt(keys, q_head)
        probs_t = jnp.exp(scores_t - lse_ref[0, 0, head : head + 1, :])
        slopes_t = dot_nt(values, g_head)
        score_grad_t = (probs_t * (slopes_t - offset)).astype(BF16)
        dv += dot_nn(probs_t.astype(BF16), g_head)
        dk += dot_nn(score_grad_t, q_head)
        dq_t.append(dot_nn(keys_t[64 * head : 64 * head + 64], score_grad_t))
    dq = jnp.transpose(jnp.concatenate(dq_t, axis=0)) * SCALE
    dq_ref[0] = dq.astype(BF16)
    dk_ref[:, 0] = dk.astype(BF16).reshape(parts, length, PAIR)
    dv_ref[:, 0] = dv.astype(BF16).reshape(parts, length, PAIR)


def attend_back(queries, kv, attended, grad, lse):
    micro, length, width = queries.shape
    parts = kv.shape[0]
    pairs = width // PAIR
    row = pl.BlockSpec((1, length, PAIR), lambda m, p: (m, 0, p))
    col = pl.BlockSpec((parts, 1, length, PAIR), lambda m, p: (0, m, 0, p))
    col2 = pl.BlockSpec((parts, 1, length, PAIR), lambda m, p: (0, m, 0, pairs + p))
    return pl.pallas_call(
        attend_back_kernel,
        grid=(micro, pairs),
        in_specs=[
            row,
            col,
            col2,
            row,
            row,
            pl.BlockSpec((1, 1, 2, length), lambda m, p: (m, p, 0, 0)),
        ],
        out_specs=[row, col, col],
        out_shape=[
            jax.ShapeDtypeStruct((micro, length, width), BF16),
            jax.ShapeDtypeStruct((parts, micro, length, width), BF16),
            jax.ShapeDtypeStruct((parts, micro, length, width), BF16),
        ],
        compiler_params=pltpu.CompilerParams(vmem_limit_bytes=VMEM_LIMIT),
        name="attend_back",
    )(queries, kv, kv, attended, grad, lse)


def mean_rows(values):
    return jnp.mean(values, axis=-1, keepdims=True)


def rows_kernel(
    x_ref,
    att_ref,
    cot_ref,
    wo_ref,
    win_ref,
    wout_ref,
    vec_ref,
    ib_ref,
    out_ref,
    hidden_ref,
    active_ref,
    inner_grad_ref,
    feed_ref,
    branch_ref,
    mixed_ref,
    first_ref,
    vecg_ref,
    ibg_ref,
    vec,
    ib,
    slope,
    vecg,
    ibg,
):
    step = pl.program_id(0)
    chunks = win_ref.shape[1] // CHUNK

    @pl.when(step == 0)
    def _():
        vec[...] = jnp.transpose(vec_ref[...].astype(F32))[:8]
        ib[...] = jnp.transpose(ib_ref[...].astype(F32))[:8]
        vecg[...] = jnp.zeros_like(vecg)
        ibg[...] = jnp.zeros_like(ibg)

    o_b, g1, s1, outer_b, g2, s2 = (vec[i : i + 1] for i in range(2, 8))
    first_sum = x_ref[...].astype(F32) + (dot_nn(att_ref[...], wo_ref[...]) + o_b)
    centred = first_sum - mean_rows(first_sum)
    r1 = lax.rsqrt(mean_rows(centred * centred) + EPS)
    n1 = centred * r1
    hidden = n1 * g1 + s1
    hidden_low = hidden.astype(BF16)
    hidden_ref[...] = hidden_low
    total = hidden + outer_b
    for c in range(chunks):
        cols = slice(c * CHUNK, (c + 1) * CHUNK)
        v = dot_nn(hidden_low, win_ref[:, cols]) + ib[0:1, cols]
        square = v * v
        t = jnp.tanh(v * (GELU_C + (GELU_C * GELU_A) * square))
        half = 0.5 * (1.0 + t)
        active = (v * half).astype(BF16)
        active_ref[:, cols] = active
        slope[:, cols] = half + (0.5 * v) * (1.0 - t * t) * (
            GELU_C + (3.0 * GELU_C * GELU_A) * square
        )
        total = total + dot_nn(active, wout_ref[cols, :])
    centred = total - mean_rows(total)
    r2 = lax.rsqrt(mean_rows(centred * centred) + EPS)
    n2 = centred * r2
    out_ref[...] = (n2 * g2 + s2).astype(BF16)
    e = cot_ref[...].astype(F32)
    m = e * g2
    second = (m - mean_rows(m) - n2 * mean_rows(m * n2)) * r2
    feed = second.astype(BF16)
    feed_ref[...] = feed
    vecg[6:7] += jnp.sum(e * n2, axis=0, keepdims=True)
    vecg[7:8] += jnp.sum(e, axis=0, keepdims=True)
    vecg[5:6] += jnp.sum(feed.astype(F32), axis=0, keepdims=True)
    e = second
    for c in range(chunks):
        cols = slice(c * CHUNK, (c + 1) * CHUNK)
        inner_grad = (dot_nt(feed, wout_ref[cols, :]) * slope[:, cols]).astype(BF16)
        inner_grad_ref[:, cols] = inner_grad
        ibg[0:1, cols] += jnp.sum(inner_grad.astype(F32), axis=0, keepdims=True)
        e = e + dot_nt(inner_grad, win_ref[:, cols])
    m = e * g1
    first = (m - mean_rows(m) - n1 * mean_rows(m * n1)) * r1
    first_ref[...] = first
    branch = first.astype(BF16)
    branch_ref[...] = branch
    vecg[3:4] += jnp.sum(e * n1, axis=0, keepdims=True)
    vecg[4:5] += jnp.sum(e, axis=0, keepdims=True)
    vecg[2:3] += jnp.sum(branch.astype(F32), axis=0, keepdims=True)
    mixed_ref[...] = dot_nt(branch, wo_ref[...]).astype(BF16)

    @pl.when(step == pl.num_programs(0) - 1)
    def _():
        vecg_ref[...] = jnp.transpose(vecg[...]).astype(BF16)
        ibg_ref[...] = jnp.transpose(ibg[...]).astype(BF16)


def row_stage(x, attended, cotangent, wo, win, wout, vec, ib):
    rows, width = x.shape
    hidden_width = win.shape[1]
    block = min(ROWS, rows)
    whole = lambda a: pl.BlockSpec(a.shape, lambda i: (0, 0), pipeline_mode=pl.Buffered(1))
    narrow = pl.BlockSpec((block, width), lambda i: (i, 0))
    wide = pl.BlockSpec((block, hidden_width), lambda i: (i, 0))
    low = jax.ShapeDtypeStruct((rows, width), BF16)
    low_wide = jax.ShapeDtypeStruct((rows, hidden_width), BF16)
    return pl.pallas_call(
        rows_kernel,
        grid=(rows // block,),
        in_specs=[narrow] * 3 + [whole(a) for a in (wo, win, wout, vec, ib)],
        out_specs=[
            narrow,
            narrow,
            wide,
            wide,
            narrow,
            narrow,
            narrow,
            narrow,
            pl.BlockSpec(vec.shape, lambda i: (0, 0)),
            pl.BlockSpec(ib.shape, lambda i: (0, 0)),
        ],
        out_shape=[
            low,
            low,
            low_wide,
            low_wide,
            low,
            low,
            low,
            jax.ShapeDtypeStruct((rows, width), F32),
            jax.ShapeDtypeStruct(vec.shape, BF16),
            jax.ShapeDtypeStruct(ib.shape, BF16),
        ],
        scratch_shapes=[
            pltpu.VMEM((8, width), F32),
            pltpu.VMEM((8, hidden_width), F32),
            pltpu.VMEM((block, hidden_width), F32),
            pltpu.VMEM((LANES, width), F32),
            pltpu.VMEM((LANES, hidden_width), F32),
        ],
        compiler_params=pltpu.CompilerParams(vmem_limit_bytes=VMEM_LIMIT),
        name="row_stage",
    )(x, attended, cotangent, wo, win, wout, vec, ib)


def product_kernel(left_ref, right_ref, out_ref):
    out_ref[...] = dot_tn(left_ref[...], right_ref[...]).astype(BF16)


def product(left, right, block_m, block_n):
    depth, rows = left.shape
    cols = right.shape[1]
    return pl.pallas_call(
        product_kernel,
        grid=(rows // block_m, cols // block_n),
        in_specs=[
            pl.BlockSpec((depth, block_m), lambda i, j: (0, i)),
            pl.BlockSpec((depth, block_n), lambda i, j: (0, j)),
        ],
        out_specs=pl.BlockSpec((block_m, block_n), lambda i, j: (i, j)),
        out_shape=jax.ShapeDtypeStruct((rows, cols), BF16),
        compiler_params=pltpu.CompilerParams(vmem_limit_bytes=VMEM_LIMIT),
        name="weight_gradient",
    )(left, right)


def input_kernel(first_ref, dq_ref, dk_ref, dv_ref, wq_ref, wk_ref, wv_ref, out_ref, vecg_ref, acc):
    step = pl.program_id(0)

    @pl.when(step == 0)
    def _():
        acc[...] = jnp.zeros_like(acc)

    out_ref[...] = (
        first_ref[...]
        + dot_nt(dq_ref[...], wq_ref[...])
        + dot_nt(dk_ref[...], wk_ref[...])
        + dot_nt(dv_ref[...], wv_ref[...])
    ).astype(BF16)
    acc[0:1] += jnp.sum(dq_ref[...].astype(F32), axis=0, keepdims=True)
    acc[1:2] += jnp.sum(dv_ref[...].astype(F32), axis=0, keepdims=True)

    @pl.when(step == pl.num_programs(0) - 1)
    def _():
        vecg_ref[...] = jnp.transpose(acc[...]).astype(BF16)


def input_stage(first, dq, dk, dv, wq, wk, wv):
    rows, width = first.shape
    block = min(ROWS, rows)
    narrow = pl.BlockSpec((block, width), lambda i: (i, 0))
    whole = pl.BlockSpec((width, width), lambda i: (0, 0))
    return pl.pallas_call(
        input_kernel,
        grid=(rows // block,),
        in_specs=[narrow] * 4 + [whole] * 3,
        out_specs=[narrow, pl.BlockSpec((width, LANES), lambda i: (0, 0))],
        out_shape=[
            jax.ShapeDtypeStruct((rows, width), BF16),
            jax.ShapeDtypeStruct((width, LANES), BF16),
        ],
        scratch_shapes=[pltpu.VMEM((LANES, width), F32)],
        compiler_params=pltpu.CompilerParams(vmem_limit_bytes=VMEM_LIMIT),
        name="input_stage",
    )(first, dq, dk, dv, wq, wk, wv)


def body(
    inputs,
    cotangent,
    query_weight,
    query_bias,
    key_weight,
    value_weight,
    value_bias,
    output_weight,
    output_bias,
    first_gain,
    first_shift,
    inner_weight,
    inner_bias,
    outer_weight,
    outer_bias,
    second_gain,
    second_shift,
):
    micro, _, length, width = inputs.shape
    parts = lax.axis_size("seq")
    boxed = parts == 2 and lax.axis_size("grp") == 16 and query_weight.shape[0] % 8 == 0
    own = inputs[:, 0]
    tokens = own.reshape(-1, width)
    vectors = jnp.stack(
        (
            query_bias,
            value_bias,
            output_bias,
            first_gain,
            first_shift,
            outer_bias,
            second_gain,
            second_shift,
        ),
        axis=1,
    )
    vectors = jnp.pad(vectors, ((0, 0), (0, LANES - vectors.shape[1])))
    inner_column = jnp.pad(inner_bias[:, None], ((0, 0), (0, LANES - 1)))
    shards = (
        query_weight,
        key_weight,
        value_weight,
        vectors,
        output_weight,
        inner_weight,
        inner_column,
        outer_weight,
    )
    if boxed:
        fulls, all_rows = gather_box(shards, own)
    else:
        fulls = [lax.all_gather(a, ("seq", "grp"), axis=0, tiled=True) for a in shards]
        all_rows = lax.all_gather(own, "seq", axis=0)
    wq, wk, wv, vec, wo, win, ib, wout = fulls

    queries, kv = project(own, all_rows, wq, wk, wv, vec)
    attended, lse = attend(queries, kv)
    flat = attended.reshape(-1, width)
    (
        layer_out,
        hidden_low,
        active,
        inner_grad,
        feed_grad,
        branch_grad,
        mixed_grad,
        first_grad,
        vec_grad,
        ib_grad,
    ) = row_stage(tokens, flat, cotangent[:, 0].reshape(-1, width), wo, win, wout, vec, ib)
    wout_grad = product(active, feed_grad, 768, 768)
    win_grad = product(hidden_low, inner_grad, 768, 768)
    wo_grad = product(flat, branch_grad, 768, 768)
    dq, dk, dv = attend_back(queries, kv, attended, mixed_grad.reshape(micro, length, width), lse)
    if boxed:
        s = lax.axis_index("seq")
        flip = [(0, 1), (1, 0)]

        def joined(terms):
            mine = lax.dynamic_index_in_dim(terms, s, 0, keepdims=False)
            other = lax.ppermute(
                lax.dynamic_index_in_dim(terms, 1 - s, 0, keepdims=False), "seq", flip
            )
            return (mine.astype(F32) + other.astype(F32)).astype(BF16)

        dk, dv = joined(dk), joined(dv)
    else:
        dk = lax.psum_scatter(dk, "seq", scatter_dimension=0)
        dv = lax.psum_scatter(dv, "seq", scatter_dimension=0)
    dq, dk, dv = (a.reshape(-1, width) for a in (dq, dk, dv))
    wq_grad = product(tokens, dq, 768, 768)
    wk_grad = product(tokens, dk, 768, 768)
    wv_grad = product(tokens, dv, 768, 768)
    input_grad, vec2_grad = input_stage(first_grad, dq, dk, dv, wq, wk, wv)

    terms = (wout_grad, ib_grad, win_grad, wo_grad, vec_grad, wq_grad, wk_grad, wv_grad, vec2_grad)
    if boxed:
        summed = scatter_box(terms)
    else:
        summed = [
            lax.psum_scatter(a.astype(F32), ("seq", "grp"), scatter_dimension=0, tiled=True)
            for a in terms
        ]
        summed = lax.optimization_barrier(summed)
    wout_s, ib_s, win_s, wo_s, vec_s, wq_s, wk_s, wv_s, vec2_s = summed
    return (
        layer_out.reshape(inputs.shape),
        input_grad.reshape(inputs.shape),
        wq_s,
        vec2_s[:, 0],
        wk_s,
        wv_s,
        vec2_s[:, 1],
        wo_s,
        vec_s[:, 2],
        vec_s[:, 3],
        vec_s[:, 4],
        win_s,
        ib_s[:, 0],
        wout_s,
        vec_s[:, 5],
        vec_s[:, 6],
        vec_s[:, 7],
    )


def solution(mesh):
    rows = P(("seq", "grp"), None)
    line = P(("seq", "grp"))
    tokens = P(None, "grp", "seq", None)
    return jax.shard_map(
        body,
        mesh=mesh,
        in_specs=(
            tokens,
            tokens,
            rows,
            line,
            rows,
            rows,
            line,
            rows,
            line,
            line,
            line,
            rows,
            line,
            rows,
            line,
            line,
            line,
        ),
        out_specs=(
            tokens,
            tokens,
            rows,
            line,
            rows,
            rows,
            line,
            rows,
            line,
            line,
            line,
            rows,
            line,
            rows,
            line,
            line,
            line,
        ),
        check_vma=False,
    )
```

```python
import functools

import jax
import jax.numpy as jnp
from jax import lax
from jax.experimental import pallas as pl
from jax.experimental.pallas import tpu as pltpu
from jax.sharding import PartitionSpec as P

HEADS = 12
SCALE = 0.125
EPS = 1e-05
PAIR = 128
ROWS = 256
CHUNK = 768
LANES = 128
GROUP = 256
LAG = 3
AHEAD = 4
VMEM_LIMIT = 64 * 1024 * 1024 - 65536
GELU_C = 0.7978845608028654
GELU_A = 0.044715
MESH = pl.DeviceIdType.MESH
F32 = jnp.float32
BF16 = jnp.bfloat16


def dot_nn(left, right):
    return lax.dot_general(left, right, (((1,), (0,)), ((), ())), preferred_element_type=F32)


def dot_nt(left, right):
    return lax.dot_general(left, right, (((1,), (1,)), ((), ())), preferred_element_type=F32)


def dot_tn(left, right):
    return lax.dot_general(left, right, (((0,), (0,)), ((), ())), preferred_element_type=F32)


def place():
    s = lax.axis_index("seq")
    g = lax.axis_index("grp")
    return s, g // 4, (g // 2) % 2, g % 2


def device(s, z, y, x):
    return (s, z * 4 + y * 2 + x)


def first_partner(s, z, y, x):
    return device(s, z, y * s + (1 - y) * (1 - s), x * (1 - s) + (1 - x) * s)


def second_partner(s, z, y, x):
    return device(s, z, y * (1 - s) + (1 - y) * s, x * s + (1 - x) * (1 - s))


def greet(s, z, y, x):
    barrier = pltpu.get_barrier_semaphore()
    partners = [device(1 - s, z, y, x), first_partner(s, z, y, x), second_partner(s, z, y, x)]
    partners += [device(s, (z + k) % 4, y, x) for k in (1, 2, 3)]
    for partner in partners:
        pl.semaphore_signal(barrier, inc=1, device_id=partner, device_id_type=MESH)
    pl.semaphore_wait(barrier, len(partners))


def remote(src, dst, send, recv, target):
    return pltpu.make_async_remote_copy(
        src_ref=src, dst_ref=dst, send_sem=send, recv_sem=recv, device_id=target, device_id_type=MESH
    )


def selector(lanes, width, piece):
    lane = lax.broadcasted_iota(jnp.int32, (lanes, width), 0)
    col = lax.broadcasted_iota(jnp.int32, (lanes, width), 1)
    return (lax.rem(col, piece) == lane).astype(BF16)


def owned(devices, rows, width, piece):
    dev = lax.broadcasted_iota(jnp.int32, (devices, rows, width), 0)
    col = lax.broadcasted_iota(jnp.int32, (devices, rows, width), 2)
    return col // piece == dev


def spread(pieces, width):
    devices, rows, lanes = pieces.shape
    piece = width // devices
    flat = pieces.reshape(devices * rows, lanes).astype(BF16)
    tiled = dot_nn(flat, selector(lanes, width, piece)).reshape(devices, rows, width)
    return jnp.sum(jnp.where(owned(devices, rows, width, piece), tiled, 0.0), axis=0)


def collect(values, devices):
    rows, width = values.shape
    piece = width // devices
    mine = jnp.where(owned(devices, rows, width, piece), values[None], 0.0)
    flat = mine.reshape(devices * rows, width).astype(BF16)
    return dot_nt(flat, selector(LANES, width, piece)).reshape(devices, rows, LANES)


class Gather:
    def __init__(self, shards, fulls, own_sem, send, recv, chunks, where):
        self.shards, self.fulls, self.chunks, self.where = shards, fulls, chunks, where
        self.own_sem, self.send, self.recv = own_sem, send, recv

    def piece(self, i):
        a, r, nr, c, nc = self.chunks[i]
        return self.shards[a].at[r : r + nr, c : c + nc]

    def full(self, i, *where):
        a, r, nr, c, nc = self.chunks[i]
        return self.fulls[a].at[(*where, slice(r, r + nr), slice(c, c + nc))]

    def own(self, i):
        return pltpu.make_async_copy(self.piece(i), self.full(i, *self.where), self.own_sem.at[i])

    def along_z(self, i, k):
        s, z, y, x = self.where
        return remote(
            self.piece(i),
            self.full(i, s, z, y, x),
            self.send.at[i, k - 1],
            self.recv.at[i, k - 1],
            device(s, (z + k) % 4, y, x),
        )

    def first(self, i):
        s, z, y, x = self.where
        part = self.full(i, s, slice(None), y, x)
        return remote(
            part, part, self.send.at[i, 3], self.recv.at[i, 3], second_partner(s, z, y, x)
        )

    def second(self, i, j):
        s, z, y, x = self.where
        yy = y * (1 - s) + j * s
        xx = j * (1 - s) + x * s
        part = self.full(i, s, slice(None), yy, xx)
        return remote(
            part, part, self.send.at[i, 4 + j], self.recv.at[i, 4 + j], first_partner(s, z, y, x)
        )

    def across(self, i):
        s, z, y, x = self.where
        part = self.full(i, s, slice(None), slice(None), slice(None))
        return remote(part, part, self.send.at[i, 6], self.recv.at[i, 6], device(1 - s, z, y, x))

    def stage(self, t, i):
        if not 0 <= i < len(self.chunks):
            return
        if t == 0:
            for k in (1, 2, 3):
                self.along_z(i, k).start()
            self.own(i).start()
        elif t == 1:
            self.own(i).wait()
            for k in (1, 2, 3):
                self.along_z(i, k).wait_recv()
            self.first(i).start()
        elif t == 2:
            self.first(i).wait_recv()
            for j in (0, 1):
                self.second(i, j).start()
        elif t == 3:
            for j in (0, 1):
                self.second(i, j).wait_recv()
            self.across(i).start()

    def begin(self):
        for i in range(AHEAD):
            self.stage(0, i)

    def steps(self):
        return len(self.chunks) + 2 * LAG

    def step(self, n):
        self.stage(3, n - 2 * LAG)
        self.stage(2, n - LAG)
        self.stage(1, n)
        self.stage(0, n + AHEAD)

    def sent(self):
        for i in range(len(self.chunks)):
            for k in (1, 2, 3):
                self.along_z(i, k).wait_send()
            self.first(i).wait_send()
            for j in (0, 1):
                self.second(i, j).wait_send()
            self.across(i).wait_send()


class Scatter:
    def __init__(self, fulls, gots, outs, send, recv, chunks, where):
        self.fulls, self.gots, self.outs, self.chunks = fulls, gots, outs, chunks
        self.send, self.recv, self.where = send, recv, where

    def full(self, i, *where):
        a, r, nr, c, nc = self.chunks[i]
        return self.fulls[a].at[(*where, slice(r, r + nr), slice(c, c + nc))]

    def got(self, level, i, *where):
        a, r, nr, c, nc = self.chunks[i]
        return self.gots[level][a].at[(*where, slice(r, r + nr), slice(c, c + nc))]

    def out(self, i):
        a, r, nr, c, nc = self.chunks[i]
        return self.outs[a].at[r : r + nr, c : c + nc]

    def across(self, i):
        s, z, y, x = self.where
        every = (slice(None),) * 3
        return remote(
            self.full(i, 1 - s, *every),
            self.got(0, i, *every),
            self.send.at[i, 0],
            self.recv.at[i, 0],
            device(1 - s, z, y, x),
        )

    def first(self, i, j):
        s, z, y, x = self.where
        yy = (1 - y) * (1 - s) + j * s
        xx = j * (1 - s) + (1 - x) * s
        return remote(
            self.full(i, s, slice(None), yy, xx),
            self.got(1, i, slice(None), j),
            self.send.at[i, 1 + j],
            self.recv.at[i, 1 + j],
            first_partner(s, z, y, x),
        )

    def second(self, i):
        s, z, y, x = self.where
        y2 = y * (1 - s) + (1 - y) * s
        x2 = (1 - x) * (1 - s) + x * s
        return remote(
            self.full(i, s, slice(None), y2, x2),
            self.got(2, i, slice(None)),
            self.send.at[i, 3],
            self.recv.at[i, 3],
            second_partner(s, z, y, x),
        )

    def along_z(self, i, k):
        s, z, y, x = self.where
        zt = (z + k) % 4
        return remote(
            self.full(i, s, zt, y, x),
            self.got(3, i, k - 1),
            self.send.at[i, 3 + k],
            self.recv.at[i, 3 + k],
            device(s, zt, y, x),
        )

    def add(self, to, term):
        to[...] = (to[...].astype(F32) + term[...].astype(F32)).astype(BF16)

    def stage(self, t, i):
        if not 0 <= i < len(self.chunks):
            return
        s, z, y, x = self.where
        if t == 0:
            self.across(i).start()
        elif t == 1:
            self.across(i).wait_recv()

            def add1(n, unused):
                at = (n // 4, (n // 2) % 2, n % 2)
                self.add(self.full(i, s, *at), self.got(0, i, *at))
                return unused

            lax.fori_loop(0, 16, add1, 0)
            for j in (0, 1):
                self.first(i, j).start()
        elif t == 2:
            for j in (0, 1):
                self.first(i, j).wait_recv()

            def add2(n, unused):
                zz, j = n // 2, n % 2
                yy = y * (1 - s) + j * s
                xx = j * (1 - s) + x * s
                self.add(self.full(i, s, zz, yy, xx), self.got(1, i, zz, j))
                return unused

            lax.fori_loop(0, 8, add2, 0)
            self.second(i).start()
        elif t == 3:
            self.second(i).wait_recv()

            def add3(zz, unused):
                self.add(self.full(i, s, zz, y, x), self.got(2, i, zz))
                return unused

            lax.fori_loop(0, 4, add3, 0)
            for k in (1, 2, 3):
                self.along_z(i, k).start()
        elif t == 4:
            for k in (1, 2, 3):
                self.along_z(i, k).wait_recv()
            total = self.full(i, s, z, y, x)[...].astype(F32)
            for k in (0, 1, 2):
                total = total + self.got(3, i, k)[...].astype(F32)
            self.out(i)[...] = total

    def sent(self):
        for i in range(len(self.chunks)):
            self.across(i).wait_send()
            for j in (0, 1):
                self.first(i, j).wait_send()
            self.second(i).wait_send()
            for k in (1, 2, 3):
                self.along_z(i, k).wait_send()


def got_shapes(sizes):
    return [pltpu.VMEM(lead + size, BF16) for lead in ((4, 2, 2), (4, 2), (4,), (3,)) for size in sizes]


def got_levels(refs, count):
    return [refs[level * count : (level + 1) * count] for level in range(4)]


def head_of(shape):
    return lax.broadcasted_iota(jnp.int32, shape, len(shape) - 1) // 64


def pick(values, head):
    return jnp.where(head_of(values.shape) == head, values, jnp.zeros_like(values))


def attend_pair(queries, keys, values):
    length = queries.shape[0]
    mixed, logs = [], []
    for head in (0, 1):
        scores = dot_nt(pick(queries, head), keys)
        top = jnp.max(scores, axis=1, keepdims=True)
        powers = jnp.exp(scores - top)
        total = jnp.sum(powers, axis=1, keepdims=True)
        mixed.append(dot_nn(powers.astype(BF16), values) * (1.0 / total))
        column = jnp.broadcast_to(top + jnp.log(total), (length, LANES))
        logs.append(jnp.transpose(column)[0:1])
    attended = jnp.where(head_of(mixed[0].shape) == 0, mixed[0], mixed[1]).astype(BF16)
    return attended, jnp.concatenate(logs, axis=0)


def attend_pair_back(queries, keys, values, attended, grad, logs):
    keys_t = jnp.transpose(keys)
    products = jnp.transpose(grad.astype(F32) * attended.astype(F32))
    dk = jnp.zeros(keys.shape, F32)
    dv = jnp.zeros(keys.shape, F32)
    dq_t = []
    for head in (0, 1):
        offset = jnp.sum(products[64 * head : 64 * head + 64], axis=0, keepdims=True)
        q_head = pick(queries, head)
        g_head = pick(grad, head)
        scores_t = dot_nt(keys, q_head)
        probs_t = jnp.exp(scores_t - logs[head : head + 1, :])
        slopes_t = dot_nt(values, g_head)
        score_grad_t = (probs_t * (slopes_t - offset)).astype(BF16)
        dv += dot_nn(probs_t.astype(BF16), g_head)
        dk += dot_nn(score_grad_t, q_head)
        dq_t.append(dot_nn(keys_t[64 * head : 64 * head + 64], score_grad_t))
    dq = jnp.transpose(jnp.concatenate(dq_t, axis=0)) * SCALE
    return dq.astype(BF16), dk.astype(BF16), dv.astype(BF16)


def attend_kernel(q_ref, k_ref, v_ref, o_ref, lse_ref):
    keys = k_ref[:, 0].reshape(-1, PAIR)
    values = v_ref[:, 0].reshape(-1, PAIR)
    o_ref[0], lse_ref[0, 0] = attend_pair(q_ref[0], keys, values)


def attend(queries, keys, values):
    micro, length, width = queries.shape
    parts = keys.shape[0]
    pairs = width // PAIR
    row = pl.BlockSpec((1, length, PAIR), lambda m, p: (m, 0, p))
    col = pl.BlockSpec((parts, 1, length, PAIR), lambda m, p: (0, m, 0, p))
    return pl.pallas_call(
        attend_kernel,
        grid=(micro, pairs),
        in_specs=[row, col, col],
        out_specs=[row, pl.BlockSpec((1, 1, 2, length), lambda m, p: (m, p, 0, 0))],
        out_shape=[
            jax.ShapeDtypeStruct(queries.shape, BF16),
            jax.ShapeDtypeStruct((micro, pairs, 2, length), F32),
        ],
        compiler_params=pltpu.CompilerParams(vmem_limit_bytes=VMEM_LIMIT),
        name="attend",
    )(queries, keys, values)


def attend_back_kernel(q_ref, k_ref, v_ref, o_ref, g_ref, lse_ref, dq_ref, dk_ref, dv_ref):
    parts, length = k_ref.shape[0], q_ref.shape[1]
    keys = k_ref[:, 0].reshape(-1, PAIR)
    values = v_ref[:, 0].reshape(-1, PAIR)
    dq, dk, dv = attend_pair_back(q_ref[0], keys, values, o_ref[0], g_ref[0], lse_ref[0, 0])
    dq_ref[0] = dq
    dk_ref[:, 0] = dk.reshape(parts, length, PAIR)
    dv_ref[:, 0] = dv.reshape(parts, length, PAIR)


def attend_back(queries, keys, values, attended, grad, lse):
    micro, length, width = queries.shape
    parts = keys.shape[0]
    pairs = width // PAIR
    row = pl.BlockSpec((1, length, PAIR), lambda m, p: (m, 0, p))
    col = pl.BlockSpec((parts, 1, length, PAIR), lambda m, p: (0, m, 0, p))
    log = pl.BlockSpec((1, 1, 2, length), lambda m, p: (m, p, 0, 0))
    return pl.pallas_call(
        attend_back_kernel,
        grid=(micro, pairs),
        in_specs=[row, col, col, row, row, log],
        out_specs=[row, col, col],
        out_shape=[
            jax.ShapeDtypeStruct((micro, length, width), BF16),
            jax.ShapeDtypeStruct((parts, micro, length, width), BF16),
            jax.ShapeDtypeStruct((parts, micro, length, width), BF16),
        ],
        compiler_params=pltpu.CompilerParams(vmem_limit_bytes=VMEM_LIMIT),
        name="attend_back",
    )(queries, keys, values, attended, grad, lse)


def project_kernel(own_ref, all_ref, wq_ref, wk_ref, wv_ref, small_ref, q_ref, k_ref, v_ref, bias):
    @pl.when(pl.program_id(0) == 0)
    def _():
        bias[...] = spread(small_ref[:, 0:8].astype(F32), bias.shape[1])

    @pl.when(pl.program_id(0) < own_ref.shape[0] * 2)
    def _():
        queries = dot_nn(own_ref[0], wq_ref[...]) + bias[0:1]
        q_ref[0] = (queries.astype(BF16).astype(F32) * SCALE).astype(BF16)

    rows = all_ref[0, 0]
    k_ref[0, 0] = dot_nn(rows, wk_ref[...]).astype(BF16)
    v_ref[0, 0] = (dot_nn(rows, wv_ref[...]) + bias[1:2]).astype(BF16)


def project(own, all_rows, wq, wk, wv, small):
    micro, length, width = own.shape
    parts = all_rows.shape[0]
    whole = lambda a: pl.BlockSpec(a.shape, lambda i: (0,) * a.ndim)
    last = micro - 1
    mine = pl.BlockSpec((1, length, width), lambda i: (jnp.minimum(i, last), 0, 0))
    every = pl.BlockSpec((1, 1, length, width), lambda i: (i // micro, i % micro, 0, 0))
    return pl.pallas_call(
        project_kernel,
        grid=(parts * micro,),
        in_specs=[mine, every, whole(wq), whole(wk), whole(wv), whole(small)],
        out_specs=[mine, every, every],
        out_shape=[
            jax.ShapeDtypeStruct((micro, length, width), BF16),
            jax.ShapeDtypeStruct((parts, micro, length, width), BF16),
            jax.ShapeDtypeStruct((parts, micro, length, width), BF16),
        ],
        scratch_shapes=[pltpu.VMEM((8, width), F32)],
        compiler_params=pltpu.CompilerParams(vmem_limit_bytes=VMEM_LIMIT),
        name="project",
    )(own, all_rows, wq, wk, wv, small)


SMALL, WQ, WK, WV, WO, WIN, WOUT = range(7)


def forward_chunks(shapes):
    chunks = [(SMALL, 0, shapes[SMALL][0], 0, LANES)]
    rows, width = shapes[WQ]
    for c in range(0, width, GROUP):
        chunks += [(w, 0, rows, c, GROUP) for w in (WQ, WK, WV)]
    chunks.append((WO, 0, rows, 0, width))
    chunks += [(WIN, 0, rows, c, CHUNK) for c in range(0, shapes[WIN][1], CHUNK)]
    chunks += [(WOUT, 0, shapes[WOUT][0], c, GROUP) for c in range(0, width, GROUP)]
    return chunks


def forward_kernel(chunks, *refs):
    shards, x_ref, fulls = refs[:7], refs[7], refs[8:15]
    q_out, k_out, v_out, att_ref, lse_ref = refs[15:20]
    other, pieces, weights, small, bias, q_s, k_s, v_s = refs[20:28]
    own_sem, send, recv, row_send, row_recv, load, back = refs[28:]
    where = place()
    s, z, y, x = where
    width = q_s.shape[2]
    length = q_s.shape[1]
    groups = width // GROUP
    greet(s, z, y, x)
    gather = Gather(shards, fulls, own_sem, send, recv, chunks, where)
    rows = remote(x_ref, other, row_send, row_recv, device(1 - s, z, y, x))
    gather.begin()
    rows.start()

    def fetch(g):
        copies = []
        for n, w in enumerate((WQ, WK, WV)):
            source = fulls[w].at[:, :, :, :, :, g * GROUP : (g + 1) * GROUP]
            target = pieces.at[:, :, :, :, :, n * GROUP : (n + 1) * GROUP]
            copies.append(pltpu.make_async_copy(source, target, load.at[n]))
        return copies

    def arrived(g):
        for i in range(3 * g + 1, 3 * g + 4):
            gather.across(i).wait_recv()
        for copy in fetch(g):
            copy.start()

    def written(g):
        cols = slice(g * GROUP, (g + 1) * GROUP)
        return [
            pltpu.make_async_copy(q_s.at[:, :, cols], q_out.at[:, :, cols], back.at[g, 0]),
            pltpu.make_async_copy(k_s.at[:, :, :, cols], k_out.at[:, :, :, cols], back.at[g, 1]),
            pltpu.make_async_copy(v_s.at[:, :, :, cols], v_out.at[:, :, :, cols], back.at[g, 2]),
        ]

    ready = 4 + 2 * LAG
    for n in range(ready):
        gather.step(n)
    gather.across(0).wait_recv()
    small_copy = pltpu.make_async_copy(fulls[SMALL], small, load.at[3])
    small_copy.start()
    arrived(0)
    small_copy.wait()
    vectors = small[...].reshape(32, 16, LANES)[:, 0:8]
    bias[...] = spread(vectors.astype(F32), width)
    rows.wait_recv()

    for g in range(groups):
        for copy in fetch(g):
            copy.wait()
        weights[...] = pieces[...].reshape(weights.shape)
        cols = slice(g * GROUP, (g + 1) * GROUP)

        def mine(m, unused):
            made = dot_nn(x_ref[m], weights[...])
            queries = made[:, :GROUP] + bias[0:1, cols]
            q_s[m, :, cols] = (queries.astype(BF16).astype(F32) * SCALE).astype(BF16)
            k_s[0, m, :, cols] = made[:, GROUP : 2 * GROUP].astype(BF16)
            v_s[0, m, :, cols] = (made[:, 2 * GROUP :] + bias[1:2, cols]).astype(BF16)
            return unused

        def others(m, unused):
            made = dot_nn(other[m], weights[:, GROUP:])
            k_s[1, m, :, cols] = made[:, :GROUP].astype(BF16)
            v_s[1, m, :, cols] = (made[:, GROUP:] + bias[1:2, cols]).astype(BF16)
            return unused

        lax.fori_loop(0, 2, mine, 0)
        lax.fori_loop(0, 2, others, 0)
        for copy in written(g):
            copy.start()

        def one(j, unused):
            for n in range(3):

                @pl.when(j == n)
                def _():
                    gather.step(ready + 3 * g + n)

            if g + 1 < groups:

                @pl.when(j == 3)
                def _():
                    arrived(g + 1)

            m = j // 2
            p = 2 * g + j % 2
            lanes = pl.ds(pl.multiple_of(p * PAIR, PAIR), PAIR)
            keys = k_s[:, m, :, lanes].reshape(2 * length, PAIR)
            values = v_s[:, m, :, lanes].reshape(2 * length, PAIR)
            attended, logs = attend_pair(q_s[m, :, lanes], keys, values)
            att_ref[m, :, lanes] = attended
            lse_ref[m, p] = logs
            return unused

        lax.fori_loop(0, 4, one, 0)

    for n in range(ready + 3 * groups, gather.steps()):
        gather.step(n)
    for i in range(3 * groups + 1, len(chunks)):
        gather.across(i).wait_recv()
    for g in range(groups):
        for copy in written(g):
            copy.wait()
    rows.wait_send()
    gather.sent()


def forward_box(shards, own):
    micro, length, width = own.shape
    chunks = forward_chunks([a.shape for a in shards])
    any_spec = pl.BlockSpec(memory_space=pl.ANY)
    vmem_spec = pl.BlockSpec(memory_space=pltpu.VMEM)
    count = len(chunks)
    pairs = width // PAIR
    twice = (2, micro, length, width)
    outs = pl.pallas_call(
        functools.partial(forward_kernel, chunks),
        out_shape=[jax.ShapeDtypeStruct((2, 4, 2, 2) + a.shape, a.dtype) for a in shards]
        + [
            jax.ShapeDtypeStruct(own.shape, BF16),
            jax.ShapeDtypeStruct(twice, BF16),
            jax.ShapeDtypeStruct(twice, BF16),
            jax.ShapeDtypeStruct(own.shape, BF16),
            jax.ShapeDtypeStruct((micro, pairs, 2, length), F32),
        ],
        in_specs=[vmem_spec] * 8,
        out_specs=[any_spec] * 10 + [vmem_spec] * 2,
        scratch_shapes=[
            pltpu.VMEM(own.shape, BF16),
            pltpu.VMEM((2, 4, 2, 2, width // 32, 3 * GROUP), BF16),
            pltpu.VMEM((width, 3 * GROUP), BF16),
            pltpu.VMEM((2, 4, 2, 2, 16, LANES), BF16),
            pltpu.VMEM((8, width), F32),
            pltpu.VMEM(own.shape, BF16),
            pltpu.VMEM(twice, BF16),
            pltpu.VMEM(twice, BF16),
            pltpu.SemaphoreType.DMA((count,)),
            pltpu.SemaphoreType.DMA((count, 7)),
            pltpu.SemaphoreType.DMA((count, 7)),
            pltpu.SemaphoreType.DMA,
            pltpu.SemaphoreType.DMA,
            pltpu.SemaphoreType.DMA((4,)),
            pltpu.SemaphoreType.DMA((width // GROUP, 3)),
        ],
        compiler_params=pltpu.CompilerParams(
            collective_id=1, has_side_effects=True, vmem_limit_bytes=VMEM_LIMIT
        ),
        name="forward_attention",
    )(*shards, own)
    fulls = [full.reshape((-1, full.shape[-1])) for full in outs[1:7]]
    return [outs[0].reshape(32, 16, LANES)] + fulls, outs[7:]


def mean_rows(values):
    return jnp.mean(values, axis=-1, keepdims=True)


def rows_kernel(
    x_ref,
    att_ref,
    cot_ref,
    wo_ref,
    win_ref,
    wout_ref,
    small_ref,
    out_ref,
    hidden_ref,
    active_ref,
    inner_grad_ref,
    feed_ref,
    branch_ref,
    mixed_ref,
    first_ref,
    smallg_ref,
    vec,
    ib,
    slope,
    vecg,
    ibg,
):
    step = pl.program_id(0)
    chunks = win_ref.shape[1] // CHUNK

    @pl.when(step == 0)
    def _():
        vec[...] = spread(small_ref[:, 0:8].astype(F32), vec.shape[1])
        ib[...] = spread(small_ref[:, 8:16].astype(F32), ib.shape[1])
        vecg[...] = jnp.zeros_like(vecg)
        ibg[...] = jnp.zeros_like(ibg)

    o_b, g1, s1, outer_b, g2, s2 = (vec[i : i + 1] for i in range(2, 8))
    first_sum = x_ref[...].astype(F32) + (dot_nn(att_ref[...], wo_ref[...]) + o_b)
    centred = first_sum - mean_rows(first_sum)
    r1 = lax.rsqrt(mean_rows(centred * centred) + EPS)
    n1 = centred * r1
    hidden = n1 * g1 + s1
    hidden_low = hidden.astype(BF16)
    hidden_ref[...] = hidden_low
    total = hidden + outer_b
    for c in range(chunks):
        cols = slice(c * CHUNK, (c + 1) * CHUNK)
        v = dot_nn(hidden_low, win_ref[:, cols]) + ib[0:1, cols]
        square = v * v
        t = jnp.tanh(v * (GELU_C + (GELU_C * GELU_A) * square))
        half = 0.5 * (1.0 + t)
        active = (v * half).astype(BF16)
        active_ref[:, cols] = active
        slope[:, cols] = half + (0.5 * v) * (1.0 - t * t) * (
            GELU_C + (3.0 * GELU_C * GELU_A) * square
        )
        total = total + dot_nn(active, wout_ref[cols, :])
    centred = total - mean_rows(total)
    r2 = lax.rsqrt(mean_rows(centred * centred) + EPS)
    n2 = centred * r2
    out_ref[...] = (n2 * g2 + s2).astype(BF16)
    e = cot_ref[...].astype(F32)
    m = e * g2
    second = (m - mean_rows(m) - n2 * mean_rows(m * n2)) * r2
    feed = second.astype(BF16)
    feed_ref[...] = feed
    vecg[6:7] += jnp.sum(e * n2, axis=0, keepdims=True)
    vecg[7:8] += jnp.sum(e, axis=0, keepdims=True)
    vecg[5:6] += jnp.sum(feed.astype(F32), axis=0, keepdims=True)
    e = second
    for c in range(chunks):
        cols = slice(c * CHUNK, (c + 1) * CHUNK)
        inner_grad = (dot_nt(feed, wout_ref[cols, :]) * slope[:, cols]).astype(BF16)
        inner_grad_ref[:, cols] = inner_grad
        ibg[0:1, cols] += jnp.sum(inner_grad.astype(F32), axis=0, keepdims=True)
        e = e + dot_nt(inner_grad, win_ref[:, cols])
    m = e * g1
    first = (m - mean_rows(m) - n1 * mean_rows(m * n1)) * r1
    first_ref[...] = first
    branch = first.astype(BF16)
    branch_ref[...] = branch
    vecg[3:4] += jnp.sum(e * n1, axis=0, keepdims=True)
    vecg[4:5] += jnp.sum(e, axis=0, keepdims=True)
    vecg[2:3] += jnp.sum(branch.astype(F32), axis=0, keepdims=True)
    mixed_ref[...] = dot_nt(branch, wo_ref[...]).astype(BF16)

    @pl.when(step == pl.num_programs(0) - 1)
    def _():
        devices = smallg_ref.shape[0]
        smallg_ref[:, 0:8] = collect(vecg[...], devices).astype(BF16)
        smallg_ref[:, 8:16] = collect(ibg[...], devices).astype(BF16)


def row_stage(x, attended, cotangent, wo, win, wout, small):
    rows, width = x.shape
    hidden_width = win.shape[1]
    block = min(ROWS, rows)
    whole = lambda a: pl.BlockSpec(
        a.shape, lambda i: (0,) * a.ndim, pipeline_mode=pl.Buffered(1)
    )
    narrow = pl.BlockSpec((block, width), lambda i: (i, 0))
    wide = pl.BlockSpec((block, hidden_width), lambda i: (i, 0))
    low = jax.ShapeDtypeStruct((rows, width), BF16)
    low_wide = jax.ShapeDtypeStruct((rows, hidden_width), BF16)
    return pl.pallas_call(
        rows_kernel,
        grid=(rows // block,),
        in_specs=[narrow] * 3 + [whole(a) for a in (wo, win, wout, small)],
        out_specs=[
            narrow,
            narrow,
            wide,
            wide,
            narrow,
            narrow,
            narrow,
            narrow,
            pl.BlockSpec(small.shape, lambda i: (0, 0, 0)),
        ],
        out_shape=[
            low,
            low,
            low_wide,
            low_wide,
            low,
            low,
            low,
            jax.ShapeDtypeStruct((rows, width), F32),
            jax.ShapeDtypeStruct(small.shape, BF16),
        ],
        scratch_shapes=[
            pltpu.VMEM((8, width), F32),
            pltpu.VMEM((8, hidden_width), F32),
            pltpu.VMEM((block, hidden_width), F32),
            pltpu.VMEM((8, width), F32),
            pltpu.VMEM((8, hidden_width), F32),
        ],
        compiler_params=pltpu.CompilerParams(vmem_limit_bytes=VMEM_LIMIT),
        name="row_stage",
    )(x, attended, cotangent, wo, win, wout, small)


def product_kernel(left_ref, right_ref, out_ref):
    out_ref[...] = dot_tn(left_ref[...], right_ref[...]).astype(BF16)


def product(left, right, block_m, block_n):
    depth, rows = left.shape
    cols = right.shape[1]
    return pl.pallas_call(
        product_kernel,
        grid=(rows // block_m, cols // block_n),
        in_specs=[
            pl.BlockSpec((depth, block_m), lambda i, j: (0, i)),
            pl.BlockSpec((depth, block_n), lambda i, j: (0, j)),
        ],
        out_specs=pl.BlockSpec((block_m, block_n), lambda i, j: (i, j)),
        out_shape=jax.ShapeDtypeStruct((rows, cols), BF16),
        compiler_params=pltpu.CompilerParams(vmem_limit_bytes=VMEM_LIMIT),
        name="weight_gradient",
    )(left, right)


def input_kernel(first_ref, dq_ref, dk_ref, dv_ref, wq_ref, wk_ref, wv_ref, out_ref, vecg_ref, acc):
    step = pl.program_id(0)

    @pl.when(step == 0)
    def _():
        acc[...] = jnp.zeros_like(acc)

    out_ref[...] = (
        first_ref[...]
        + dot_nt(dq_ref[...], wq_ref[...])
        + dot_nt(dk_ref[...], wk_ref[...])
        + dot_nt(dv_ref[...], wv_ref[...])
    ).astype(BF16)
    acc[0:1] += jnp.sum(dq_ref[...].astype(F32), axis=0, keepdims=True)
    acc[1:2] += jnp.sum(dv_ref[...].astype(F32), axis=0, keepdims=True)

    @pl.when(step == pl.num_programs(0) - 1)
    def _():
        vecg_ref[:, 0:8] = collect(acc[...], vecg_ref.shape[0]).astype(BF16)
        vecg_ref[:, 8:16] = jnp.zeros((vecg_ref.shape[0], 8, LANES), BF16)


def input_stage(first, dq, dk, dv, wq, wk, wv, small_shape):
    rows, width = first.shape
    block = min(ROWS, rows)
    narrow = pl.BlockSpec((block, width), lambda i: (i, 0))
    whole = pl.BlockSpec((width, width), lambda i: (0, 0))
    return pl.pallas_call(
        input_kernel,
        grid=(rows // block,),
        in_specs=[narrow] * 4 + [whole] * 3,
        out_specs=[narrow, pl.BlockSpec(small_shape, lambda i: (0, 0, 0))],
        out_shape=[
            jax.ShapeDtypeStruct((rows, width), BF16),
            jax.ShapeDtypeStruct(small_shape, BF16),
        ],
        scratch_shapes=[pltpu.VMEM((8, width), F32)],
        compiler_params=pltpu.CompilerParams(vmem_limit_bytes=VMEM_LIMIT),
        name="input_stage",
    )(first, dq, dk, dv, wq, wk, wv)


G_IN, G_OUT, G_O, G_SMALL = range(4)
BACK_PRODUCTS = 9
BACK_CHUNKS = (
    [(G_IN, c * CHUNK, CHUNK, c + 1, (2, 5, 8, 11)) for c in range(4)]
    + [(G_O, 0, CHUNK, 5, (2, 5, 8, 11)), (G_SMALL, 0, LANES, 5, (2, 5, 8, 11))]
    + [(G_OUT, c * GROUP, GROUP, 9 + c, (2, 4, 6, 9)) for c in range(3)]
)


def backward_kernel(sizes, *refs):
    (hidden, inner, active, feed, flat, branch, small_in) = refs[:7]
    (q_ref, k_ref, v_ref, o_ref, g_ref, lse_ref) = refs[7:13]
    outs = refs[13:17]
    (dq_ref, dk_ref, dv_ref, dk_far, dv_far) = refs[17:22]
    fulls = refs[22:26]
    gots = got_levels(refs[26:42], 4)
    away, send, recv, far_send, far_recv = refs[42:]
    where = place()
    s, z, y, x = where
    step = pl.program_id(0)
    length = q_ref.shape[1]
    pairs = dk_far.shape[2] // PAIR
    units = dk_far.shape[0] * pairs
    chunks = [(a, 0, sizes[a][0], c, nc) for a, c, nc, _, _ in BACK_CHUNKS]
    scatter = Scatter(fulls, gots, outs, send, recv, chunks, where)

    @pl.when(step == 0)
    def _():
        greet(s, z, y, x)
        fulls[G_SMALL][...] = small_in[...].reshape(fulls[G_SMALL].shape)

    for n in range(1, BACK_PRODUCTS + 12):
        todo = []
        for i, (_, _, _, start, lags) in enumerate(BACK_CHUNKS):
            for t, lag in enumerate((0,) + lags):
                if start + lag == n:
                    todo.append((t, i))
        if todo:

            @pl.when(step == n)
            def _():
                for t, i in sorted(todo, reverse=True):
                    scatter.stage(t, i)

    def shaped(value, a):
        return value.astype(BF16).reshape((-1,) + sizes[a][:1] + (CHUNK,))

    @pl.when(step < 4)
    def _():
        cols = pl.ds(pl.multiple_of(step * CHUNK, CHUNK), CHUNK)
        value = shaped(dot_tn(hidden[...], inner[...]), G_IN)
        fulls[G_IN][:, :, :, :, :, cols] = value.reshape((2, 4, 2, 2) + value.shape[1:])

    @pl.when(step == 4)
    def _():
        value = shaped(dot_tn(flat[...], branch[...]), G_O)
        fulls[G_O][...] = value.reshape((2, 4, 2, 2) + value.shape[1:])

    @pl.when((step >= 5) & (step < BACK_PRODUCTS))
    def _():
        c = step - 5
        value = shaped(dot_tn(active[...], feed[...]), G_OUT)
        fulls[G_OUT][c // 2, pl.ds((c % 2) * 2, 2)] = value.reshape((2, 2, 2) + value.shape[1:])

    def far(j):
        m = j // pairs
        lanes = pl.ds(pl.multiple_of((j % pairs) * PAIR, PAIR), PAIR)
        target = device(1 - s, z, y, x)
        return [
            remote(away.at[j, 0], dk_far.at[m, :, lanes], far_send.at[j, 0], far_recv.at[j, 0], target),
            remote(away.at[j, 1], dv_far.at[m, :, lanes], far_send.at[j, 1], far_recv.at[j, 1], target),
        ]

    @pl.when(step > BACK_PRODUCTS)
    def _():
        for copy in far(step - BACK_PRODUCTS - 1):
            copy.start()

    @pl.when(step >= BACK_PRODUCTS)
    def _():
        j = step - BACK_PRODUCTS
        keys = k_ref[:, 0].reshape(-1, PAIR)
        values = v_ref[:, 0].reshape(-1, PAIR)
        dq, dk, dv = attend_pair_back(q_ref[0], keys, values, o_ref[0], g_ref[0], lse_ref[0, 0])
        dq_ref[0] = dq
        dk_ref[0] = dk[:length]
        dv_ref[0] = dv[:length]
        away[j, 0] = dk[length:]
        away[j, 1] = dv[length:]

    @pl.when(step == BACK_PRODUCTS + units - 1)
    def _():
        for copy in far(units - 1):
            copy.start()
        for j in range(units):
            for copy in far(j):
                copy.wait_recv()
        for j in range(units):
            for copy in far(j):
                copy.wait_send()
        scatter.sent()


def backward_box(hidden, inner, active, feed, flat, branch, small, q, k, v, o, g, lse):
    micro, length, width = q.shape
    tokens, hidden_width = active.shape
    pairs = width // PAIR
    units = micro * pairs
    sizes = [(width // 32, hidden_width), (hidden_width // 32, width), (width // 32, width), (16, LANES)]
    buffered = lambda a: pl.BlockSpec(
        a.shape, lambda i: (0,) * a.ndim, pipeline_mode=pl.Buffered(1)
    )
    unit = lambda i: jnp.clip(i - BACK_PRODUCTS, 0, units - 1)
    row = pl.BlockSpec((1, length, PAIR), lambda i: (unit(i) // pairs, 0, unit(i) % pairs))
    col = pl.BlockSpec(
        (2, 1, length, PAIR), lambda i: (0, unit(i) // pairs, 0, unit(i) % pairs)
    )
    log = pl.BlockSpec((1, 1, 2, length), lambda i: (unit(i) // pairs, unit(i) % pairs, 0, 0))
    any_spec = pl.BlockSpec(memory_space=pl.ANY)
    low = jax.ShapeDtypeStruct((micro, length, width), BF16)
    outs = pl.pallas_call(
        functools.partial(backward_kernel, sizes),
        grid=(BACK_PRODUCTS + units,),
        in_specs=[
            buffered(hidden),
            pl.BlockSpec((tokens, CHUNK), lambda i: (0, jnp.clip(i, 0, 3))),
            pl.BlockSpec((tokens, CHUNK), lambda i: (0, jnp.clip(i - 5, 0, 3))),
            buffered(feed),
            buffered(flat),
            buffered(branch),
            buffered(small),
            row,
            col,
            col,
            row,
            row,
            log,
        ],
        out_specs=[pl.BlockSpec(size, lambda i: (0, 0)) for size in sizes]
        + [row, row, row, any_spec, any_spec],
        out_shape=[jax.ShapeDtypeStruct(size, F32) for size in sizes] + [low] * 5,
        scratch_shapes=[pltpu.VMEM((2, 4, 2, 2) + size, BF16) for size in sizes]
        + got_shapes(sizes)
        + [
            pltpu.VMEM((units, 2, length, PAIR), BF16),
            pltpu.SemaphoreType.DMA((len(BACK_CHUNKS), 7)),
            pltpu.SemaphoreType.DMA((len(BACK_CHUNKS), 7)),
            pltpu.SemaphoreType.DMA((units, 2)),
            pltpu.SemaphoreType.DMA((units, 2)),
        ],
        compiler_params=pltpu.CompilerParams(
            collective_id=2, has_side_effects=True, vmem_limit_bytes=VMEM_LIMIT
        ),
        name="backward_attention",
    )(hidden, inner, active, feed, flat, branch, small, q, k, v, o, g, lse)
    return outs[:4], outs[4:]


def finish_kernel(sizes, *refs):
    x_in, dq_in, dk_in, dk_far, dv_in, dv_far, wq_in, wk_in, wv_in, first_in = refs[:10]
    outs, dx_ref = refs[10:14], refs[14]
    x_v, dq_v, dk_v, dkf_v, dv_v, dvf_v, wq_v, wk_v, wv_v, first_v, x_t, sums = refs[15:27]
    fulls = refs[27:31]
    gots = got_levels(refs[31:47], 4)
    load, send, recv = refs[47:]
    where = place()
    s, z, y, x = where
    pairs = list(
        zip(
            (x_in, dq_in, dk_in, dk_far, dv_in, dv_far, wq_in, wk_in, wv_in, first_in),
            (x_v, dq_v, dk_v, dkf_v, dv_v, dvf_v, wq_v, wk_v, wv_v, first_v),
        )
    )
    copies = [pltpu.make_async_copy(a, b, load.at[n]) for n, (a, b) in enumerate(pairs)]
    for copy in copies:
        copy.start()
    greet(s, z, y, x)
    chunks = [(a, 0, sizes[a][0], 0, sizes[a][1]) for a in range(4)]
    scatter = Scatter(fulls, gots, outs, send, recv, chunks, where)

    def product_of(right, a):
        value = dot_nn(x_t[...], right[...]).astype(BF16)
        fulls[a][...] = value.reshape((2, 4, 2, 2) + sizes[a])

    def join(to, term):
        to[...] = (to[...].astype(F32) + term[...].astype(F32)).astype(BF16)

    copies[0].wait()
    x_t[...] = jnp.transpose(x_v[...])
    copies[1].wait()
    product_of(dq_v, 0)
    copies[2].wait()
    copies[3].wait()
    join(dk_v, dkf_v)
    scatter.stage(0, 0)
    product_of(dk_v, 1)
    copies[4].wait()
    copies[5].wait()
    join(dv_v, dvf_v)
    scatter.stage(1, 0)
    scatter.stage(0, 1)
    product_of(dv_v, 2)
    sums[...] = jnp.zeros_like(sums)
    sums[0:1] = jnp.sum(dq_v[...].astype(F32), axis=0, keepdims=True)
    sums[1:2] = jnp.sum(dv_v[...].astype(F32), axis=0, keepdims=True)
    fulls[3][...] = jnp.zeros_like(fulls[3])
    fulls[3][:, :, :, :, 0:8] = (
        collect(sums[...], 32).astype(BF16).reshape((2, 4, 2, 2, 8, LANES))
    )
    scatter.stage(2, 0)
    scatter.stage(1, 1)
    scatter.stage(0, 2)
    for copy in copies[6:]:
        copy.wait()
    block = ROWS
    blocks = x_v.shape[0] // block
    plan = {0: [(0, 3), (3, 0), (2, 1), (1, 2)], 1: [(1, 3)], 2: [(4, 0), (3, 1), (2, 2), (2, 3)], 3: []}
    for n in range(blocks):
        rows = slice(n * block, (n + 1) * block)
        dx_ref[rows] = (
            first_v[rows]
            + dot_nt(dq_v[rows], wq_v[...])
            + dot_nt(dk_v[rows], wk_v[...])
            + dot_nt(dv_v[rows], wv_v[...])
        ).astype(BF16)
        for t, i in plan.get(n, []):
            scatter.stage(t, i)
    for t, i in ((4, 1), (3, 2), (3, 3), (4, 2), (4, 3)):
        scatter.stage(t, i)
    scatter.sent()


def finish_box(tokens, dq, dk, dk_far, dv, dv_far, wq, wk, wv, first):
    rows, width = tokens.shape
    sizes = [(width // 32, width)] * 3 + [(16, LANES)]
    any_spec = pl.BlockSpec(memory_space=pl.ANY)
    vmem_spec = pl.BlockSpec(memory_space=pltpu.VMEM)
    low = pltpu.VMEM((rows, width), BF16)
    square = pltpu.VMEM((width, width), BF16)
    outs = pl.pallas_call(
        functools.partial(finish_kernel, sizes),
        in_specs=[any_spec] * 10,
        out_specs=[vmem_spec] * 5,
        out_shape=[jax.ShapeDtypeStruct(size, F32) for size in sizes]
        + [jax.ShapeDtypeStruct((rows, width), BF16)],
        scratch_shapes=[low] * 6
        + [square] * 3
        + [pltpu.VMEM((rows, width), F32), pltpu.VMEM((width, rows), BF16), pltpu.VMEM((8, width), F32)]
        + [pltpu.VMEM((2, 4, 2, 2) + size, BF16) for size in sizes]
        + got_shapes(sizes)
        + [
            pltpu.SemaphoreType.DMA((10,)),
            pltpu.SemaphoreType.DMA((4, 7)),
            pltpu.SemaphoreType.DMA((4, 7)),
        ],
        compiler_params=pltpu.CompilerParams(
            collective_id=3, has_side_effects=True, vmem_limit_bytes=VMEM_LIMIT
        ),
        name="input_gradient",
    )(tokens, dq, dk, dk_far, dv, dv_far, wq, wk, wv, first)
    return outs[:4], outs[4]


def hand_out_kernel(*refs):
    (win, wout, wo, small, wq, wk, wv, small2) = refs[:8]
    (wq_o, qb, wk_o, wv_o, vb, wo_o, ob, g1, s1, win_o, ib, wout_o, outb, g2, s2) = refs[8:]
    for source, target in (
        (win, win_o),
        (wout, wout_o),
        (wo, wo_o),
        (wq, wq_o),
        (wk, wk_o),
        (wv, wv_o),
    ):
        target[...] = source[...]
    piece = qb.shape[1]
    qb[...] = small2[0:1, :piece]
    vb[...] = small2[1:2, :piece]
    for row, target in zip(range(2, 8), (ob, g1, s1, outb, g2, s2)):
        target[...] = small[row : row + 1, :piece]
    ib[...] = small[8:9, : ib.shape[1]]


def hand_out(win, wout, wo, small, wq, wk, wv, small2, piece, wide):
    vmem_spec = pl.BlockSpec(memory_space=pltpu.VMEM)
    line = jax.ShapeDtypeStruct((1, piece), F32)
    like = lambda a: jax.ShapeDtypeStruct(a.shape, F32)
    shapes = [like(wq), line, like(wk), like(wv), line, like(wo), line, line, line, like(win)]
    shapes += [jax.ShapeDtypeStruct((1, wide), F32), like(wout), line, line, line]
    outs = pl.pallas_call(
        hand_out_kernel,
        in_specs=[vmem_spec] * 8,
        out_specs=[vmem_spec] * 15,
        out_shape=shapes,
        compiler_params=pltpu.CompilerParams(vmem_limit_bytes=VMEM_LIMIT),
        name="hand_out",
    )(win, wout, wo, small, wq, wk, wv, small2)
    return [a.reshape(-1) if a.shape[0] == 1 else a for a in outs]


def body(
    inputs,
    cotangent,
    query_weight,
    query_bias,
    key_weight,
    value_weight,
    value_bias,
    output_weight,
    output_bias,
    first_gain,
    first_shift,
    inner_weight,
    inner_bias,
    outer_weight,
    outer_bias,
    second_gain,
    second_shift,
):
    micro, _, length, width = inputs.shape
    devices = lax.axis_size(("seq", "grp"))
    piece, wide = query_bias.shape[0], inner_bias.shape[0]
    boxed = lax.axis_size("seq") == 2 and lax.axis_size("grp") == 16 and piece % 8 == 0
    own = inputs[:, 0]
    tokens = own.reshape(-1, width)
    upstream = cotangent[:, 0].reshape(-1, width)
    vectors = jnp.stack(
        (
            query_bias,
            value_bias,
            output_bias,
            first_gain,
            first_shift,
            outer_bias,
            second_gain,
            second_shift,
        )
    )
    vectors = jnp.pad(vectors, ((0, 8), (0, LANES - piece)))
    small = vectors + jnp.pad(inner_bias[None], ((8, 7), (0, LANES - wide)))
    shards = (
        small,
        query_weight,
        key_weight,
        value_weight,
        output_weight,
        inner_weight,
        outer_weight,
    )
    if boxed:
        fulls, made = forward_box(shards, own)
        small, wq, wk, wv, wo, win, wout = fulls
        queries, keys, values, attended, lse = made
    else:
        fulls = [lax.all_gather(a, ("seq", "grp"), axis=0, tiled=True) for a in shards]
        small, wq, wk, wv, wo, win, wout = fulls
        small = small.reshape(devices, 16, LANES)
        all_rows = lax.all_gather(own, "seq", axis=0)
        queries, keys, values = project(own, all_rows, wq, wk, wv, small)
        attended, lse = attend(queries, keys, values)
    flat = attended.reshape(-1, width)
    (
        layer_out,
        hidden_low,
        active,
        inner_grad,
        feed_grad,
        branch_grad,
        mixed_grad,
        first_grad,
        small_grad,
    ) = row_stage(tokens, flat, upstream, wo, win, wout, small)
    mixed_grad = mixed_grad.reshape(micro, length, width)
    if boxed:
        early, made = backward_box(
            hidden_low,
            inner_grad,
            active,
            feed_grad,
            flat,
            branch_grad,
            small_grad,
            queries,
            keys,
            values,
            attended,
            mixed_grad,
            lse,
        )
        dq, dk, dv, dk_far, dv_far = (a.reshape(-1, width) for a in made)
        late, input_grad = finish_box(
            tokens, dq, dk, dk_far, dv, dv_far, wq, wk, wv, first_grad
        )
        win_s, wout_s, wo_s, small_s = early
        wq_s, wk_s, wv_s, small2_s = late
    else:
        wout_grad = product(active, feed_grad, 768, 768)
        win_grad = product(hidden_low, inner_grad, 768, 768)
        wo_grad = product(flat, branch_grad, 768, 768)
        dq, dk, dv = attend_back(queries, keys, values, attended, mixed_grad, lse)
        dk = lax.psum_scatter(dk, "seq", scatter_dimension=0)
        dv = lax.psum_scatter(dv, "seq", scatter_dimension=0)
        dq, dk, dv = (a.reshape(-1, width) for a in (dq, dk, dv))
        input_grad, small2_grad = input_stage(
            first_grad, dq, dk, dv, wq, wk, wv, (devices, 16, LANES)
        )
        terms = (
            win_grad,
            wout_grad,
            wo_grad,
            small_grad.reshape(-1, LANES),
            product(tokens, dq, 768, 768),
            product(tokens, dk, 768, 768),
            product(tokens, dv, 768, 768),
            small2_grad.reshape(-1, LANES),
        )
        summed = [
            lax.psum_scatter(a.astype(F32), ("seq", "grp"), scatter_dimension=0, tiled=True)
            for a in terms
        ]
        summed = lax.optimization_barrier(summed)
        win_s, wout_s, wo_s, small_s, wq_s, wk_s, wv_s, small2_s = summed
    grads = hand_out(win_s, wout_s, wo_s, small_s, wq_s, wk_s, wv_s, small2_s, piece, wide)
    return (layer_out.reshape(inputs.shape), input_grad.reshape(inputs.shape)) + tuple(grads)


def solution(mesh):
    rows = P(("seq", "grp"), None)
    line = P(("seq", "grp"))
    tokens = P(None, "grp", "seq", None)
    return jax.shard_map(
        body,
        mesh=mesh,
        in_specs=(
            tokens,
            tokens,
            rows,
            line,
            rows,
            rows,
            line,
            rows,
            line,
            line,
            line,
            rows,
            line,
            rows,
            line,
            line,
            line,
        ),
        out_specs=(
            tokens,
            tokens,
            rows,
            line,
            rows,
            rows,
            line,
            rows,
            line,
            line,
            line,
            rows,
            line,
            rows,
            line,
            line,
            line,
        ),
        check_vma=False,
    )
```

```python
import functools

import jax
import jax.numpy as jnp
from jax import lax
from jax.experimental import pallas as pl
from jax.experimental.pallas import tpu as pltpu
from jax.sharding import PartitionSpec as P

HEADS = 12
SCALE = 0.125
EPS = 1e-05
PAIR = 128
ROWS = 256
CHUNK = 768
LANES = 128
GROUP = 256
LAG = 3
AHEAD = 4
VMEM_LIMIT = 64 * 1024 * 1024 - 65536
GELU_C = 0.7978845608028654
GELU_A = 0.044715
MESH = pl.DeviceIdType.MESH
F32 = jnp.float32
BF16 = jnp.bfloat16


def dot_nn(left, right):
    return lax.dot_general(left, right, (((1,), (0,)), ((), ())), preferred_element_type=F32)


def dot_nt(left, right):
    return lax.dot_general(left, right, (((1,), (1,)), ((), ())), preferred_element_type=F32)


def dot_tn(left, right):
    return lax.dot_general(left, right, (((0,), (0,)), ((), ())), preferred_element_type=F32)


def place():
    s = lax.axis_index("seq")
    g = lax.axis_index("grp")
    return s, g // 4, (g // 2) % 2, g % 2


def device(s, z, y, x):
    return (s, z * 4 + y * 2 + x)


def first_partner(s, z, y, x):
    return device(s, z, y * s + (1 - y) * (1 - s), x * (1 - s) + (1 - x) * s)


def second_partner(s, z, y, x):
    return device(s, z, y * (1 - s) + (1 - y) * s, x * s + (1 - x) * (1 - s))


def greet(s, z, y, x):
    barrier = pltpu.get_barrier_semaphore()
    partners = [device(1 - s, z, y, x), first_partner(s, z, y, x), second_partner(s, z, y, x)]
    partners += [device(s, (z + k) % 4, y, x) for k in (1, 2, 3)]
    for partner in partners:
        pl.semaphore_signal(barrier, inc=1, device_id=partner, device_id_type=MESH)
    pl.semaphore_wait(barrier, len(partners))


def remote(src, dst, send, recv, target):
    return pltpu.make_async_remote_copy(
        src_ref=src, dst_ref=dst, send_sem=send, recv_sem=recv, device_id=target, device_id_type=MESH
    )


def selector(lanes, width, piece):
    lane = lax.broadcasted_iota(jnp.int32, (lanes, width), 0)
    col = lax.broadcasted_iota(jnp.int32, (lanes, width), 1)
    return (lax.rem(col, piece) == lane).astype(BF16)


def owned(devices, rows, width, piece):
    dev = lax.broadcasted_iota(jnp.int32, (devices, rows, width), 0)
    col = lax.broadcasted_iota(jnp.int32, (devices, rows, width), 2)
    return col // piece == dev


def spread(pieces, width):
    devices, rows, lanes = pieces.shape
    piece = width // devices
    flat = pieces.reshape(devices * rows, lanes).astype(BF16)
    tiled = dot_nn(flat, selector(lanes, width, piece)).reshape(devices, rows, width)
    return jnp.sum(jnp.where(owned(devices, rows, width, piece), tiled, 0.0), axis=0)


def collect(values, devices):
    rows, width = values.shape
    piece = width // devices
    mine = jnp.where(owned(devices, rows, width, piece), values[None], 0.0)
    flat = mine.reshape(devices * rows, width).astype(BF16)
    return dot_nt(flat, selector(LANES, width, piece)).reshape(devices, rows, LANES)


class Gather:
    def __init__(self, shards, fulls, own_sem, send, recv, chunks, where):
        self.shards, self.fulls, self.chunks, self.where = shards, fulls, chunks, where
        self.own_sem, self.send, self.recv = own_sem, send, recv

    def piece(self, i):
        a, r, nr, c, nc = self.chunks[i]
        return self.shards[a].at[r : r + nr, c : c + nc]

    def full(self, i, *where):
        a, r, nr, c, nc = self.chunks[i]
        return self.fulls[a].at[(*where, slice(r, r + nr), slice(c, c + nc))]

    def own(self, i):
        return pltpu.make_async_copy(self.piece(i), self.full(i, *self.where), self.own_sem.at[i])

    def along_z(self, i, k):
        s, z, y, x = self.where
        return remote(
            self.piece(i),
            self.full(i, s, z, y, x),
            self.send.at[i, k - 1],
            self.recv.at[i, k - 1],
            device(s, (z + k) % 4, y, x),
        )

    def first(self, i):
        s, z, y, x = self.where
        part = self.full(i, s, slice(None), y, x)
        return remote(
            part, part, self.send.at[i, 3], self.recv.at[i, 3], second_partner(s, z, y, x)
        )

    def second(self, i, j):
        s, z, y, x = self.where
        yy = y * (1 - s) + j * s
        xx = j * (1 - s) + x * s
        part = self.full(i, s, slice(None), yy, xx)
        return remote(
            part, part, self.send.at[i, 4 + j], self.recv.at[i, 4 + j], first_partner(s, z, y, x)
        )

    def across(self, i):
        s, z, y, x = self.where
        part = self.full(i, s, slice(None), slice(None), slice(None))
        return remote(part, part, self.send.at[i, 6], self.recv.at[i, 6], device(1 - s, z, y, x))

    def stage(self, t, i):
        if not 0 <= i < len(self.chunks):
            return
        if t == 0:
            for k in (1, 2, 3):
                self.along_z(i, k).start()
            self.own(i).start()
        elif t == 1:
            self.own(i).wait()
            for k in (1, 2, 3):
                self.along_z(i, k).wait_recv()
            self.first(i).start()
        elif t == 2:
            self.first(i).wait_recv()
            for j in (0, 1):
                self.second(i, j).start()
        elif t == 3:
            for j in (0, 1):
                self.second(i, j).wait_recv()
            self.across(i).start()

    def begin(self):
        for i in range(AHEAD):
            self.stage(0, i)

    def steps(self):
        return len(self.chunks) + 2 * LAG

    def step(self, n):
        self.stage(3, n - 2 * LAG)
        self.stage(2, n - LAG)
        self.stage(1, n)
        self.stage(0, n + AHEAD)

    def sent(self):
        for i in range(len(self.chunks)):
            for k in (1, 2, 3):
                self.along_z(i, k).wait_send()
            self.first(i).wait_send()
            for j in (0, 1):
                self.second(i, j).wait_send()
            self.across(i).wait_send()


class Scatter:
    def __init__(self, terms, held, gots, outs, load, send, recv, chunks, where):
        self.terms, self.held, self.gots, self.outs, self.chunks = terms, held, gots, outs, chunks
        self.load, self.send, self.recv, self.where = load, send, recv, where

    def cut(self, refs, i, *where):
        a, r, nr, c, nc = self.chunks[i]
        return refs[a].at[(*where, slice(r, r + nr), slice(c, c + nc))]

    def out(self, i):
        a, r, nr, c, nc = self.chunks[i]
        return self.outs[a].at[r : r + nr, c : c + nc]

    def fetch(self, i):
        s = self.where[0]
        every = (slice(None),) * 3
        return pltpu.make_async_copy(
            self.cut(self.terms, i, s, *every), self.cut(self.held, i, *every), self.load.at[i]
        )

    def fetched(self, i):
        return self.load is not None and i < self.load.shape[0]

    def across(self, i):
        s, z, y, x = self.where
        every = (slice(None),) * 3
        return remote(
            self.cut(self.terms, i, 1 - s, *every),
            self.cut(self.gots[0], i, *every),
            self.send.at[i, 0],
            self.recv.at[i, 0],
            device(1 - s, z, y, x),
        )

    def first(self, i, j):
        s, z, y, x = self.where
        yy = (1 - y) * (1 - s) + j * s
        xx = j * (1 - s) + (1 - x) * s
        return remote(
            self.cut(self.held, i, slice(None), yy, xx),
            self.cut(self.gots[1], i, slice(None), j),
            self.send.at[i, 1 + j],
            self.recv.at[i, 1 + j],
            first_partner(s, z, y, x),
        )

    def second(self, i):
        s, z, y, x = self.where
        y2 = y * (1 - s) + (1 - y) * s
        x2 = (1 - x) * (1 - s) + x * s
        return remote(
            self.cut(self.held, i, slice(None), y2, x2),
            self.cut(self.gots[2], i, slice(None)),
            self.send.at[i, 3],
            self.recv.at[i, 3],
            second_partner(s, z, y, x),
        )

    def along_z(self, i, k):
        s, z, y, x = self.where
        zt = (z + k) % 4
        return remote(
            self.cut(self.held, i, zt, y, x),
            self.cut(self.gots[3], i, k - 1),
            self.send.at[i, 3 + k],
            self.recv.at[i, 3 + k],
            device(s, zt, y, x),
        )

    def add(self, to, term):
        to[...] = to[...] + term[...]

    def stage(self, t, i):
        s, z, y, x = self.where
        if t == 0:
            self.across(i).start()
            if self.fetched(i):
                self.fetch(i).start()
        elif t == 1:
            if self.fetched(i):
                self.fetch(i).wait()
            self.across(i).wait_recv()

            def add1(n, unused):
                at = (n // 4, (n // 2) % 2, n % 2)
                self.add(self.cut(self.held, i, *at), self.cut(self.gots[0], i, *at))
                return unused

            lax.fori_loop(0, 16, add1, 0)
            for j in (0, 1):
                self.first(i, j).start()
        elif t == 2:
            for j in (0, 1):
                self.first(i, j).wait_recv()

            def add2(n, unused):
                zz, j = n // 2, n % 2
                yy = y * (1 - s) + j * s
                xx = j * (1 - s) + x * s
                self.add(self.cut(self.held, i, zz, yy, xx), self.cut(self.gots[1], i, zz, j))
                return unused

            lax.fori_loop(0, 8, add2, 0)
            self.second(i).start()
        elif t == 3:
            self.second(i).wait_recv()

            def add3(zz, unused):
                self.add(self.cut(self.held, i, zz, y, x), self.cut(self.gots[2], i, zz))
                return unused

            lax.fori_loop(0, 4, add3, 0)
            for k in (1, 2, 3):
                self.along_z(i, k).start()
        elif t == 4:
            for k in (1, 2, 3):
                self.along_z(i, k).wait_recv()
            total = self.cut(self.held, i, z, y, x)[...].astype(F32)
            for k in (0, 1, 2):
                total = total + self.cut(self.gots[3], i, k)[...].astype(F32)
            self.out(i)[...] = total

    def sent(self):
        for i in range(len(self.chunks)):
            self.across(i).wait_send()
            for j in (0, 1):
                self.first(i, j).wait_send()
            self.second(i).wait_send()
            for k in (1, 2, 3):
                self.along_z(i, k).wait_send()


def got_shapes(sizes):
    return [pltpu.VMEM(lead + size, BF16) for lead in ((4, 2, 2), (4, 2), (4,), (3,)) for size in sizes]


def got_levels(refs, count):
    return [refs[level * count : (level + 1) * count] for level in range(4)]


def head_of(shape):
    return lax.broadcasted_iota(jnp.int32, shape, len(shape) - 1) // 64


def pick(values, head):
    return jnp.where(head_of(values.shape) == head, values, jnp.zeros_like(values))


def attend_pair(queries, keys, values):
    length = queries.shape[0]
    mixed, logs = [], []
    for head in (0, 1):
        scores = dot_nt(pick(queries, head), keys)
        top = jnp.max(scores, axis=1, keepdims=True)
        powers = jnp.exp(scores - top)
        total = jnp.sum(powers, axis=1, keepdims=True)
        mixed.append(dot_nn(powers.astype(BF16), values) * (1.0 / total))
        column = jnp.broadcast_to(top + jnp.log(total), (length, LANES))
        logs.append(jnp.transpose(column)[0:1])
    attended = jnp.where(head_of(mixed[0].shape) == 0, mixed[0], mixed[1]).astype(BF16)
    return attended, jnp.concatenate(logs, axis=0)


def attend_pair_back(queries, keys, values, attended, grad, logs):
    keys_t = jnp.transpose(keys)
    products = jnp.transpose(grad.astype(F32) * attended.astype(F32))
    dk = jnp.zeros(keys.shape, F32)
    dv = jnp.zeros(keys.shape, F32)
    dq_t = []
    for head in (0, 1):
        offset = jnp.sum(products[64 * head : 64 * head + 64], axis=0, keepdims=True)
        q_head = pick(queries, head)
        g_head = pick(grad, head)
        scores_t = dot_nt(keys, q_head)
        probs_t = jnp.exp(scores_t - logs[head : head + 1, :])
        slopes_t = dot_nt(values, g_head)
        score_grad_t = (probs_t * (slopes_t - offset)).astype(BF16)
        dv += dot_nn(probs_t.astype(BF16), g_head)
        dk += dot_nn(score_grad_t, q_head)
        dq_t.append(dot_nn(keys_t[64 * head : 64 * head + 64], score_grad_t))
    dq = jnp.transpose(jnp.concatenate(dq_t, axis=0)) * SCALE
    return dq.astype(BF16), dk.astype(BF16), dv.astype(BF16)


def attend_kernel(q_ref, k_ref, v_ref, o_ref, lse_ref):
    keys = k_ref[:, 0].reshape(-1, PAIR)
    values = v_ref[:, 0].reshape(-1, PAIR)
    o_ref[0], lse_ref[0, 0] = attend_pair(q_ref[0], keys, values)


def attend(queries, keys, values):
    micro, length, width = queries.shape
    parts = keys.shape[0]
    pairs = width // PAIR
    row = pl.BlockSpec((1, length, PAIR), lambda m, p: (m, 0, p))
    col = pl.BlockSpec((parts, 1, length, PAIR), lambda m, p: (0, m, 0, p))
    return pl.pallas_call(
        attend_kernel,
        grid=(micro, pairs),
        in_specs=[row, col, col],
        out_specs=[row, pl.BlockSpec((1, 1, 2, length), lambda m, p: (m, p, 0, 0))],
        out_shape=[
            jax.ShapeDtypeStruct(queries.shape, BF16),
            jax.ShapeDtypeStruct((micro, pairs, 2, length), F32),
        ],
        compiler_params=pltpu.CompilerParams(vmem_limit_bytes=VMEM_LIMIT),
        name="attend",
    )(queries, keys, values)


def attend_back_kernel(q_ref, k_ref, v_ref, o_ref, g_ref, lse_ref, dq_ref, dk_ref, dv_ref):
    parts, length = k_ref.shape[0], q_ref.shape[1]
    keys = k_ref[:, 0].reshape(-1, PAIR)
    values = v_ref[:, 0].reshape(-1, PAIR)
    dq, dk, dv = attend_pair_back(q_ref[0], keys, values, o_ref[0], g_ref[0], lse_ref[0, 0])
    dq_ref[0] = dq
    dk_ref[:, 0] = dk.reshape(parts, length, PAIR)
    dv_ref[:, 0] = dv.reshape(parts, length, PAIR)


def attend_back(queries, keys, values, attended, grad, lse):
    micro, length, width = queries.shape
    parts = keys.shape[0]
    pairs = width // PAIR
    row = pl.BlockSpec((1, length, PAIR), lambda m, p: (m, 0, p))
    col = pl.BlockSpec((parts, 1, length, PAIR), lambda m, p: (0, m, 0, p))
    log = pl.BlockSpec((1, 1, 2, length), lambda m, p: (m, p, 0, 0))
    return pl.pallas_call(
        attend_back_kernel,
        grid=(micro, pairs),
        in_specs=[row, col, col, row, row, log],
        out_specs=[row, col, col],
        out_shape=[
            jax.ShapeDtypeStruct((micro, length, width), BF16),
            jax.ShapeDtypeStruct((parts, micro, length, width), BF16),
            jax.ShapeDtypeStruct((parts, micro, length, width), BF16),
        ],
        compiler_params=pltpu.CompilerParams(vmem_limit_bytes=VMEM_LIMIT),
        name="attend_back",
    )(queries, keys, values, attended, grad, lse)


def project_kernel(own_ref, all_ref, wq_ref, wk_ref, wv_ref, small_ref, q_ref, k_ref, v_ref, bias):
    @pl.when(pl.program_id(0) == 0)
    def _():
        bias[...] = spread(small_ref[:, 0:8].astype(F32), bias.shape[1])

    @pl.when(pl.program_id(0) < own_ref.shape[0] * 2)
    def _():
        queries = dot_nn(own_ref[0], wq_ref[...]) + bias[0:1]
        q_ref[0] = (queries.astype(BF16).astype(F32) * SCALE).astype(BF16)

    rows = all_ref[0, 0]
    k_ref[0, 0] = dot_nn(rows, wk_ref[...]).astype(BF16)
    v_ref[0, 0] = (dot_nn(rows, wv_ref[...]) + bias[1:2]).astype(BF16)


def project(own, all_rows, wq, wk, wv, small):
    micro, length, width = own.shape
    parts = all_rows.shape[0]
    whole = lambda a: pl.BlockSpec(a.shape, lambda i: (0,) * a.ndim)
    last = micro - 1
    mine = pl.BlockSpec((1, length, width), lambda i: (jnp.minimum(i, last), 0, 0))
    every = pl.BlockSpec((1, 1, length, width), lambda i: (i // micro, i % micro, 0, 0))
    return pl.pallas_call(
        project_kernel,
        grid=(parts * micro,),
        in_specs=[mine, every, whole(wq), whole(wk), whole(wv), whole(small)],
        out_specs=[mine, every, every],
        out_shape=[
            jax.ShapeDtypeStruct((micro, length, width), BF16),
            jax.ShapeDtypeStruct((parts, micro, length, width), BF16),
            jax.ShapeDtypeStruct((parts, micro, length, width), BF16),
        ],
        scratch_shapes=[pltpu.VMEM((8, width), F32)],
        compiler_params=pltpu.CompilerParams(vmem_limit_bytes=VMEM_LIMIT),
        name="project",
    )(own, all_rows, wq, wk, wv, small)


SMALL, WQ, WK, WV, WO, WIN, WOUT = range(7)


def forward_chunks(shapes):
    chunks = [(SMALL, 0, shapes[SMALL][0], 0, LANES)]
    rows, width = shapes[WQ]
    for c in range(0, width, GROUP):
        chunks += [(w, 0, rows, c, GROUP) for w in (WQ, WK, WV)]
    chunks.append((WO, 0, rows, 0, width))
    chunks += [(WIN, 0, rows, c, CHUNK) for c in range(0, shapes[WIN][1], CHUNK)]
    chunks += [(WOUT, 0, shapes[WOUT][0], c, GROUP) for c in range(0, width, GROUP)]
    return chunks


def forward_kernel(chunks, *refs):
    shards, x_ref, fulls = refs[:7], refs[7], refs[8:15]
    q_out, k_out, v_out, att_ref, lse_ref = refs[15:20]
    other, pieces, weights, small, bias, q_s, k_s, v_s = refs[20:28]
    own_sem, send, recv, row_send, row_recv, load, back = refs[28:]
    where = place()
    s, z, y, x = where
    width = q_s.shape[2]
    length = q_s.shape[1]
    groups = width // GROUP
    greet(s, z, y, x)
    gather = Gather(shards, fulls, own_sem, send, recv, chunks, where)
    rows = remote(x_ref, other, row_send, row_recv, device(1 - s, z, y, x))
    gather.begin()
    rows.start()

    def fetch(g):
        copies = []
        for n, w in enumerate((WQ, WK, WV)):
            source = fulls[w].at[:, :, :, :, :, g * GROUP : (g + 1) * GROUP]
            target = pieces.at[:, :, :, :, :, n * GROUP : (n + 1) * GROUP]
            copies.append(pltpu.make_async_copy(source, target, load.at[n]))
        return copies

    def arrived(g):
        for i in range(3 * g + 1, 3 * g + 4):
            gather.across(i).wait_recv()
        for copy in fetch(g):
            copy.start()

    def written(g):
        cols = slice(g * GROUP, (g + 1) * GROUP)
        return [
            pltpu.make_async_copy(q_s.at[:, :, cols], q_out.at[:, :, cols], back.at[g, 0]),
            pltpu.make_async_copy(k_s.at[:, :, :, cols], k_out.at[:, :, :, cols], back.at[g, 1]),
            pltpu.make_async_copy(v_s.at[:, :, :, cols], v_out.at[:, :, :, cols], back.at[g, 2]),
        ]

    ready = 4 + 2 * LAG
    for n in range(ready):
        gather.step(n)
    gather.across(0).wait_recv()
    small_copy = pltpu.make_async_copy(fulls[SMALL], small, load.at[3])
    small_copy.start()
    arrived(0)
    small_copy.wait()
    vectors = small[...].reshape(32, 16, LANES)[:, 0:8]
    bias[...] = spread(vectors.astype(F32), width)
    rows.wait_recv()

    for g in range(groups):
        for copy in fetch(g):
            copy.wait()
        weights[...] = pieces[...].reshape(weights.shape)
        cols = slice(g * GROUP, (g + 1) * GROUP)

        def mine(m, unused):
            made = dot_nn(x_ref[m], weights[...])
            queries = made[:, :GROUP] + bias[0:1, cols]
            q_s[m, :, cols] = (queries.astype(BF16).astype(F32) * SCALE).astype(BF16)
            k_s[0, m, :, cols] = made[:, GROUP : 2 * GROUP].astype(BF16)
            v_s[0, m, :, cols] = (made[:, 2 * GROUP :] + bias[1:2, cols]).astype(BF16)
            return unused

        def others(m, unused):
            made = dot_nn(other[m], weights[:, GROUP:])
            k_s[1, m, :, cols] = made[:, :GROUP].astype(BF16)
            v_s[1, m, :, cols] = (made[:, GROUP:] + bias[1:2, cols]).astype(BF16)
            return unused

        lax.fori_loop(0, 2, mine, 0)
        lax.fori_loop(0, 2, others, 0)
        for copy in written(g):
            copy.start()

        def one(j, unused):
            for n in range(3):

                @pl.when(j == n)
                def _():
                    gather.step(ready + 3 * g + n)

            if g + 1 < groups:

                @pl.when(j == 3)
                def _():
                    arrived(g + 1)

            m = j // 2
            p = 2 * g + j % 2
            lanes = pl.ds(pl.multiple_of(p * PAIR, PAIR), PAIR)
            keys = k_s[:, m, :, lanes].reshape(2 * length, PAIR)
            values = v_s[:, m, :, lanes].reshape(2 * length, PAIR)
            attended, logs = attend_pair(q_s[m, :, lanes], keys, values)
            att_ref[m, :, lanes] = attended
            lse_ref[m, p] = logs
            return unused

        lax.fori_loop(0, 4, one, 0)

    for n in range(ready + 3 * groups, gather.steps()):
        gather.step(n)
    for i in range(3 * groups + 1, len(chunks)):
        gather.across(i).wait_recv()
    for g in range(groups):
        for copy in written(g):
            copy.wait()
    rows.wait_send()
    gather.sent()


def forward_box(shards, own):
    micro, length, width = own.shape
    chunks = forward_chunks([a.shape for a in shards])
    any_spec = pl.BlockSpec(memory_space=pl.ANY)
    vmem_spec = pl.BlockSpec(memory_space=pltpu.VMEM)
    count = len(chunks)
    pairs = width // PAIR
    twice = (2, micro, length, width)
    outs = pl.pallas_call(
        functools.partial(forward_kernel, chunks),
        out_shape=[jax.ShapeDtypeStruct((2, 4, 2, 2) + a.shape, a.dtype) for a in shards]
        + [
            jax.ShapeDtypeStruct(own.shape, BF16),
            jax.ShapeDtypeStruct(twice, BF16),
            jax.ShapeDtypeStruct(twice, BF16),
            jax.ShapeDtypeStruct(own.shape, BF16),
            jax.ShapeDtypeStruct((micro, pairs, 2, length), F32),
        ],
        in_specs=[vmem_spec] * 8,
        out_specs=[any_spec] * 10 + [vmem_spec] * 2,
        scratch_shapes=[
            pltpu.VMEM(own.shape, BF16),
            pltpu.VMEM((2, 4, 2, 2, width // 32, 3 * GROUP), BF16),
            pltpu.VMEM((width, 3 * GROUP), BF16),
            pltpu.VMEM((2, 4, 2, 2, 16, LANES), BF16),
            pltpu.VMEM((8, width), F32),
            pltpu.VMEM(own.shape, BF16),
            pltpu.VMEM(twice, BF16),
            pltpu.VMEM(twice, BF16),
            pltpu.SemaphoreType.DMA((count,)),
            pltpu.SemaphoreType.DMA((count, 7)),
            pltpu.SemaphoreType.DMA((count, 7)),
            pltpu.SemaphoreType.DMA,
            pltpu.SemaphoreType.DMA,
            pltpu.SemaphoreType.DMA((4,)),
            pltpu.SemaphoreType.DMA((width // GROUP, 3)),
        ],
        compiler_params=pltpu.CompilerParams(
            collective_id=1, has_side_effects=True, vmem_limit_bytes=VMEM_LIMIT
        ),
        name="forward_attention",
    )(*shards, own)
    fulls = [full.reshape((-1, full.shape[-1])) for full in outs[1:7]]
    return [outs[0].reshape(32, 16, LANES)] + fulls, outs[7:]


def mean_rows(values):
    return jnp.mean(values, axis=-1, keepdims=True)


def rows_kernel(
    x_ref,
    att_ref,
    cot_ref,
    wo_ref,
    win_ref,
    wout_ref,
    small_ref,
    out_ref,
    hidden_ref,
    active_ref,
    inner_grad_ref,
    feed_ref,
    branch_ref,
    mixed_ref,
    first_ref,
    smallg_ref,
    vec,
    ib,
    slope,
    vecg,
    ibg,
):
    step = pl.program_id(0)
    chunks = win_ref.shape[1] // CHUNK

    @pl.when(step == 0)
    def _():
        vec[...] = spread(small_ref[:, 0:8].astype(F32), vec.shape[1])
        ib[...] = spread(small_ref[:, 8:16].astype(F32), ib.shape[1])
        vecg[...] = jnp.zeros_like(vecg)
        ibg[...] = jnp.zeros_like(ibg)

    o_b, g1, s1, outer_b, g2, s2 = (vec[i : i + 1] for i in range(2, 8))
    first_sum = x_ref[...].astype(F32) + (dot_nn(att_ref[...], wo_ref[...]) + o_b)
    centred = first_sum - mean_rows(first_sum)
    r1 = lax.rsqrt(mean_rows(centred * centred) + EPS)
    n1 = centred * r1
    hidden = n1 * g1 + s1
    hidden_low = hidden.astype(BF16)
    hidden_ref[...] = hidden_low
    total = hidden + outer_b
    for c in range(chunks):
        cols = slice(c * CHUNK, (c + 1) * CHUNK)
        v = dot_nn(hidden_low, win_ref[:, cols]) + ib[0:1, cols]
        square = v * v
        t = jnp.tanh(v * (GELU_C + (GELU_C * GELU_A) * square))
        half = 0.5 * (1.0 + t)
        active = (v * half).astype(BF16)
        active_ref[:, cols] = active
        slope[:, cols] = half + (0.5 * v) * (1.0 - t * t) * (
            GELU_C + (3.0 * GELU_C * GELU_A) * square
        )
        total = total + dot_nn(active, wout_ref[cols, :])
    centred = total - mean_rows(total)
    r2 = lax.rsqrt(mean_rows(centred * centred) + EPS)
    n2 = centred * r2
    out_ref[...] = (n2 * g2 + s2).astype(BF16)
    e = cot_ref[...].astype(F32)
    m = e * g2
    second = (m - mean_rows(m) - n2 * mean_rows(m * n2)) * r2
    feed = second.astype(BF16)
    feed_ref[...] = feed
    vecg[6:7] += jnp.sum(e * n2, axis=0, keepdims=True)
    vecg[7:8] += jnp.sum(e, axis=0, keepdims=True)
    vecg[5:6] += jnp.sum(feed.astype(F32), axis=0, keepdims=True)
    e = second
    for c in range(chunks):
        cols = slice(c * CHUNK, (c + 1) * CHUNK)
        inner_grad = (dot_nt(feed, wout_ref[cols, :]) * slope[:, cols]).astype(BF16)
        inner_grad_ref[:, cols] = inner_grad
        ibg[0:1, cols] += jnp.sum(inner_grad.astype(F32), axis=0, keepdims=True)
        e = e + dot_nt(inner_grad, win_ref[:, cols])
    m = e * g1
    first = (m - mean_rows(m) - n1 * mean_rows(m * n1)) * r1
    first_ref[...] = first
    branch = first.astype(BF16)
    branch_ref[...] = branch
    vecg[3:4] += jnp.sum(e * n1, axis=0, keepdims=True)
    vecg[4:5] += jnp.sum(e, axis=0, keepdims=True)
    vecg[2:3] += jnp.sum(branch.astype(F32), axis=0, keepdims=True)
    mixed_ref[...] = dot_nt(branch, wo_ref[...]).astype(BF16)

    @pl.when(step == pl.num_programs(0) - 1)
    def _():
        devices = smallg_ref.shape[0]
        smallg_ref[:, 0:8] = collect(vecg[...], devices).astype(BF16)
        smallg_ref[:, 8:16] = collect(ibg[...], devices).astype(BF16)


def row_stage(x, attended, cotangent, wo, win, wout, small):
    rows, width = x.shape
    hidden_width = win.shape[1]
    block = min(ROWS, rows)
    whole = lambda a: pl.BlockSpec(
        a.shape, lambda i: (0,) * a.ndim, pipeline_mode=pl.Buffered(1)
    )
    narrow = pl.BlockSpec((block, width), lambda i: (i, 0))
    wide = pl.BlockSpec((block, hidden_width), lambda i: (i, 0))
    low = jax.ShapeDtypeStruct((rows, width), BF16)
    low_wide = jax.ShapeDtypeStruct((rows, hidden_width), BF16)
    return pl.pallas_call(
        rows_kernel,
        grid=(rows // block,),
        in_specs=[narrow] * 3 + [whole(a) for a in (wo, win, wout, small)],
        out_specs=[
            narrow,
            narrow,
            wide,
            wide,
            narrow,
            narrow,
            narrow,
            narrow,
            pl.BlockSpec(small.shape, lambda i: (0, 0, 0)),
        ],
        out_shape=[
            low,
            low,
            low_wide,
            low_wide,
            low,
            low,
            low,
            jax.ShapeDtypeStruct((rows, width), F32),
            jax.ShapeDtypeStruct(small.shape, BF16),
        ],
        scratch_shapes=[
            pltpu.VMEM((8, width), F32),
            pltpu.VMEM((8, hidden_width), F32),
            pltpu.VMEM((block, hidden_width), F32),
            pltpu.VMEM((8, width), F32),
            pltpu.VMEM((8, hidden_width), F32),
        ],
        compiler_params=pltpu.CompilerParams(vmem_limit_bytes=VMEM_LIMIT),
        name="row_stage",
    )(x, attended, cotangent, wo, win, wout, small)


def product_kernel(left_ref, right_ref, out_ref):
    out_ref[...] = dot_tn(left_ref[...], right_ref[...]).astype(BF16)


def product(left, right, block_m, block_n):
    depth, rows = left.shape
    cols = right.shape[1]
    return pl.pallas_call(
        product_kernel,
        grid=(rows // block_m, cols // block_n),
        in_specs=[
            pl.BlockSpec((depth, block_m), lambda i, j: (0, i)),
            pl.BlockSpec((depth, block_n), lambda i, j: (0, j)),
        ],
        out_specs=pl.BlockSpec((block_m, block_n), lambda i, j: (i, j)),
        out_shape=jax.ShapeDtypeStruct((rows, cols), BF16),
        compiler_params=pltpu.CompilerParams(vmem_limit_bytes=VMEM_LIMIT),
        name="weight_gradient",
    )(left, right)


def input_kernel(first_ref, dq_ref, dk_ref, dv_ref, wq_ref, wk_ref, wv_ref, out_ref, vecg_ref, acc):
    step = pl.program_id(0)

    @pl.when(step == 0)
    def _():
        acc[...] = jnp.zeros_like(acc)

    out_ref[...] = (
        first_ref[...]
        + dot_nt(dq_ref[...], wq_ref[...])
        + dot_nt(dk_ref[...], wk_ref[...])
        + dot_nt(dv_ref[...], wv_ref[...])
    ).astype(BF16)
    acc[0:1] += jnp.sum(dq_ref[...].astype(F32), axis=0, keepdims=True)
    acc[1:2] += jnp.sum(dv_ref[...].astype(F32), axis=0, keepdims=True)

    @pl.when(step == pl.num_programs(0) - 1)
    def _():
        vecg_ref[:, 0:8] = collect(acc[...], vecg_ref.shape[0]).astype(BF16)
        vecg_ref[:, 8:16] = jnp.zeros((vecg_ref.shape[0], 8, LANES), BF16)


def input_stage(first, dq, dk, dv, wq, wk, wv, small_shape):
    rows, width = first.shape
    block = min(ROWS, rows)
    narrow = pl.BlockSpec((block, width), lambda i: (i, 0))
    whole = pl.BlockSpec((width, width), lambda i: (0, 0))
    return pl.pallas_call(
        input_kernel,
        grid=(rows // block,),
        in_specs=[narrow] * 4 + [whole] * 3,
        out_specs=[narrow, pl.BlockSpec(small_shape, lambda i: (0, 0, 0))],
        out_shape=[
            jax.ShapeDtypeStruct((rows, width), BF16),
            jax.ShapeDtypeStruct(small_shape, BF16),
        ],
        scratch_shapes=[pltpu.VMEM((8, width), F32)],
        compiler_params=pltpu.CompilerParams(vmem_limit_bytes=VMEM_LIMIT),
        name="input_stage",
    )(first, dq, dk, dv, wq, wk, wv)


PLAN_IN = ((1, 2, 6, 9, 11), (1, 4, 6, 8, 18), (1, 2, 5, 7, 19), (0, 1, 9, 11, 16),)
PLAN_OUT = ((0, 1, 5, 9, 19), (9, 10, 13, 15, 17), (2, 8, 11, 13, 19))
PLAN_O, PLAN_SMALL, PLAN_SMALL2 = (2, 5, 9, 10, 19), (5, 6, 9, 10, 19), (13, 15, 16, 18, 24)
PLAN_QKV = (
    (6, 7, 10, 12, 19),
    (10, 11, 14, 16, 23),
    (13, 14, 16, 20, 23),
    (13, 15, 20, 21, 24),
)
G_IN, G_OUT, G_O, G_SMALL, G_QKV, G_SMALL2 = 0, 1, 2, 3, 4, 8
UNITS = 12
BACK_STEPS = UNITS + 5
BACK_PLAN = (
    [(G_OUT, c * GROUP, GROUP, plan) for c, plan in enumerate(PLAN_OUT)]
    + [(G_IN, c * CHUNK, CHUNK, plan) for c, plan in enumerate(PLAN_IN)]
    + [(G_O, 0, CHUNK, PLAN_O), (G_SMALL, 0, LANES, PLAN_SMALL)]
    + [(G_QKV + g, 0, 3 * w, plan) for g, (w, plan) in enumerate(zip((256, 256, 128, 128), PLAN_QKV))]
    + [(G_SMALL2, 0, LANES, PLAN_SMALL2)]
)
FETCHED = 9


def unit_of(step):
    u = jnp.clip(step, 0, UNITS - 1)
    return u % 2, u // 2


def backward_kernel(sizes, *refs):
    terms1 = refs[:4]
    (q_ref, k_ref, v_ref, o_ref, g_ref, lse_ref, x_in, wq_in, wk_in, wv_in, first_ref) = refs[4:15]
    outs, dx_ref = refs[15:24], refs[24]
    held1 = refs[25:29]
    broad, slim, small2, sums = refs[29:33]
    gots = got_levels(refs[33:69], 9)
    dq_all, dk_all, dv_all, away, far, x_t, x_v, wq_v, wk_v, wv_v = refs[69:79]
    load, send, recv, far_send, far_recv, bring = refs[79:]
    where = place()
    s, z, y, x = where
    step = pl.program_id(0)
    length = q_ref.shape[1]
    rows = dq_all.shape[0] * length
    chunks = [(a, 0, sizes[a][0], c, nc) for a, c, nc, _ in BACK_PLAN]
    terms = list(terms1) + [a.at[g] for a in (broad, slim) for g in (0, 1)] + [small2]
    held = list(held1) + [a.at[g, s] for a in (broad, slim) for g in (0, 1)] + [small2.at[s]]
    scatter = Scatter(terms, held, gots, outs, load, send, recv, chunks, where)
    copies = [
        pltpu.make_async_copy(a, b, bring.at[n])
        for n, (a, b) in enumerate(zip((x_in, wq_in, wk_in, wv_in), (x_v, wq_v, wk_v, wv_v)))
    ]

    def far_copies(u):
        m, p = unit_of(u)
        lanes = pl.ds(pl.multiple_of(p * PAIR, PAIR), PAIR)
        target = device(1 - s, z, y, x)
        return [
            remote(
                away.at[u, n], far.at[n, m, :, lanes], far_send.at[u, n], far_recv.at[u, n], target
            )
            for n in (0, 1)
        ]

    @pl.when(step == 0)
    def _():
        for copy in copies:
            copy.start()
        greet(s, z, y, x)

    for n in range(BACK_STEPS):
        todo = [(t, i) for i, c in enumerate(BACK_PLAN) for t, at in enumerate(c[3]) if at == n]
        if todo:

            @pl.when(step == n)
            def _():
                for t, i in sorted(todo, reverse=True):
                    scatter.stage(t, i)

    @pl.when((step > 0) & (step < UNITS))
    def _():
        for copy in far_copies(step - 1):
            copy.start()

    @pl.when(step == 1)
    def _():
        copies[0].wait()
        x_t[...] = jnp.transpose(x_v[...])

    @pl.when(step < UNITS)
    def _():
        m, p = unit_of(step)
        lanes = pl.ds(pl.multiple_of(p * PAIR, PAIR), PAIR)
        keys = k_ref[:, 0].reshape(-1, PAIR)
        values = v_ref[:, 0].reshape(-1, PAIR)
        dq, dk, dv = attend_pair_back(q_ref[0], keys, values, o_ref[0], g_ref[0], lse_ref[0, 0])
        dq_all[m, :, lanes] = dq
        dk_all[m, :, lanes] = dk[:length]
        dv_all[m, :, lanes] = dv[:length]
        away[step, 0] = dk[length:]
        away[step, 1] = dv[length:]

    @pl.when(step == UNITS)
    def _():
        for copy in far_copies(UNITS - 1):
            copy.start()

    def products(to, g, unit, units, lane, lanes):
        for n in range(units):
            for copy in far_copies(unit + n):
                copy.wait_recv()
        cols = pl.ds(pl.multiple_of(lane, PAIR), lanes)
        for m in range(dq_all.shape[0]):
            for n, whole in enumerate((dk_all, dv_all)):
                whole[m, :, cols] = whole[m, :, cols] + far[n, m, :, cols]
        for n, whole in enumerate((dq_all, dk_all, dv_all)):
            value = dot_nn(x_t[...], whole[:, :, cols].reshape(rows, lanes)).astype(BF16)
            to[g, :, :, :, :, :, n * lanes : (n + 1) * lanes] = value.reshape(
                (2, 4, 2, 2) + (sizes[G_QKV][0], lanes)
            )

    @pl.when((step == 5) | (step == 9))
    def _():
        g = (step - 5) // 4
        products(broad, g, 4 * g, 4, g * GROUP, GROUP)

    @pl.when((step == 11) | (step == 12))
    def _():
        g = step - 11
        products(slim, g, 8 + 2 * g, 2, 2 * GROUP + g * PAIR, PAIR)

    @pl.when(step == UNITS)
    def _():
        sums[...] = jnp.zeros_like(sums)
        for n, whole in enumerate((dq_all, dv_all)):
            total = jnp.sum(whole[...].astype(F32).reshape(rows, -1), axis=0, keepdims=True)
            sums[n : n + 1] = total
        small2[...] = jnp.zeros_like(small2)
        small2[:, :, :, :, 0:8] = (
            collect(sums[...], 32).astype(BF16).reshape((2, 4, 2, 2, 8, LANES))
        )
        for copy in copies[1:]:
            copy.wait()

    @pl.when(step > UNITS)
    def _():
        block = first_ref.shape[0]
        r = step - UNITS - 1
        per = length // block
        at = pl.ds(pl.multiple_of((r % per) * block, block), block)
        dx_ref[...] = (
            first_ref[...]
            + dot_nt(dq_all[r // per, at], wq_v[...])
            + dot_nt(dk_all[r // per, at], wk_v[...])
            + dot_nt(dv_all[r // per, at], wv_v[...])
        ).astype(BF16)

    @pl.when(step == BACK_STEPS - 1)
    def _():
        late = [(at, -t, i) for i, c in enumerate(BACK_PLAN) for t, at in enumerate(c[3])]
        for at, t, i in sorted(late):
            if at >= BACK_STEPS:
                scatter.stage(-t, i)
        for u in range(UNITS):
            for copy in far_copies(u):
                copy.wait_send()
        scatter.sent()


def backward_box(win_grad, wout_grad, wo_grad, small, q, k, v, o, g, lse, tokens, wq, wk, wv, first):
    micro, length, width = q.shape
    rows = tokens.shape[0]
    narrow, thin = (width // 32, width), (16, LANES)
    sizes = [(width // 32, win_grad.shape[1]), (wout_grad.shape[0] // 32, width), narrow, thin]
    sizes += [(narrow[0], 3 * w) for w in (GROUP, GROUP, PAIR, PAIR)] + [thin]
    terms = [
        a.reshape((2, 4, 2, 2) + size)
        for a, size in zip((win_grad, wout_grad, wo_grad, small), sizes)
    ]
    block = rows // 4

    def at(i):
        return unit_of(i)

    row = pl.BlockSpec((1, length, PAIR), lambda i: (at(i)[0], 0, at(i)[1]))
    col = pl.BlockSpec((2, 1, length, PAIR), lambda i: (0, at(i)[0], 0, at(i)[1]))
    log = pl.BlockSpec((1, 1, 2, length), lambda i: (at(i)[0], at(i)[1], 0, 0))
    flat = pl.BlockSpec((block, width), lambda i: (jnp.clip(i - UNITS - 1, 0, 3), 0))
    any_spec = pl.BlockSpec(memory_space=pl.ANY)
    square = pltpu.VMEM((width, width), BF16)
    low = pltpu.VMEM((micro, length, width), BF16)
    outs = pl.pallas_call(
        functools.partial(backward_kernel, sizes),
        grid=(BACK_STEPS,),
        in_specs=[any_spec] * 4 + [row, col, col, row, row, log] + [any_spec] * 4 + [flat],
        out_specs=[pl.BlockSpec(size, lambda i: (0, 0)) for size in sizes] + [flat],
        out_shape=[jax.ShapeDtypeStruct(size, F32) for size in sizes]
        + [jax.ShapeDtypeStruct((rows, width), BF16)],
        scratch_shapes=[pltpu.VMEM((4, 2, 2) + size, BF16) for size in sizes[:4]]
        + [
            pltpu.VMEM((2, 2, 4, 2, 2) + sizes[G_QKV], BF16),
            pltpu.VMEM((2, 2, 4, 2, 2) + sizes[G_QKV + 2], BF16),
            pltpu.VMEM((2, 4, 2, 2) + thin, BF16),
            pltpu.VMEM((8, width), F32),
        ]
        + got_shapes(sizes)
        + [
            low,
            low,
            low,
            pltpu.VMEM((UNITS, 2, length, PAIR), BF16),
            pltpu.VMEM((2, micro, length, width), BF16),
            pltpu.VMEM((width, rows), BF16),
            pltpu.VMEM((rows, width), BF16),
            square,
            square,
            square,
            pltpu.SemaphoreType.DMA((FETCHED,)),
            pltpu.SemaphoreType.DMA((len(BACK_PLAN), 7)),
            pltpu.SemaphoreType.DMA((len(BACK_PLAN), 7)),
            pltpu.SemaphoreType.DMA((UNITS, 2)),
            pltpu.SemaphoreType.DMA((UNITS, 2)),
            pltpu.SemaphoreType.DMA((4,)),
        ],
        compiler_params=pltpu.CompilerParams(
            collective_id=2, has_side_effects=True, vmem_limit_bytes=VMEM_LIMIT
        ),
        name="backward_attention",
    )(*terms, q, k, v, o, g, lse, tokens, wq, wk, wv, first)
    return outs[:9], outs[9]


def hand_out_kernel(*refs):
    (win, wout, wo, small) = refs[:4]
    qkv, small2, outs = refs[4:8], refs[8], refs[9:]
    (wq_o, qb, wk_o, wv_o, vb, wo_o, ob, g1, s1, win_o, ib, wout_o, outb, g2, s2) = outs
    win_o[...] = win[...]
    wout_o[...] = wout[...]
    wo_o[...] = wo[...]
    first = 0
    for group in qkv:
        lanes = group.shape[1] // 3
        for n, target in enumerate((wq_o, wk_o, wv_o)):
            target[:, first : first + lanes] = group[:, n * lanes : (n + 1) * lanes]
        first += lanes
    piece = qb.shape[1]
    qb[...] = small2[0:1, :piece]
    vb[...] = small2[1:2, :piece]
    for row, target in zip(range(2, 8), (ob, g1, s1, outb, g2, s2)):
        target[...] = small[row : row + 1, :piece]
    ib[...] = small[8:9, : ib.shape[1]]


def hand_out(win, wout, wo, small, qkv, small2, piece, wide):
    vmem_spec = pl.BlockSpec(memory_space=pltpu.VMEM)
    line = jax.ShapeDtypeStruct((1, piece), F32)
    like = lambda a: jax.ShapeDtypeStruct(a.shape, F32)
    shapes = [like(wo), line, like(wo), like(wo), line, like(wo), line, line, line, like(win)]
    shapes += [jax.ShapeDtypeStruct((1, wide), F32), like(wout), line, line, line]
    outs = pl.pallas_call(
        hand_out_kernel,
        in_specs=[vmem_spec] * 9,
        out_specs=[vmem_spec] * 15,
        out_shape=shapes,
        compiler_params=pltpu.CompilerParams(vmem_limit_bytes=VMEM_LIMIT),
        name="hand_out",
    )(win, wout, wo, small, *qkv, small2)
    return [a.reshape(-1) if a.shape[0] == 1 else a for a in outs]


def body(
    inputs,
    cotangent,
    query_weight,
    query_bias,
    key_weight,
    value_weight,
    value_bias,
    output_weight,
    output_bias,
    first_gain,
    first_shift,
    inner_weight,
    inner_bias,
    outer_weight,
    outer_bias,
    second_gain,
    second_shift,
):
    micro, _, length, width = inputs.shape
    devices = lax.axis_size(("seq", "grp"))
    piece, wide = query_bias.shape[0], inner_bias.shape[0]
    boxed = lax.axis_size("seq") == 2 and lax.axis_size("grp") == 16 and piece % 8 == 0
    own = inputs[:, 0]
    tokens = own.reshape(-1, width)
    upstream = cotangent[:, 0].reshape(-1, width)
    vectors = jnp.stack(
        (
            query_bias,
            value_bias,
            output_bias,
            first_gain,
            first_shift,
            outer_bias,
            second_gain,
            second_shift,
        )
    )
    vectors = jnp.pad(vectors, ((0, 8), (0, LANES - piece)))
    small = vectors + jnp.pad(inner_bias[None], ((8, 7), (0, LANES - wide)))
    shards = (
        small,
        query_weight,
        key_weight,
        value_weight,
        output_weight,
        inner_weight,
        outer_weight,
    )
    if boxed:
        fulls, made = forward_box(shards, own)
        small, wq, wk, wv, wo, win, wout = fulls
        queries, keys, values, attended, lse = made
    else:
        fulls = [lax.all_gather(a, ("seq", "grp"), axis=0, tiled=True) for a in shards]
        small, wq, wk, wv, wo, win, wout = fulls
        small = small.reshape(devices, 16, LANES)
        all_rows = lax.all_gather(own, "seq", axis=0)
        queries, keys, values = project(own, all_rows, wq, wk, wv, small)
        attended, lse = attend(queries, keys, values)
    flat = attended.reshape(-1, width)
    (
        layer_out,
        hidden_low,
        active,
        inner_grad,
        feed_grad,
        branch_grad,
        mixed_grad,
        first_grad,
        small_grad,
    ) = row_stage(tokens, flat, upstream, wo, win, wout, small)
    mixed_grad = mixed_grad.reshape(micro, length, width)
    win_grad = product(hidden_low, inner_grad, 768, 768)
    wout_grad = product(active, feed_grad, 768, 768)
    wo_grad = product(flat, branch_grad, 768, 768)
    if boxed:
        summed, input_grad = backward_box(
            win_grad,
            wout_grad,
            wo_grad,
            small_grad,
            queries,
            keys,
            values,
            attended,
            mixed_grad,
            lse,
            tokens,
            wq,
            wk,
            wv,
            first_grad,
        )
    else:
        dq, dk, dv = attend_back(queries, keys, values, attended, mixed_grad, lse)
        dk = lax.psum_scatter(dk, "seq", scatter_dimension=0)
        dv = lax.psum_scatter(dv, "seq", scatter_dimension=0)
        dq, dk, dv = (a.reshape(-1, width) for a in (dq, dk, dv))
        input_grad, small2_grad = input_stage(
            first_grad, dq, dk, dv, wq, wk, wv, (devices, 16, LANES)
        )
        groups = [
            jnp.concatenate([a[:, c : c + w] for a in (dq, dk, dv)], axis=1)
            for c, w in ((0, GROUP), (GROUP, GROUP), (2 * GROUP, PAIR), (2 * GROUP + PAIR, PAIR))
        ]
        terms = [win_grad, wout_grad, wo_grad, small_grad.reshape(-1, LANES)]
        terms += [product(tokens, a, 768, a.shape[1]) for a in groups]
        terms.append(small2_grad.reshape(-1, LANES))
        summed = [
            lax.psum_scatter(a.astype(F32), ("seq", "grp"), scatter_dimension=0, tiled=True)
            for a in terms
        ]
        summed = lax.optimization_barrier(summed)
    grads = hand_out(*summed[:4], summed[4:8], summed[8], piece, wide)
    return (layer_out.reshape(inputs.shape), input_grad.reshape(inputs.shape)) + tuple(grads)


def solution(mesh):
    rows = P(("seq", "grp"), None)
    line = P(("seq", "grp"))
    tokens = P(None, "grp", "seq", None)
    return jax.shard_map(
        body,
        mesh=mesh,
        in_specs=(
            tokens,
            tokens,
            rows,
            line,
            rows,
            rows,
            line,
            rows,
            line,
            line,
            line,
            rows,
            line,
            rows,
            line,
            line,
            line,
        ),
        out_specs=(
            tokens,
            tokens,
            rows,
            line,
            rows,
            rows,
            line,
            rows,
            line,
            line,
            line,
            rows,
            line,
            rows,
            line,
            line,
            line,
        ),
        check_vma=False,
    )
```

```python
import functools

import jax
import jax.numpy as jnp
from jax import lax
from jax.experimental import pallas as pl
from jax.experimental.pallas import tpu as pltpu
from jax.sharding import PartitionSpec as P

HEADS = 12
SCALE = 0.125
EPS = 1e-05
PAIR = 128
ROWS = 256
CHUNK = 768
LANES = 128
GROUP = 256
LAG = 3
AHEAD = 4
VMEM_LIMIT = 64 * 1024 * 1024 - 65536
GELU_C = 0.7978845608028654
GELU_A = 0.044715
MESH = pl.DeviceIdType.MESH
F32 = jnp.float32
BF16 = jnp.bfloat16


def dot_nn(left, right):
    return lax.dot_general(left, right, (((1,), (0,)), ((), ())), preferred_element_type=F32)


def dot_nt(left, right):
    return lax.dot_general(left, right, (((1,), (1,)), ((), ())), preferred_element_type=F32)


def dot_tn(left, right):
    return lax.dot_general(left, right, (((0,), (0,)), ((), ())), preferred_element_type=F32)


def place():
    s = lax.axis_index("seq")
    g = lax.axis_index("grp")
    return s, g // 4, (g // 2) % 2, g % 2


def device(s, z, y, x):
    return (s, z * 4 + y * 2 + x)


def first_partner(s, z, y, x):
    return device(s, z, y * s + (1 - y) * (1 - s), x * (1 - s) + (1 - x) * s)


def second_partner(s, z, y, x):
    return device(s, z, y * (1 - s) + (1 - y) * s, x * s + (1 - x) * (1 - s))


def greet(s, z, y, x):
    barrier = pltpu.get_barrier_semaphore()
    partners = [device(1 - s, z, y, x), first_partner(s, z, y, x), second_partner(s, z, y, x)]
    partners += [device(s, (z + k) % 4, y, x) for k in (1, 2, 3)]
    for partner in partners:
        pl.semaphore_signal(barrier, inc=1, device_id=partner, device_id_type=MESH)
    pl.semaphore_wait(barrier, len(partners))


def remote(src, dst, send, recv, target):
    return pltpu.make_async_remote_copy(
        src_ref=src, dst_ref=dst, send_sem=send, recv_sem=recv, device_id=target, device_id_type=MESH
    )


def selector(lanes, width, piece):
    lane = lax.broadcasted_iota(jnp.int32, (lanes, width), 0)
    col = lax.broadcasted_iota(jnp.int32, (lanes, width), 1)
    return (lax.rem(col, piece) == lane).astype(BF16)


def owned(devices, rows, width, piece):
    dev = lax.broadcasted_iota(jnp.int32, (devices, rows, width), 0)
    col = lax.broadcasted_iota(jnp.int32, (devices, rows, width), 2)
    return col // piece == dev


def spread(pieces, width):
    devices, rows, lanes = pieces.shape
    piece = width // devices
    flat = pieces.reshape(devices * rows, lanes).astype(BF16)
    tiled = dot_nn(flat, selector(lanes, width, piece)).reshape(devices, rows, width)
    return jnp.sum(jnp.where(owned(devices, rows, width, piece), tiled, 0.0), axis=0)


def collect(values, devices):
    rows, width = values.shape
    piece = width // devices
    mine = jnp.where(owned(devices, rows, width, piece), values[None], 0.0)
    flat = mine.reshape(devices * rows, width).astype(BF16)
    return dot_nt(flat, selector(LANES, width, piece)).reshape(devices, rows, LANES)


class Gather:
    def __init__(self, shards, fulls, own_sem, send, recv, chunks, where):
        self.shards, self.fulls, self.chunks, self.where = shards, fulls, chunks, where
        self.own_sem, self.send, self.recv = own_sem, send, recv

    def piece(self, i):
        a, r, nr, c, nc = self.chunks[i]
        return self.shards[a].at[r : r + nr, c : c + nc]

    def full(self, i, *where):
        a, r, nr, c, nc = self.chunks[i]
        return self.fulls[a].at[(*where, slice(r, r + nr), slice(c, c + nc))]

    def own(self, i):
        return pltpu.make_async_copy(self.piece(i), self.full(i, *self.where), self.own_sem.at[i])

    def along_z(self, i, k):
        s, z, y, x = self.where
        return remote(
            self.piece(i),
            self.full(i, s, z, y, x),
            self.send.at[i, k - 1],
            self.recv.at[i, k - 1],
            device(s, (z + k) % 4, y, x),
        )

    def first(self, i):
        s, z, y, x = self.where
        part = self.full(i, s, slice(None), y, x)
        return remote(
            part, part, self.send.at[i, 3], self.recv.at[i, 3], second_partner(s, z, y, x)
        )

    def second(self, i, j):
        s, z, y, x = self.where
        yy = y * (1 - s) + j * s
        xx = j * (1 - s) + x * s
        part = self.full(i, s, slice(None), yy, xx)
        return remote(
            part, part, self.send.at[i, 4 + j], self.recv.at[i, 4 + j], first_partner(s, z, y, x)
        )

    def across(self, i):
        s, z, y, x = self.where
        part = self.full(i, s, slice(None), slice(None), slice(None))
        return remote(part, part, self.send.at[i, 6], self.recv.at[i, 6], device(1 - s, z, y, x))

    def stage(self, t, i):
        if not 0 <= i < len(self.chunks):
            return
        if t == 0:
            for k in (1, 2, 3):
                self.along_z(i, k).start()
            self.own(i).start()
        elif t == 1:
            self.own(i).wait()
            for k in (1, 2, 3):
                self.along_z(i, k).wait_recv()
            self.first(i).start()
        elif t == 2:
            self.first(i).wait_recv()
            for j in (0, 1):
                self.second(i, j).start()
        elif t == 3:
            for j in (0, 1):
                self.second(i, j).wait_recv()
            self.across(i).start()

    def begin(self):
        for i in range(AHEAD):
            self.stage(0, i)

    def steps(self):
        return len(self.chunks) + 2 * LAG

    def step(self, n):
        self.stage(3, n - 2 * LAG)
        self.stage(2, n - LAG)
        self.stage(1, n)
        self.stage(0, n + AHEAD)

    def sent(self):
        for i in range(len(self.chunks)):
            for k in (1, 2, 3):
                self.along_z(i, k).wait_send()
            self.first(i).wait_send()
            for j in (0, 1):
                self.second(i, j).wait_send()
            self.across(i).wait_send()


class Scatter:
    def __init__(self, terms, held, gots, outs, load, send, recv, chunks, where):
        self.terms, self.held, self.gots, self.outs, self.chunks = terms, held, gots, outs, chunks
        self.load, self.send, self.recv, self.where = load, send, recv, where

    def cut(self, refs, i, *where):
        a, r, nr, c, nc = self.chunks[i]
        return refs[a].at[(*where, slice(r, r + nr), slice(c, c + nc))]

    def out(self, i):
        a, r, nr, c, nc = self.chunks[i]
        return self.outs[a].at[r : r + nr, c : c + nc]

    def fetch(self, i):
        s = self.where[0]
        every = (slice(None),) * 3
        return pltpu.make_async_copy(
            self.cut(self.terms, i, s, *every), self.cut(self.held, i, *every), self.load.at[i]
        )

    def fetched(self, i):
        return self.load is not None and i < self.load.shape[0]

    def across(self, i):
        s, z, y, x = self.where
        every = (slice(None),) * 3
        return remote(
            self.cut(self.terms, i, 1 - s, *every),
            self.cut(self.gots[0], i, *every),
            self.send.at[i, 0],
            self.recv.at[i, 0],
            device(1 - s, z, y, x),
        )

    def first(self, i, j):
        s, z, y, x = self.where
        yy = (1 - y) * (1 - s) + j * s
        xx = j * (1 - s) + (1 - x) * s
        return remote(
            self.cut(self.held, i, slice(None), yy, xx),
            self.cut(self.gots[1], i, slice(None), j),
            self.send.at[i, 1 + j],
            self.recv.at[i, 1 + j],
            first_partner(s, z, y, x),
        )

    def second(self, i):
        s, z, y, x = self.where
        y2 = y * (1 - s) + (1 - y) * s
        x2 = (1 - x) * (1 - s) + x * s
        return remote(
            self.cut(self.held, i, slice(None), y2, x2),
            self.cut(self.gots[2], i, slice(None)),
            self.send.at[i, 3],
            self.recv.at[i, 3],
            second_partner(s, z, y, x),
        )

    def along_z(self, i, k):
        s, z, y, x = self.where
        zt = (z + k) % 4
        return remote(
            self.cut(self.held, i, zt, y, x),
            self.cut(self.gots[3], i, k - 1),
            self.send.at[i, 3 + k],
            self.recv.at[i, 3 + k],
            device(s, zt, y, x),
        )

    def add(self, to, term):
        to[...] = to[...] + term[...]

    def stage(self, t, i):
        s, z, y, x = self.where
        if t == 0:
            self.across(i).start()
            if self.fetched(i):
                self.fetch(i).start()
        elif t == 1:
            if self.fetched(i):
                self.fetch(i).wait()
            self.across(i).wait_recv()

            def add1(n, unused):
                at = (n // 4, (n // 2) % 2, n % 2)
                self.add(self.cut(self.held, i, *at), self.cut(self.gots[0], i, *at))
                return unused

            lax.fori_loop(0, 16, add1, 0)
            for j in (0, 1):
                self.first(i, j).start()
        elif t == 2:
            for j in (0, 1):
                self.first(i, j).wait_recv()

            def add2(n, unused):
                zz, j = n // 2, n % 2
                yy = y * (1 - s) + j * s
                xx = j * (1 - s) + x * s
                self.add(self.cut(self.held, i, zz, yy, xx), self.cut(self.gots[1], i, zz, j))
                return unused

            lax.fori_loop(0, 8, add2, 0)
            self.second(i).start()
        elif t == 3:
            self.second(i).wait_recv()

            def add3(zz, unused):
                self.add(self.cut(self.held, i, zz, y, x), self.cut(self.gots[2], i, zz))
                return unused

            lax.fori_loop(0, 4, add3, 0)
            for k in (1, 2, 3):
                self.along_z(i, k).start()
        elif t == 4:
            for k in (1, 2, 3):
                self.along_z(i, k).wait_recv()
            total = self.cut(self.held, i, z, y, x)[...].astype(F32)
            for k in (0, 1, 2):
                total = total + self.cut(self.gots[3], i, k)[...].astype(F32)
            self.out(i)[...] = total

    def sent(self):
        for i in range(len(self.chunks)):
            self.across(i).wait_send()
            for j in (0, 1):
                self.first(i, j).wait_send()
            self.second(i).wait_send()
            for k in (1, 2, 3):
                self.along_z(i, k).wait_send()


def got_shapes(sizes):
    return [pltpu.VMEM(lead + size, BF16) for lead in ((4, 2, 2), (4, 2), (4,), (3,)) for size in sizes]


def got_levels(refs, count):
    return [refs[level * count : (level + 1) * count] for level in range(4)]


def head_of(shape):
    return lax.broadcasted_iota(jnp.int32, shape, len(shape) - 1) // 64


def pick(values, head):
    return jnp.where(head_of(values.shape) == head, values, jnp.zeros_like(values))


def attend_pair(queries, keys, values):
    length = queries.shape[0]
    mixed, logs = [], []
    for head in (0, 1):
        scores = dot_nt(pick(queries, head), keys)
        top = jnp.max(scores, axis=1, keepdims=True)
        powers = jnp.exp(scores - top)
        total = jnp.sum(powers, axis=1, keepdims=True)
        mixed.append(dot_nn(powers.astype(BF16), values) * (1.0 / total))
        column = jnp.broadcast_to(top + jnp.log(total), (length, LANES))
        logs.append(jnp.transpose(column)[0:1])
    attended = jnp.where(head_of(mixed[0].shape) == 0, mixed[0], mixed[1]).astype(BF16)
    return attended, jnp.concatenate(logs, axis=0)


def attend_pair_back(queries, keys, values, attended, grad, logs):
    keys_t = jnp.transpose(keys)
    products = jnp.transpose(grad.astype(F32) * attended.astype(F32))
    dk = jnp.zeros(keys.shape, F32)
    dv = jnp.zeros(keys.shape, F32)
    dq_t = []
    for head in (0, 1):
        offset = jnp.sum(products[64 * head : 64 * head + 64], axis=0, keepdims=True)
        q_head = pick(queries, head)
        g_head = pick(grad, head)
        scores_t = dot_nt(keys, q_head)
        probs_t = jnp.exp(scores_t - logs[head : head + 1, :])
        slopes_t = dot_nt(values, g_head)
        score_grad_t = (probs_t * (slopes_t - offset)).astype(BF16)
        dv += dot_nn(probs_t.astype(BF16), g_head)
        dk += dot_nn(score_grad_t, q_head)
        dq_t.append(dot_nn(keys_t[64 * head : 64 * head + 64], score_grad_t))
    dq = jnp.transpose(jnp.concatenate(dq_t, axis=0)) * SCALE
    return dq.astype(BF16), dk.astype(BF16), dv.astype(BF16)


def attend_kernel(q_ref, k_ref, v_ref, o_ref, lse_ref):
    keys = k_ref[:, 0].reshape(-1, PAIR)
    values = v_ref[:, 0].reshape(-1, PAIR)
    o_ref[0], lse_ref[0, 0] = attend_pair(q_ref[0], keys, values)


def attend(queries, keys, values):
    micro, length, width = queries.shape
    parts = keys.shape[0]
    pairs = width // PAIR
    row = pl.BlockSpec((1, length, PAIR), lambda m, p: (m, 0, p))
    col = pl.BlockSpec((parts, 1, length, PAIR), lambda m, p: (0, m, 0, p))
    return pl.pallas_call(
        attend_kernel,
        grid=(micro, pairs),
        in_specs=[row, col, col],
        out_specs=[row, pl.BlockSpec((1, 1, 2, length), lambda m, p: (m, p, 0, 0))],
        out_shape=[
            jax.ShapeDtypeStruct(queries.shape, BF16),
            jax.ShapeDtypeStruct((micro, pairs, 2, length), F32),
        ],
        compiler_params=pltpu.CompilerParams(vmem_limit_bytes=VMEM_LIMIT),
        name="attend",
    )(queries, keys, values)


def attend_back_kernel(q_ref, k_ref, v_ref, o_ref, g_ref, lse_ref, dq_ref, dk_ref, dv_ref):
    parts, length = k_ref.shape[0], q_ref.shape[1]
    keys = k_ref[:, 0].reshape(-1, PAIR)
    values = v_ref[:, 0].reshape(-1, PAIR)
    dq, dk, dv = attend_pair_back(q_ref[0], keys, values, o_ref[0], g_ref[0], lse_ref[0, 0])
    dq_ref[0] = dq
    dk_ref[:, 0] = dk.reshape(parts, length, PAIR)
    dv_ref[:, 0] = dv.reshape(parts, length, PAIR)


def attend_back(queries, keys, values, attended, grad, lse):
    micro, length, width = queries.shape
    parts = keys.shape[0]
    pairs = width // PAIR
    row = pl.BlockSpec((1, length, PAIR), lambda m, p: (m, 0, p))
    col = pl.BlockSpec((parts, 1, length, PAIR), lambda m, p: (0, m, 0, p))
    log = pl.BlockSpec((1, 1, 2, length), lambda m, p: (m, p, 0, 0))
    return pl.pallas_call(
        attend_back_kernel,
        grid=(micro, pairs),
        in_specs=[row, col, col, row, row, log],
        out_specs=[row, col, col],
        out_shape=[
            jax.ShapeDtypeStruct((micro, length, width), BF16),
            jax.ShapeDtypeStruct((parts, micro, length, width), BF16),
            jax.ShapeDtypeStruct((parts, micro, length, width), BF16),
        ],
        compiler_params=pltpu.CompilerParams(vmem_limit_bytes=VMEM_LIMIT),
        name="attend_back",
    )(queries, keys, values, attended, grad, lse)


def project_kernel(own_ref, all_ref, wq_ref, wk_ref, wv_ref, small_ref, q_ref, k_ref, v_ref, bias):
    @pl.when(pl.program_id(0) == 0)
    def _():
        bias[...] = spread(small_ref[:, 0:8].astype(F32), bias.shape[1])

    @pl.when(pl.program_id(0) < own_ref.shape[0] * 2)
    def _():
        queries = dot_nn(own_ref[0], wq_ref[...]) + bias[0:1]
        q_ref[0] = (queries.astype(BF16).astype(F32) * SCALE).astype(BF16)

    rows = all_ref[0, 0]
    k_ref[0, 0] = dot_nn(rows, wk_ref[...]).astype(BF16)
    v_ref[0, 0] = (dot_nn(rows, wv_ref[...]) + bias[1:2]).astype(BF16)


def project(own, all_rows, wq, wk, wv, small):
    micro, length, width = own.shape
    parts = all_rows.shape[0]
    whole = lambda a: pl.BlockSpec(a.shape, lambda i: (0,) * a.ndim)
    last = micro - 1
    mine = pl.BlockSpec((1, length, width), lambda i: (jnp.minimum(i, last), 0, 0))
    every = pl.BlockSpec((1, 1, length, width), lambda i: (i // micro, i % micro, 0, 0))
    return pl.pallas_call(
        project_kernel,
        grid=(parts * micro,),
        in_specs=[mine, every, whole(wq), whole(wk), whole(wv), whole(small)],
        out_specs=[mine, every, every],
        out_shape=[
            jax.ShapeDtypeStruct((micro, length, width), BF16),
            jax.ShapeDtypeStruct((parts, micro, length, width), BF16),
            jax.ShapeDtypeStruct((parts, micro, length, width), BF16),
        ],
        scratch_shapes=[pltpu.VMEM((8, width), F32)],
        compiler_params=pltpu.CompilerParams(vmem_limit_bytes=VMEM_LIMIT),
        name="project",
    )(own, all_rows, wq, wk, wv, small)


SMALL, WQ, WK, WV, WO, WIN, WOUT = range(7)


def forward_chunks(shapes):
    chunks = [(SMALL, 0, shapes[SMALL][0], 0, LANES)]
    rows, width = shapes[WQ]
    for c in range(0, width, GROUP):
        chunks += [(w, 0, rows, c, GROUP) for w in (WQ, WK, WV)]
    chunks.append((WO, 0, rows, 0, width))
    chunks += [(WIN, 0, rows, c, CHUNK) for c in range(0, shapes[WIN][1], CHUNK)]
    chunks += [(WOUT, 0, shapes[WOUT][0], c, GROUP) for c in range(0, width, GROUP)]
    return chunks


def forward_kernel(chunks, *refs):
    shards, x_ref, fulls = refs[:7], refs[7], refs[8:15]
    q_out, k_out, v_out, att_ref, lse_ref = refs[15:20]
    other, pieces, weights, small, bias, q_s, k_s, v_s = refs[20:28]
    own_sem, send, recv, row_send, row_recv, load, back = refs[28:]
    where = place()
    s, z, y, x = where
    width = q_s.shape[2]
    length = q_s.shape[1]
    groups = width // GROUP
    greet(s, z, y, x)
    gather = Gather(shards, fulls, own_sem, send, recv, chunks, where)
    rows = remote(x_ref, other, row_send, row_recv, device(1 - s, z, y, x))
    gather.begin()
    rows.start()

    def fetch(g):
        copies = []
        for n, w in enumerate((WQ, WK, WV)):
            source = fulls[w].at[:, :, :, :, :, g * GROUP : (g + 1) * GROUP]
            target = pieces.at[:, :, :, :, :, n * GROUP : (n + 1) * GROUP]
            copies.append(pltpu.make_async_copy(source, target, load.at[n]))
        return copies

    def arrived(g):
        for i in range(3 * g + 1, 3 * g + 4):
            gather.across(i).wait_recv()
        for copy in fetch(g):
            copy.start()

    def written(g):
        cols = slice(g * GROUP, (g + 1) * GROUP)
        return [
            pltpu.make_async_copy(q_s.at[:, :, cols], q_out.at[:, :, cols], back.at[g, 0]),
            pltpu.make_async_copy(k_s.at[:, :, :, cols], k_out.at[:, :, :, cols], back.at[g, 1]),
            pltpu.make_async_copy(v_s.at[:, :, :, cols], v_out.at[:, :, :, cols], back.at[g, 2]),
        ]

    ready = 4 + 2 * LAG
    for n in range(ready):
        gather.step(n)
    gather.across(0).wait_recv()
    small_copy = pltpu.make_async_copy(fulls[SMALL], small, load.at[3])
    small_copy.start()
    arrived(0)
    small_copy.wait()
    vectors = small[...].reshape(32, 16, LANES)[:, 0:8]
    bias[...] = spread(vectors.astype(F32), width)
    rows.wait_recv()

    for g in range(groups):
        for copy in fetch(g):
            copy.wait()
        weights[...] = pieces[...].reshape(weights.shape)
        cols = slice(g * GROUP, (g + 1) * GROUP)

        def mine(m, unused):
            made = dot_nn(x_ref[m], weights[...])
            queries = made[:, :GROUP] + bias[0:1, cols]
            q_s[m, :, cols] = (queries.astype(BF16).astype(F32) * SCALE).astype(BF16)
            k_s[0, m, :, cols] = made[:, GROUP : 2 * GROUP].astype(BF16)
            v_s[0, m, :, cols] = (made[:, 2 * GROUP :] + bias[1:2, cols]).astype(BF16)
            return unused

        def others(m, unused):
            made = dot_nn(other[m], weights[:, GROUP:])
            k_s[1, m, :, cols] = made[:, :GROUP].astype(BF16)
            v_s[1, m, :, cols] = (made[:, GROUP:] + bias[1:2, cols]).astype(BF16)
            return unused

        lax.fori_loop(0, 2, mine, 0)
        lax.fori_loop(0, 2, others, 0)
        for copy in written(g):
            copy.start()

        def one(j, unused):
            for n in range(4):

                @pl.when(j == n)
                def _():
                    gather.step(ready + 4 * g + n)

            if g + 1 < groups:

                @pl.when(j == 3)
                def _():
                    arrived(g + 1)

            m = j // 2
            p = 2 * g + j % 2
            lanes = pl.ds(pl.multiple_of(p * PAIR, PAIR), PAIR)
            keys = k_s[:, m, :, lanes].reshape(2 * length, PAIR)
            values = v_s[:, m, :, lanes].reshape(2 * length, PAIR)
            attended, logs = attend_pair(q_s[m, :, lanes], keys, values)
            att_ref[m, :, lanes] = attended
            lse_ref[m, p] = logs
            return unused

        lax.fori_loop(0, 4, one, 0)

    for n in range(ready + 4 * groups, gather.steps()):
        gather.step(n)
    for i in range(3 * groups + 1, len(chunks)):
        gather.across(i).wait_recv()
    for g in range(groups):
        for copy in written(g):
            copy.wait()
    rows.wait_send()
    gather.sent()


def forward_box(shards, own):
    micro, length, width = own.shape
    chunks = forward_chunks([a.shape for a in shards])
    any_spec = pl.BlockSpec(memory_space=pl.ANY)
    vmem_spec = pl.BlockSpec(memory_space=pltpu.VMEM)
    count = len(chunks)
    pairs = width // PAIR
    twice = (2, micro, length, width)
    outs = pl.pallas_call(
        functools.partial(forward_kernel, chunks),
        out_shape=[jax.ShapeDtypeStruct((2, 4, 2, 2) + a.shape, a.dtype) for a in shards]
        + [
            jax.ShapeDtypeStruct(own.shape, BF16),
            jax.ShapeDtypeStruct(twice, BF16),
            jax.ShapeDtypeStruct(twice, BF16),
            jax.ShapeDtypeStruct(own.shape, BF16),
            jax.ShapeDtypeStruct((micro, pairs, 2, length), F32),
        ],
        in_specs=[vmem_spec] * 8,
        out_specs=[any_spec] * 10 + [vmem_spec] * 2,
        scratch_shapes=[
            pltpu.VMEM(own.shape, BF16),
            pltpu.VMEM((2, 4, 2, 2, width // 32, 3 * GROUP), BF16),
            pltpu.VMEM((width, 3 * GROUP), BF16),
            pltpu.VMEM((2, 4, 2, 2, 16, LANES), BF16),
            pltpu.VMEM((8, width), F32),
            pltpu.VMEM(own.shape, BF16),
            pltpu.VMEM(twice, BF16),
            pltpu.VMEM(twice, BF16),
            pltpu.SemaphoreType.DMA((count,)),
            pltpu.SemaphoreType.DMA((count, 7)),
            pltpu.SemaphoreType.DMA((count, 7)),
            pltpu.SemaphoreType.DMA,
            pltpu.SemaphoreType.DMA,
            pltpu.SemaphoreType.DMA((4,)),
            pltpu.SemaphoreType.DMA((width // GROUP, 3)),
        ],
        compiler_params=pltpu.CompilerParams(
            collective_id=1, has_side_effects=True, vmem_limit_bytes=VMEM_LIMIT
        ),
        name="forward_attention",
    )(*shards, own)
    fulls = [full.reshape((-1, full.shape[-1])) for full in outs[1:7]]
    return [outs[0].reshape(32, 16, LANES)] + fulls, outs[7:]


def mean_rows(values):
    return jnp.mean(values, axis=-1, keepdims=True)


def rows_kernel(
    x_ref,
    att_ref,
    cot_ref,
    wo_ref,
    small_ref,
    win_in,
    wout_in,
    out_ref,
    hidden_ref,
    active_ref,
    inner_grad_ref,
    feed_ref,
    branch_ref,
    mixed_ref,
    first_ref,
    smallg_ref,
    vec,
    ib,
    slope,
    vecg,
    ibg,
    win_ref,
    wout_ref,
    load,
):
    step = pl.program_id(0)
    chunks = win_ref.shape[1] // CHUNK
    win_copy = pltpu.make_async_copy(win_in, win_ref, load.at[0])
    wout_copy = pltpu.make_async_copy(wout_in, wout_ref, load.at[1])

    @pl.when(step == 0)
    def _():
        win_copy.start()
        wout_copy.start()
        vec[...] = spread(small_ref[:, 0:8].astype(F32), vec.shape[1])
        ib[...] = spread(small_ref[:, 8:16].astype(F32), ib.shape[1])
        vecg[...] = jnp.zeros_like(vecg)
        ibg[...] = jnp.zeros_like(ibg)

    o_b, g1, s1, outer_b, g2, s2 = (vec[i : i + 1] for i in range(2, 8))
    first_sum = x_ref[...].astype(F32) + (dot_nn(att_ref[...], wo_ref[...]) + o_b)
    centred = first_sum - mean_rows(first_sum)
    r1 = lax.rsqrt(mean_rows(centred * centred) + EPS)
    n1 = centred * r1
    hidden = n1 * g1 + s1
    hidden_low = hidden.astype(BF16)
    hidden_ref[...] = hidden_low

    @pl.when(step == 0)
    def _():
        win_copy.wait()
        wout_copy.wait()

    total = hidden + outer_b
    for c in range(chunks):
        cols = slice(c * CHUNK, (c + 1) * CHUNK)
        v = dot_nn(hidden_low, win_ref[:, cols]) + ib[0:1, cols]
        square = v * v
        t = jnp.tanh(v * (GELU_C + (GELU_C * GELU_A) * square))
        half = 0.5 * (1.0 + t)
        active = (v * half).astype(BF16)
        active_ref[:, cols] = active
        slope[:, cols] = half + (0.5 * v) * (1.0 - t * t) * (
            GELU_C + (3.0 * GELU_C * GELU_A) * square
        )
        total = total + dot_nn(active, wout_ref[cols, :])
    centred = total - mean_rows(total)
    r2 = lax.rsqrt(mean_rows(centred * centred) + EPS)
    n2 = centred * r2
    out_ref[...] = (n2 * g2 + s2).astype(BF16)
    e = cot_ref[...].astype(F32)
    m = e * g2
    second = (m - mean_rows(m) - n2 * mean_rows(m * n2)) * r2
    feed = second.astype(BF16)
    feed_ref[...] = feed
    vecg[6:7] += jnp.sum(e * n2, axis=0, keepdims=True)
    vecg[7:8] += jnp.sum(e, axis=0, keepdims=True)
    vecg[5:6] += jnp.sum(feed.astype(F32), axis=0, keepdims=True)
    e = second
    for c in range(chunks):
        cols = slice(c * CHUNK, (c + 1) * CHUNK)
        inner_grad = (dot_nt(feed, wout_ref[cols, :]) * slope[:, cols]).astype(BF16)
        inner_grad_ref[:, cols] = inner_grad
        ibg[0:1, cols] += jnp.sum(inner_grad.astype(F32), axis=0, keepdims=True)
        e = e + dot_nt(inner_grad, win_ref[:, cols])
    m = e * g1
    first = (m - mean_rows(m) - n1 * mean_rows(m * n1)) * r1
    first_ref[...] = first
    branch = first.astype(BF16)
    branch_ref[...] = branch
    vecg[3:4] += jnp.sum(e * n1, axis=0, keepdims=True)
    vecg[4:5] += jnp.sum(e, axis=0, keepdims=True)
    vecg[2:3] += jnp.sum(branch.astype(F32), axis=0, keepdims=True)
    mixed_ref[...] = dot_nt(branch, wo_ref[...]).astype(BF16)

    @pl.when(step == pl.num_programs(0) - 1)
    def _():
        devices = smallg_ref.shape[0]
        smallg_ref[:, 0:8] = collect(vecg[...], devices).astype(BF16)
        smallg_ref[:, 8:16] = collect(ibg[...], devices).astype(BF16)


def row_stage(x, attended, cotangent, wo, win, wout, small):
    rows, width = x.shape
    hidden_width = win.shape[1]
    block = min(ROWS, rows)
    whole = lambda a: pl.BlockSpec(
        a.shape, lambda i: (0,) * a.ndim, pipeline_mode=pl.Buffered(1)
    )
    narrow = pl.BlockSpec((block, width), lambda i: (i, 0))
    wide = pl.BlockSpec((block, hidden_width), lambda i: (i, 0))
    low = jax.ShapeDtypeStruct((rows, width), BF16)
    low_wide = jax.ShapeDtypeStruct((rows, hidden_width), BF16)
    return pl.pallas_call(
        rows_kernel,
        grid=(rows // block,),
        in_specs=[narrow] * 3
        + [whole(wo), whole(small)]
        + [pl.BlockSpec(memory_space=pl.ANY)] * 2,
        out_specs=[
            narrow,
            narrow,
            wide,
            wide,
            narrow,
            narrow,
            narrow,
            narrow,
            pl.BlockSpec(small.shape, lambda i: (0, 0, 0)),
        ],
        out_shape=[
            low,
            low,
            low_wide,
            low_wide,
            low,
            low,
            low,
            jax.ShapeDtypeStruct((rows, width), F32),
            jax.ShapeDtypeStruct(small.shape, BF16),
        ],
        scratch_shapes=[
            pltpu.VMEM((8, width), F32),
            pltpu.VMEM((8, hidden_width), F32),
            pltpu.VMEM((block, hidden_width), F32),
            pltpu.VMEM((8, width), F32),
            pltpu.VMEM((8, hidden_width), F32),
            pltpu.VMEM(win.shape, BF16),
            pltpu.VMEM(wout.shape, BF16),
            pltpu.SemaphoreType.DMA((2,)),
        ],
        compiler_params=pltpu.CompilerParams(vmem_limit_bytes=VMEM_LIMIT),
        name="row_stage",
    )(x, attended, cotangent, wo, small, win, wout)


def product_kernel(left_ref, right_ref, out_ref):
    out_ref[...] = dot_tn(left_ref[...], right_ref[...]).astype(BF16)


def product(left, right, block_m, block_n):
    depth, rows = left.shape
    cols = right.shape[1]
    return pl.pallas_call(
        product_kernel,
        grid=(rows // block_m, cols // block_n),
        in_specs=[
            pl.BlockSpec((depth, block_m), lambda i, j: (0, i)),
            pl.BlockSpec((depth, block_n), lambda i, j: (0, j)),
        ],
        out_specs=pl.BlockSpec((block_m, block_n), lambda i, j: (i, j)),
        out_shape=jax.ShapeDtypeStruct((rows, cols), BF16),
        compiler_params=pltpu.CompilerParams(vmem_limit_bytes=VMEM_LIMIT),
        name="weight_gradient",
    )(left, right)


def products_kernel(hidden, inner, active, feed_in, flat_in, branch_in, win, wo, wout, *scratch):
    feed, flat, branch, load = scratch
    step = pl.program_id(0)
    wide = pl.num_programs(0) // 2
    copies = [
        pltpu.make_async_copy(source, target, load.at[n])
        for n, (source, target) in enumerate(
            ((feed_in, feed), (flat_in, flat), (branch_in, branch))
        )
    ]

    @pl.when(step == 0)
    def _():
        for copy in copies:
            copy.start()

    @pl.when(step < wide)
    def _():
        win[...] = dot_tn(hidden[...], inner[...]).astype(BF16)

    @pl.when(step == wide - 1)
    def _():
        for copy in copies:
            copy.wait()

    @pl.when((step >= wide) & (step < 2 * wide))
    def _():
        wout[...] = dot_tn(active[...], feed[...]).astype(BF16)

    @pl.when(step == 2 * wide)
    def _():
        wo[...] = dot_tn(flat[...], branch[...]).astype(BF16)


def products(hidden, inner, active, feed, flat, branch):
    tokens, width = hidden.shape
    wide = inner.shape[1] // CHUNK
    low = lambda *shape: jax.ShapeDtypeStruct(shape, BF16)
    any_spec = pl.BlockSpec(memory_space=pl.ANY)
    return pl.pallas_call(
        products_kernel,
        grid=(2 * wide + 1,),
        in_specs=[
            pl.BlockSpec((tokens, width), lambda i: (0, 0), pipeline_mode=pl.Buffered(1)),
            pl.BlockSpec((tokens, CHUNK), lambda i: (0, jnp.clip(i, 0, wide - 1))),
            pl.BlockSpec((tokens, CHUNK), lambda i: (0, jnp.clip(i - wide, 0, wide - 1))),
            any_spec,
            any_spec,
            any_spec,
        ],
        out_specs=[
            pl.BlockSpec((width, CHUNK), lambda i: (0, jnp.clip(i, 0, wide - 1))),
            pl.BlockSpec((width, width), lambda i: (0, 0)),
            pl.BlockSpec((CHUNK, width), lambda i: (jnp.clip(i - wide, 0, wide - 1), 0)),
        ],
        out_shape=[
            low(width, inner.shape[1]),
            low(width, width),
            low(active.shape[1], width),
        ],
        scratch_shapes=[pltpu.VMEM((tokens, width), BF16)] * 3 + [pltpu.SemaphoreType.DMA((3,))],
        compiler_params=pltpu.CompilerParams(vmem_limit_bytes=VMEM_LIMIT),
        name="weight_gradients",
    )(hidden, inner, active, feed, flat, branch)


def input_kernel(first_ref, dq_ref, dk_ref, dv_ref, wq_ref, wk_ref, wv_ref, out_ref, vecg_ref, acc):
    step = pl.program_id(0)

    @pl.when(step == 0)
    def _():
        acc[...] = jnp.zeros_like(acc)

    out_ref[...] = (
        first_ref[...]
        + dot_nt(dq_ref[...], wq_ref[...])
        + dot_nt(dk_ref[...], wk_ref[...])
        + dot_nt(dv_ref[...], wv_ref[...])
    ).astype(BF16)
    acc[0:1] += jnp.sum(dq_ref[...].astype(F32), axis=0, keepdims=True)
    acc[1:2] += jnp.sum(dv_ref[...].astype(F32), axis=0, keepdims=True)

    @pl.when(step == pl.num_programs(0) - 1)
    def _():
        vecg_ref[:, 0:8] = collect(acc[...], vecg_ref.shape[0]).astype(BF16)
        vecg_ref[:, 8:16] = jnp.zeros((vecg_ref.shape[0], 8, LANES), BF16)


def input_stage(first, dq, dk, dv, wq, wk, wv, small_shape):
    rows, width = first.shape
    block = min(ROWS, rows)
    narrow = pl.BlockSpec((block, width), lambda i: (i, 0))
    whole = pl.BlockSpec((width, width), lambda i: (0, 0))
    return pl.pallas_call(
        input_kernel,
        grid=(rows // block,),
        in_specs=[narrow] * 4 + [whole] * 3,
        out_specs=[narrow, pl.BlockSpec(small_shape, lambda i: (0, 0, 0))],
        out_shape=[
            jax.ShapeDtypeStruct((rows, width), BF16),
            jax.ShapeDtypeStruct(small_shape, BF16),
        ],
        scratch_shapes=[pltpu.VMEM((8, width), F32)],
        compiler_params=pltpu.CompilerParams(vmem_limit_bytes=VMEM_LIMIT),
        name="input_stage",
    )(first, dq, dk, dv, wq, wk, wv)


PLAN_IN = ((1, 2, 6, 9, 11), (1, 4, 6, 8, 18), (1, 2, 5, 7, 19), (0, 1, 9, 11, 16),)
PLAN_OUT = ((0, 1, 5, 9, 19), (9, 10, 13, 15, 17), (2, 8, 11, 13, 19))
PLAN_O, PLAN_SMALL, PLAN_SMALL2 = (2, 5, 9, 10, 19), (5, 6, 9, 10, 19), (13, 15, 16, 18, 24)
PLAN_QKV = (
    (6, 7, 10, 12, 19),
    (10, 11, 14, 16, 23),
    (13, 14, 16, 20, 23),
    (13, 15, 20, 21, 24),
)
G_IN, G_OUT, G_O, G_SMALL, G_QKV, G_SMALL2 = 0, 1, 2, 3, 4, 8
UNITS = 12
BACK_STEPS = UNITS + 5
BACK_PLAN = (
    [(G_OUT, c * GROUP, GROUP, plan) for c, plan in enumerate(PLAN_OUT)]
    + [(G_IN, c * CHUNK, CHUNK, plan) for c, plan in enumerate(PLAN_IN)]
    + [(G_O, 0, CHUNK, PLAN_O), (G_SMALL, 0, LANES, PLAN_SMALL)]
    + [(G_QKV + g, 0, 3 * w, plan) for g, (w, plan) in enumerate(zip((256, 256, 128, 128), PLAN_QKV))]
    + [(G_SMALL2, 0, LANES, PLAN_SMALL2)]
)
FETCHED = 9


def unit_of(step):
    u = jnp.clip(step, 0, UNITS - 1)
    return u % 2, u // 2


def backward_kernel(sizes, *refs):
    terms1 = refs[:4]
    (q_ref, k_ref, v_ref, o_ref, g_ref, lse_ref, x_in, wq_in, wk_in, wv_in, first_ref) = refs[4:15]
    outs, dx_ref = refs[15:24], refs[24]
    held1 = refs[25:29]
    broad, slim, small2, sums = refs[29:33]
    gots = got_levels(refs[33:69], 9)
    dq_all, dk_all, dv_all, away, far, x_t, x_v, wq_v, wk_v, wv_v = refs[69:79]
    load, send, recv, far_send, far_recv, bring = refs[79:]
    where = place()
    s, z, y, x = where
    step = pl.program_id(0)
    length = q_ref.shape[1]
    rows = dq_all.shape[0] * length
    chunks = [(a, 0, sizes[a][0], c, nc) for a, c, nc, _ in BACK_PLAN]
    terms = list(terms1) + [a.at[g] for a in (broad, slim) for g in (0, 1)] + [small2]
    held = list(held1) + [a.at[g, s] for a in (broad, slim) for g in (0, 1)] + [small2.at[s]]
    scatter = Scatter(terms, held, gots, outs, load, send, recv, chunks, where)
    copies = [
        pltpu.make_async_copy(a, b, bring.at[n])
        for n, (a, b) in enumerate(zip((x_in, wq_in, wk_in, wv_in), (x_v, wq_v, wk_v, wv_v)))
    ]

    def far_copies(u):
        m, p = unit_of(u)
        lanes = pl.ds(pl.multiple_of(p * PAIR, PAIR), PAIR)
        target = device(1 - s, z, y, x)
        return [
            remote(
                away.at[u, n], far.at[n, m, :, lanes], far_send.at[u, n], far_recv.at[u, n], target
            )
            for n in (0, 1)
        ]

    @pl.when(step == 0)
    def _():
        for copy in copies:
            copy.start()
        greet(s, z, y, x)

    for n in range(BACK_STEPS):
        todo = [(t, i) for i, c in enumerate(BACK_PLAN) for t, at in enumerate(c[3]) if at == n]
        if todo:

            @pl.when(step == n)
            def _():
                for t, i in sorted(todo, reverse=True):
                    scatter.stage(t, i)

    @pl.when((step > 0) & (step < UNITS))
    def _():
        for copy in far_copies(step - 1):
            copy.start()

    @pl.when(step == 1)
    def _():
        copies[0].wait()
        x_t[...] = jnp.transpose(x_v[...])

    @pl.when(step < UNITS)
    def _():
        m, p = unit_of(step)
        lanes = pl.ds(pl.multiple_of(p * PAIR, PAIR), PAIR)
        keys = k_ref[:, 0].reshape(-1, PAIR)
        values = v_ref[:, 0].reshape(-1, PAIR)
        dq, dk, dv = attend_pair_back(q_ref[0], keys, values, o_ref[0], g_ref[0], lse_ref[0, 0])
        dq_all[m, :, lanes] = dq
        dk_all[m, :, lanes] = dk[:length]
        dv_all[m, :, lanes] = dv[:length]
        away[step, 0] = dk[length:]
        away[step, 1] = dv[length:]

    @pl.when(step == UNITS)
    def _():
        for copy in far_copies(UNITS - 1):
            copy.start()

    def products(to, g, unit, units, lane, lanes):
        for n in range(units):
            for copy in far_copies(unit + n):
                copy.wait_recv()
        cols = pl.ds(pl.multiple_of(lane, PAIR), lanes)
        for m in range(dq_all.shape[0]):
            for n, whole in enumerate((dk_all, dv_all)):
                whole[m, :, cols] = whole[m, :, cols] + far[n, m, :, cols]
        for n, whole in enumerate((dq_all, dk_all, dv_all)):
            value = dot_nn(x_t[...], whole[:, :, cols].reshape(rows, lanes)).astype(BF16)
            to[g, :, :, :, :, :, n * lanes : (n + 1) * lanes] = value.reshape(
                (2, 4, 2, 2) + (sizes[G_QKV][0], lanes)
            )

    @pl.when((step == 5) | (step == 9))
    def _():
        g = (step - 5) // 4
        products(broad, g, 4 * g, 4, g * GROUP, GROUP)

    @pl.when((step == 11) | (step == 12))
    def _():
        g = step - 11
        products(slim, g, 8 + 2 * g, 2, 2 * GROUP + g * PAIR, PAIR)

    @pl.when(step == UNITS)
    def _():
        sums[...] = jnp.zeros_like(sums)
        for n, whole in enumerate((dq_all, dv_all)):
            total = jnp.sum(whole[...].astype(F32).reshape(rows, -1), axis=0, keepdims=True)
            sums[n : n + 1] = total
        small2[...] = jnp.zeros_like(small2)
        small2[:, :, :, :, 0:8] = (
            collect(sums[...], 32).astype(BF16).reshape((2, 4, 2, 2, 8, LANES))
        )
        for copy in copies[1:]:
            copy.wait()

    @pl.when(step > UNITS)
    def _():
        block = first_ref.shape[0]
        r = step - UNITS - 1
        per = length // block
        at = pl.ds(pl.multiple_of((r % per) * block, block), block)
        dx_ref[...] = (
            first_ref[...]
            + dot_nt(dq_all[r // per, at], wq_v[...])
            + dot_nt(dk_all[r // per, at], wk_v[...])
            + dot_nt(dv_all[r // per, at], wv_v[...])
        ).astype(BF16)

    @pl.when(step == BACK_STEPS - 1)
    def _():
        late = [(at, -t, i) for i, c in enumerate(BACK_PLAN) for t, at in enumerate(c[3])]
        for at, t, i in sorted(late):
            if at >= BACK_STEPS:
                scatter.stage(-t, i)
        for u in range(UNITS):
            for copy in far_copies(u):
                copy.wait_send()
        scatter.sent()


def backward_box(win_grad, wout_grad, wo_grad, small, q, k, v, o, g, lse, tokens, wq, wk, wv, first):
    micro, length, width = q.shape
    rows = tokens.shape[0]
    narrow, thin = (width // 32, width), (16, LANES)
    sizes = [(width // 32, win_grad.shape[1]), (wout_grad.shape[0] // 32, width), narrow, thin]
    sizes += [(narrow[0], 3 * w) for w in (GROUP, GROUP, PAIR, PAIR)] + [thin]
    terms = [
        a.reshape((2, 4, 2, 2) + size)
        for a, size in zip((win_grad, wout_grad, wo_grad, small), sizes)
    ]
    block = rows // 4

    def at(i):
        return unit_of(i)

    row = pl.BlockSpec((1, length, PAIR), lambda i: (at(i)[0], 0, at(i)[1]))
    col = pl.BlockSpec((2, 1, length, PAIR), lambda i: (0, at(i)[0], 0, at(i)[1]))
    log = pl.BlockSpec((1, 1, 2, length), lambda i: (at(i)[0], at(i)[1], 0, 0))
    flat = pl.BlockSpec((block, width), lambda i: (jnp.clip(i - UNITS - 1, 0, 3), 0))
    any_spec = pl.BlockSpec(memory_space=pl.ANY)
    square = pltpu.VMEM((width, width), BF16)
    low = pltpu.VMEM((micro, length, width), BF16)
    outs = pl.pallas_call(
        functools.partial(backward_kernel, sizes),
        grid=(BACK_STEPS,),
        in_specs=[any_spec] * 4 + [row, col, col, row, row, log] + [any_spec] * 4 + [flat],
        out_specs=[pl.BlockSpec(size, lambda i: (0, 0)) for size in sizes] + [flat],
        out_shape=[jax.ShapeDtypeStruct(size, F32) for size in sizes]
        + [jax.ShapeDtypeStruct((rows, width), BF16)],
        scratch_shapes=[pltpu.VMEM((4, 2, 2) + size, BF16) for size in sizes[:4]]
        + [
            pltpu.VMEM((2, 2, 4, 2, 2) + sizes[G_QKV], BF16),
            pltpu.VMEM((2, 2, 4, 2, 2) + sizes[G_QKV + 2], BF16),
            pltpu.VMEM((2, 4, 2, 2) + thin, BF16),
            pltpu.VMEM((8, width), F32),
        ]
        + got_shapes(sizes)
        + [
            low,
            low,
            low,
            pltpu.VMEM((UNITS, 2, length, PAIR), BF16),
            pltpu.VMEM((2, micro, length, width), BF16),
            pltpu.VMEM((width, rows), BF16),
            pltpu.VMEM((rows, width), BF16),
            square,
            square,
            square,
            pltpu.SemaphoreType.DMA((FETCHED,)),
            pltpu.SemaphoreType.DMA((len(BACK_PLAN), 7)),
            pltpu.SemaphoreType.DMA((len(BACK_PLAN), 7)),
            pltpu.SemaphoreType.DMA((UNITS, 2)),
            pltpu.SemaphoreType.DMA((UNITS, 2)),
            pltpu.SemaphoreType.DMA((4,)),
        ],
        compiler_params=pltpu.CompilerParams(
            collective_id=2, has_side_effects=True, vmem_limit_bytes=VMEM_LIMIT
        ),
        name="backward_attention",
    )(*terms, q, k, v, o, g, lse, tokens, wq, wk, wv, first)
    return outs[:9], outs[9]


def hand_out_kernel(*refs):
    (win, wout, wo, small) = refs[:4]
    qkv, small2, outs = refs[4:8], refs[8], refs[9:]
    (wq_o, qb, wk_o, wv_o, vb, wo_o, ob, g1, s1, win_o, ib, wout_o, outb, g2, s2) = outs
    win_o[...] = win[...]
    wout_o[...] = wout[...]
    wo_o[...] = wo[...]
    first = 0
    for group in qkv:
        lanes = group.shape[1] // 3
        for n, target in enumerate((wq_o, wk_o, wv_o)):
            target[:, first : first + lanes] = group[:, n * lanes : (n + 1) * lanes]
        first += lanes
    piece = qb.shape[1]
    qb[...] = small2[0:1, :piece]
    vb[...] = small2[1:2, :piece]
    for row, target in zip(range(2, 8), (ob, g1, s1, outb, g2, s2)):
        target[...] = small[row : row + 1, :piece]
    ib[...] = small[8:9, : ib.shape[1]]


def hand_out(win, wout, wo, small, qkv, small2, piece, wide):
    vmem_spec = pl.BlockSpec(memory_space=pltpu.VMEM)
    line = jax.ShapeDtypeStruct((1, piece), F32)
    like = lambda a: jax.ShapeDtypeStruct(a.shape, F32)
    shapes = [like(wo), line, like(wo), like(wo), line, like(wo), line, line, line, like(win)]
    shapes += [jax.ShapeDtypeStruct((1, wide), F32), like(wout), line, line, line]
    outs = pl.pallas_call(
        hand_out_kernel,
        in_specs=[vmem_spec] * 9,
        out_specs=[vmem_spec] * 15,
        out_shape=shapes,
        compiler_params=pltpu.CompilerParams(vmem_limit_bytes=VMEM_LIMIT),
        name="hand_out",
    )(win, wout, wo, small, *qkv, small2)
    return [a.reshape(-1) if a.shape[0] == 1 else a for a in outs]


def body(
    inputs,
    cotangent,
    query_weight,
    query_bias,
    key_weight,
    value_weight,
    value_bias,
    output_weight,
    output_bias,
    first_gain,
    first_shift,
    inner_weight,
    inner_bias,
    outer_weight,
    outer_bias,
    second_gain,
    second_shift,
):
    micro, _, length, width = inputs.shape
    devices = lax.axis_size(("seq", "grp"))
    piece, wide = query_bias.shape[0], inner_bias.shape[0]
    boxed = lax.axis_size("seq") == 2 and lax.axis_size("grp") == 16 and piece % 8 == 0
    own = inputs[:, 0]
    tokens = own.reshape(-1, width)
    upstream = cotangent[:, 0].reshape(-1, width)
    vectors = jnp.stack(
        (
            query_bias,
            value_bias,
            output_bias,
            first_gain,
            first_shift,
            outer_bias,
            second_gain,
            second_shift,
        )
    )
    vectors = jnp.pad(vectors, ((0, 8), (0, LANES - piece)))
    small = vectors + jnp.pad(inner_bias[None], ((8, 7), (0, LANES - wide)))
    shards = (
        small,
        query_weight,
        key_weight,
        value_weight,
        output_weight,
        inner_weight,
        outer_weight,
    )
    if boxed:
        fulls, made = forward_box(shards, own)
        small, wq, wk, wv, wo, win, wout = fulls
        queries, keys, values, attended, lse = made
    else:
        fulls = [lax.all_gather(a, ("seq", "grp"), axis=0, tiled=True) for a in shards]
        small, wq, wk, wv, wo, win, wout = fulls
        small = small.reshape(devices, 16, LANES)
        all_rows = lax.all_gather(own, "seq", axis=0)
        queries, keys, values = project(own, all_rows, wq, wk, wv, small)
        attended, lse = attend(queries, keys, values)
    flat = attended.reshape(-1, width)
    (
        layer_out,
        hidden_low,
        active,
        inner_grad,
        feed_grad,
        branch_grad,
        mixed_grad,
        first_grad,
        small_grad,
    ) = row_stage(tokens, flat, upstream, wo, win, wout, small)
    mixed_grad = mixed_grad.reshape(micro, length, width)
    win_grad, wo_grad, wout_grad = products(
        hidden_low, inner_grad, active, feed_grad, flat, branch_grad
    )
    if boxed:
        summed, input_grad = backward_box(
            win_grad,
            wout_grad,
            wo_grad,
            small_grad,
            queries,
            keys,
            values,
            attended,
            mixed_grad,
            lse,
            tokens,
            wq,
            wk,
            wv,
            first_grad,
        )
    else:
        dq, dk, dv = attend_back(queries, keys, values, attended, mixed_grad, lse)
        dk = lax.psum_scatter(dk, "seq", scatter_dimension=0)
        dv = lax.psum_scatter(dv, "seq", scatter_dimension=0)
        dq, dk, dv = (a.reshape(-1, width) for a in (dq, dk, dv))
        input_grad, small2_grad = input_stage(
            first_grad, dq, dk, dv, wq, wk, wv, (devices, 16, LANES)
        )
        groups = [
            jnp.concatenate([a[:, c : c + w] for a in (dq, dk, dv)], axis=1)
            for c, w in ((0, GROUP), (GROUP, GROUP), (2 * GROUP, PAIR), (2 * GROUP + PAIR, PAIR))
        ]
        terms = [win_grad, wout_grad, wo_grad, small_grad.reshape(-1, LANES)]
        terms += [product(tokens, a, 768, a.shape[1]) for a in groups]
        terms.append(small2_grad.reshape(-1, LANES))
        summed = [
            lax.psum_scatter(a.astype(F32), ("seq", "grp"), scatter_dimension=0, tiled=True)
            for a in terms
        ]
        summed = lax.optimization_barrier(summed)
    grads = hand_out(*summed[:4], summed[4:8], summed[8], piece, wide)
    return (layer_out.reshape(inputs.shape), input_grad.reshape(inputs.shape)) + tuple(grads)


def solution(mesh):
    rows = P(("seq", "grp"), None)
    line = P(("seq", "grp"))
    tokens = P(None, "grp", "seq", None)
    return jax.shard_map(
        body,
        mesh=mesh,
        in_specs=(
            tokens,
            tokens,
            rows,
            line,
            rows,
            rows,
            line,
            rows,
            line,
            line,
            line,
            rows,
            line,
            rows,
            line,
            line,
            line,
        ),
        out_specs=(
            tokens,
            tokens,
            rows,
            line,
            rows,
            rows,
            line,
            rows,
            line,
            line,
            line,
            rows,
            line,
            rows,
            line,
            line,
            line,
        ),
        check_vma=False,
    )
```

```python
import functools

import jax
import jax.numpy as jnp
from jax import lax
from jax.experimental import pallas as pl
from jax.experimental.pallas import tpu as pltpu
from jax.sharding import PartitionSpec as P

HEADS = 12
SCALE = 0.125
EPS = 1e-05
PAIR = 128
ROWS = 256
CHUNK = 768
LANES = 128
GROUP = 256
LAG = 3
AHEAD = 4
VMEM_LIMIT = 64 * 1024 * 1024 - 65536
GELU_C = 0.7978845608028654
GELU_A = 0.044715
MESH = pl.DeviceIdType.MESH
F32 = jnp.float32
BF16 = jnp.bfloat16


def dot_nn(left, right):
    return lax.dot_general(left, right, (((1,), (0,)), ((), ())), preferred_element_type=F32)


def dot_nt(left, right):
    return lax.dot_general(left, right, (((1,), (1,)), ((), ())), preferred_element_type=F32)


def dot_tn(left, right):
    return lax.dot_general(left, right, (((0,), (0,)), ((), ())), preferred_element_type=F32)


def place():
    s = lax.axis_index("seq")
    g = lax.axis_index("grp")
    return s, g // 4, (g // 2) % 2, g % 2


def device(s, z, y, x):
    return (s, z * 4 + y * 2 + x)


def first_partner(s, z, y, x):
    return device(s, z, y * s + (1 - y) * (1 - s), x * (1 - s) + (1 - x) * s)


def second_partner(s, z, y, x):
    return device(s, z, y * (1 - s) + (1 - y) * s, x * s + (1 - x) * (1 - s))


def greet(s, z, y, x):
    barrier = pltpu.get_barrier_semaphore()
    partners = [device(1 - s, z, y, x), first_partner(s, z, y, x), second_partner(s, z, y, x)]
    partners += [device(s, (z + k) % 4, y, x) for k in (1, 2, 3)]
    for partner in partners:
        pl.semaphore_signal(barrier, inc=1, device_id=partner, device_id_type=MESH)
    pl.semaphore_wait(barrier, len(partners))


def remote(src, dst, send, recv, target):
    return pltpu.make_async_remote_copy(
        src_ref=src, dst_ref=dst, send_sem=send, recv_sem=recv, device_id=target, device_id_type=MESH
    )


def selector(lanes, width, piece):
    lane = lax.broadcasted_iota(jnp.int32, (lanes, width), 0)
    col = lax.broadcasted_iota(jnp.int32, (lanes, width), 1)
    return (lax.rem(col, piece) == lane).astype(BF16)


def owned(devices, rows, width, piece):
    dev = lax.broadcasted_iota(jnp.int32, (devices, rows, width), 0)
    col = lax.broadcasted_iota(jnp.int32, (devices, rows, width), 2)
    return col // piece == dev


def spread(pieces, width):
    devices, rows, lanes = pieces.shape
    piece = width // devices
    flat = pieces.reshape(devices * rows, lanes).astype(BF16)
    tiled = dot_nn(flat, selector(lanes, width, piece)).reshape(devices, rows, width)
    return jnp.sum(jnp.where(owned(devices, rows, width, piece), tiled, 0.0), axis=0)


def collect(values, devices):
    rows, width = values.shape
    piece = width // devices
    mine = jnp.where(owned(devices, rows, width, piece), values[None], 0.0)
    flat = mine.reshape(devices * rows, width).astype(BF16)
    return dot_nt(flat, selector(LANES, width, piece)).reshape(devices, rows, LANES)


class Gather:
    def __init__(self, shards, fulls, own_sem, send, recv, chunks, where):
        self.shards, self.fulls, self.chunks, self.where = shards, fulls, chunks, where
        self.own_sem, self.send, self.recv = own_sem, send, recv

    def piece(self, i):
        a, r, nr, c, nc = self.chunks[i]
        return self.shards[a].at[r : r + nr, c : c + nc]

    def full(self, i, *where):
        a, r, nr, c, nc = self.chunks[i]
        return self.fulls[a].at[(*where, slice(r, r + nr), slice(c, c + nc))]

    def own(self, i):
        return pltpu.make_async_copy(self.piece(i), self.full(i, *self.where), self.own_sem.at[i])

    def along_z(self, i, k):
        s, z, y, x = self.where
        return remote(
            self.piece(i),
            self.full(i, s, z, y, x),
            self.send.at[i, k - 1],
            self.recv.at[i, k - 1],
            device(s, (z + k) % 4, y, x),
        )

    def first(self, i):
        s, z, y, x = self.where
        part = self.full(i, s, slice(None), y, x)
        return remote(
            part, part, self.send.at[i, 3], self.recv.at[i, 3], second_partner(s, z, y, x)
        )

    def second(self, i, j):
        s, z, y, x = self.where
        yy = y * (1 - s) + j * s
        xx = j * (1 - s) + x * s
        part = self.full(i, s, slice(None), yy, xx)
        return remote(
            part, part, self.send.at[i, 4 + j], self.recv.at[i, 4 + j], first_partner(s, z, y, x)
        )

    def across(self, i):
        s, z, y, x = self.where
        part = self.full(i, s, slice(None), slice(None), slice(None))
        return remote(part, part, self.send.at[i, 6], self.recv.at[i, 6], device(1 - s, z, y, x))

    def stage(self, t, i):
        if not 0 <= i < len(self.chunks):
            return
        if t == 0:
            for k in (1, 2, 3):
                self.along_z(i, k).start()
            self.own(i).start()
        elif t == 1:
            self.own(i).wait()
            for k in (1, 2, 3):
                self.along_z(i, k).wait_recv()
            self.first(i).start()
        elif t == 2:
            self.first(i).wait_recv()
            for j in (0, 1):
                self.second(i, j).start()
        elif t == 3:
            for j in (0, 1):
                self.second(i, j).wait_recv()
            self.across(i).start()

    def begin(self):
        for i in range(AHEAD):
            self.stage(0, i)

    def steps(self):
        return len(self.chunks) + 2 * LAG

    def step(self, n):
        self.stage(3, n - 2 * LAG)
        self.stage(2, n - LAG)
        self.stage(1, n)
        self.stage(0, n + AHEAD)

    def sent(self):
        for i in range(len(self.chunks)):
            for k in (1, 2, 3):
                self.along_z(i, k).wait_send()
            self.first(i).wait_send()
            for j in (0, 1):
                self.second(i, j).wait_send()
            self.across(i).wait_send()


class Scatter:
    def __init__(self, terms, held, gots, outs, load, send, recv, chunks, where):
        self.terms, self.held, self.gots, self.outs, self.chunks = terms, held, gots, outs, chunks
        self.load, self.send, self.recv, self.where = load, send, recv, where

    def cut(self, refs, i, *where):
        a, r, nr, c, nc = self.chunks[i]
        return refs[a].at[(*where, slice(r, r + nr), slice(c, c + nc))]

    def out(self, i):
        a, r, nr, c, nc = self.chunks[i]
        return self.outs[a].at[r : r + nr, c : c + nc]

    def fetch(self, i):
        s = self.where[0]
        every = (slice(None),) * 3
        return pltpu.make_async_copy(
            self.terms[i](s, *every), self.cut(self.held, i, *every), self.load.at[i]
        )

    def fetched(self, i):
        return self.load is not None and i < self.load.shape[0]

    def across(self, i):
        s, z, y, x = self.where
        every = (slice(None),) * 3
        return remote(
            self.terms[i](1 - s, *every),
            self.cut(self.gots[0], i, *every),
            self.send.at[i, 0],
            self.recv.at[i, 0],
            device(1 - s, z, y, x),
        )

    def first(self, i, j):
        s, z, y, x = self.where
        yy = (1 - y) * (1 - s) + j * s
        xx = j * (1 - s) + (1 - x) * s
        return remote(
            self.cut(self.held, i, slice(None), yy, xx),
            self.cut(self.gots[1], i, slice(None), j),
            self.send.at[i, 1 + j],
            self.recv.at[i, 1 + j],
            first_partner(s, z, y, x),
        )

    def second(self, i):
        s, z, y, x = self.where
        y2 = y * (1 - s) + (1 - y) * s
        x2 = (1 - x) * (1 - s) + x * s
        return remote(
            self.cut(self.held, i, slice(None), y2, x2),
            self.cut(self.gots[2], i, slice(None)),
            self.send.at[i, 3],
            self.recv.at[i, 3],
            second_partner(s, z, y, x),
        )

    def along_z(self, i, k):
        s, z, y, x = self.where
        zt = (z + k) % 4
        return remote(
            self.cut(self.held, i, zt, y, x),
            self.cut(self.gots[3], i, k - 1),
            self.send.at[i, 3 + k],
            self.recv.at[i, 3 + k],
            device(s, zt, y, x),
        )

    def add(self, to, term):
        to[...] = to[...] + term[...]

    def stage(self, t, i):
        s, z, y, x = self.where
        if t == 0:
            self.across(i).start()
            if self.fetched(i):
                self.fetch(i).start()
        elif t == 1:
            if self.fetched(i) and i >= STAGED:
                self.fetch(i).wait()
            self.across(i).wait_recv()

            every = (slice(None),) * 3
            self.add(self.cut(self.held, i, *every), self.cut(self.gots[0], i, *every))
            for j in (0, 1):
                self.first(i, j).start()
        elif t == 2:
            for j in (0, 1):
                self.first(i, j).wait_recv()

            def add2(n, unused):
                zz, j = n // 2, n % 2
                yy = y * (1 - s) + j * s
                xx = j * (1 - s) + x * s
                self.add(self.cut(self.held, i, zz, yy, xx), self.cut(self.gots[1], i, zz, j))
                return unused

            lax.fori_loop(0, 8, add2, 0, unroll=True)
            self.second(i).start()
        elif t == 3:
            self.second(i).wait_recv()

            def add3(zz, unused):
                self.add(self.cut(self.held, i, zz, y, x), self.cut(self.gots[2], i, zz))
                return unused

            lax.fori_loop(0, 4, add3, 0, unroll=True)
            for k in (1, 2, 3):
                self.along_z(i, k).start()
        elif t == 4:
            for k in (1, 2, 3):
                self.along_z(i, k).wait_recv()
            total = self.cut(self.held, i, z, y, x)[...].astype(F32)
            for k in (0, 1, 2):
                total = total + self.cut(self.gots[3], i, k)[...].astype(F32)
            self.out(i)[...] = total

    def release(self, i):
        self.fetch(i).wait()
        self.across(i).wait_send()

    def sent(self):
        for i in range(len(self.chunks)):
            if i >= STAGED:
                self.across(i).wait_send()
            for j in (0, 1):
                self.first(i, j).wait_send()
            self.second(i).wait_send()
            for k in (1, 2, 3):
                self.along_z(i, k).wait_send()


def got_shapes(sizes):
    return [pltpu.VMEM(lead + size, BF16) for lead in ((4, 2, 2), (4, 2), (4,), (3,)) for size in sizes]


def got_levels(refs, count):
    return [refs[level * count : (level + 1) * count] for level in range(4)]


def head_of(shape):
    return lax.broadcasted_iota(jnp.int32, shape, len(shape) - 1) // 64


def pick(values, head):
    return jnp.where(head_of(values.shape) == head, values, jnp.zeros_like(values))


def attend_pair(queries, keys, values):
    length = queries.shape[0]
    mixed, logs = [], []
    both = [dot_nt(pick(queries, head), keys) for head in (0, 1)]
    for head, scores in enumerate(both):
        top = jnp.max(scores, axis=1, keepdims=True)
        powers = jnp.exp(scores - top)
        total = jnp.sum(powers, axis=1, keepdims=True)
        mixed.append(dot_nn(powers.astype(BF16), values) * (1.0 / total))
        column = jnp.broadcast_to(top + jnp.log(total), (length, LANES))
        logs.append(jnp.transpose(column)[0:1])
    attended = jnp.where(head_of(mixed[0].shape) == 0, mixed[0], mixed[1]).astype(BF16)
    return attended, jnp.concatenate(logs, axis=0)


def attend_pair_back(queries, keys, values, attended, grad, logs):
    keys_t = jnp.transpose(keys)
    products = jnp.transpose(grad.astype(F32) * attended.astype(F32))
    dk = jnp.zeros(keys.shape, F32)
    dv = jnp.zeros(keys.shape, F32)
    dq_t = []
    both = []
    for head in (0, 1):
        q_head = pick(queries, head)
        g_head = pick(grad, head)
        both.append((q_head, g_head, dot_nt(keys, q_head), dot_nt(values, g_head)))
    for head, (q_head, g_head, scores_t, slopes_t) in enumerate(both):
        offset = jnp.sum(products[64 * head : 64 * head + 64], axis=0, keepdims=True)
        probs_t = jnp.exp(scores_t - logs[head : head + 1, :])
        score_grad_t = (probs_t * (slopes_t - offset)).astype(BF16)
        dv += dot_nn(probs_t.astype(BF16), g_head)
        dk += dot_nn(score_grad_t, q_head)
        dq_t.append(dot_nn(keys_t[64 * head : 64 * head + 64], score_grad_t))
    dq = jnp.transpose(jnp.concatenate(dq_t, axis=0)) * SCALE
    return dq.astype(BF16), dk.astype(BF16), dv.astype(BF16)


def attend_kernel(q_ref, k_ref, v_ref, o_ref, lse_ref):
    keys = k_ref[:, 0].reshape(-1, PAIR)
    values = v_ref[:, 0].reshape(-1, PAIR)
    o_ref[0], lse_ref[0, 0] = attend_pair(q_ref[0], keys, values)


def attend(queries, keys, values):
    micro, length, width = queries.shape
    parts = keys.shape[0]
    pairs = width // PAIR
    row = pl.BlockSpec((1, length, PAIR), lambda m, p: (m, 0, p))
    col = pl.BlockSpec((parts, 1, length, PAIR), lambda m, p: (0, m, 0, p))
    return pl.pallas_call(
        attend_kernel,
        grid=(micro, pairs),
        in_specs=[row, col, col],
        out_specs=[row, pl.BlockSpec((1, 1, 2, length), lambda m, p: (m, p, 0, 0))],
        out_shape=[
            jax.ShapeDtypeStruct(queries.shape, BF16),
            jax.ShapeDtypeStruct((micro, pairs, 2, length), F32),
        ],
        compiler_params=pltpu.CompilerParams(vmem_limit_bytes=VMEM_LIMIT),
        name="attend",
    )(queries, keys, values)


def attend_back_kernel(q_ref, k_ref, v_ref, o_ref, g_ref, lse_ref, dq_ref, dk_ref, dv_ref):
    parts, length = k_ref.shape[0], q_ref.shape[1]
    keys = k_ref[:, 0].reshape(-1, PAIR)
    values = v_ref[:, 0].reshape(-1, PAIR)
    dq, dk, dv = attend_pair_back(q_ref[0], keys, values, o_ref[0], g_ref[0], lse_ref[0, 0])
    dq_ref[0] = dq
    dk_ref[:, 0] = dk.reshape(parts, length, PAIR)
    dv_ref[:, 0] = dv.reshape(parts, length, PAIR)


def attend_back(queries, keys, values, attended, grad, lse):
    micro, length, width = queries.shape
    parts = keys.shape[0]
    pairs = width // PAIR
    row = pl.BlockSpec((1, length, PAIR), lambda m, p: (m, 0, p))
    col = pl.BlockSpec((parts, 1, length, PAIR), lambda m, p: (0, m, 0, p))
    log = pl.BlockSpec((1, 1, 2, length), lambda m, p: (m, p, 0, 0))
    return pl.pallas_call(
        attend_back_kernel,
        grid=(micro, pairs),
        in_specs=[row, col, col, row, row, log],
        out_specs=[row, col, col],
        out_shape=[
            jax.ShapeDtypeStruct((micro, length, width), BF16),
            jax.ShapeDtypeStruct((parts, micro, length, width), BF16),
            jax.ShapeDtypeStruct((parts, micro, length, width), BF16),
        ],
        compiler_params=pltpu.CompilerParams(vmem_limit_bytes=VMEM_LIMIT),
        name="attend_back",
    )(queries, keys, values, attended, grad, lse)


def project_kernel(own_ref, all_ref, wq_ref, wk_ref, wv_ref, small_ref, q_ref, k_ref, v_ref, bias):
    @pl.when(pl.program_id(0) == 0)
    def _():
        bias[...] = spread(small_ref[:, 0:8].astype(F32), bias.shape[1])

    @pl.when(pl.program_id(0) < own_ref.shape[0] * 2)
    def _():
        queries = dot_nn(own_ref[0], wq_ref[...]) + bias[0:1]
        q_ref[0] = (queries.astype(BF16).astype(F32) * SCALE).astype(BF16)

    rows = all_ref[0, 0]
    k_ref[0, 0] = dot_nn(rows, wk_ref[...]).astype(BF16)
    v_ref[0, 0] = (dot_nn(rows, wv_ref[...]) + bias[1:2]).astype(BF16)


def project(own, all_rows, wq, wk, wv, small):
    micro, length, width = own.shape
    parts = all_rows.shape[0]
    whole = lambda a: pl.BlockSpec(a.shape, lambda i: (0,) * a.ndim)
    last = micro - 1
    mine = pl.BlockSpec((1, length, width), lambda i: (jnp.minimum(i, last), 0, 0))
    every = pl.BlockSpec((1, 1, length, width), lambda i: (i // micro, i % micro, 0, 0))
    return pl.pallas_call(
        project_kernel,
        grid=(parts * micro,),
        in_specs=[mine, every, whole(wq), whole(wk), whole(wv), whole(small)],
        out_specs=[mine, every, every],
        out_shape=[
            jax.ShapeDtypeStruct((micro, length, width), BF16),
            jax.ShapeDtypeStruct((parts, micro, length, width), BF16),
            jax.ShapeDtypeStruct((parts, micro, length, width), BF16),
        ],
        scratch_shapes=[pltpu.VMEM((8, width), F32)],
        compiler_params=pltpu.CompilerParams(vmem_limit_bytes=VMEM_LIMIT),
        name="project",
    )(own, all_rows, wq, wk, wv, small)


SMALL, WQ, WK, WV, WO, WIN, WOUT = range(7)


def forward_chunks(shapes):
    chunks = [(SMALL, 0, shapes[SMALL][0], 0, LANES)]
    rows, width = shapes[WQ]
    for c in range(0, width, GROUP):
        chunks += [(w, 0, rows, c, GROUP) for w in (WQ, WK, WV)]
    chunks.append((WO, 0, rows, 0, width))
    chunks += [(WIN, 0, rows, c, CHUNK) for c in range(0, shapes[WIN][1], CHUNK)]
    chunks += [(WOUT, 0, shapes[WOUT][0], c, GROUP) for c in range(0, width, GROUP)]
    return chunks


def forward_kernel(chunks, *refs):
    shards, x_ref, fulls = refs[:7], refs[7], refs[8:15]
    q_out, k_out, v_out, att_ref, lse_ref = refs[15:20]
    other, pieces, weights, small, bias, q_s, k_s, v_s = refs[20:28]
    own_sem, send, recv, row_send, row_recv, load, back = refs[28:]
    where = place()
    s, z, y, x = where
    width = q_s.shape[2]
    length = q_s.shape[1]
    groups = width // GROUP
    greet(s, z, y, x)
    gather = Gather(shards, fulls, own_sem, send, recv, chunks, where)
    rows = remote(x_ref, other, row_send, row_recv, device(1 - s, z, y, x))
    gather.begin()
    rows.start()

    def fetch(g):
        copies = []
        for n, w in enumerate((WQ, WK, WV)):
            source = fulls[w].at[:, :, :, :, :, g * GROUP : (g + 1) * GROUP]
            target = pieces.at[:, :, :, :, :, n * GROUP : (n + 1) * GROUP]
            copies.append(pltpu.make_async_copy(source, target, load.at[n]))
        return copies

    def arrived(g):
        for i in range(3 * g + 1, 3 * g + 4):
            gather.across(i).wait_recv()
        for copy in fetch(g):
            copy.start()

    def written(g):
        cols = slice(g * GROUP, (g + 1) * GROUP)
        return [
            pltpu.make_async_copy(q_s.at[:, :, cols], q_out.at[:, :, cols], back.at[g, 0]),
            pltpu.make_async_copy(k_s.at[:, :, :, cols], k_out.at[:, :, :, cols], back.at[g, 1]),
            pltpu.make_async_copy(v_s.at[:, :, :, cols], v_out.at[:, :, :, cols], back.at[g, 2]),
        ]

    ready = 4 + 2 * LAG
    for n in range(ready):
        gather.step(n)
    gather.across(0).wait_recv()
    small_copy = pltpu.make_async_copy(fulls[SMALL], small, load.at[3])
    small_copy.start()
    arrived(0)
    small_copy.wait()
    vectors = small[...].reshape(32, 16, LANES)[:, 0:8]
    bias[...] = spread(vectors.astype(F32), width)
    rows.wait_recv()

    for g in range(groups):
        for copy in fetch(g):
            copy.wait()
        weights[...] = pieces[...].reshape(weights.shape)
        cols = slice(g * GROUP, (g + 1) * GROUP)

        def mine(m, unused):
            made = dot_nn(x_ref[m], weights[...])
            queries = made[:, :GROUP] + bias[0:1, cols]
            q_s[m, :, cols] = (queries.astype(BF16).astype(F32) * SCALE).astype(BF16)
            k_s[0, m, :, cols] = made[:, GROUP : 2 * GROUP].astype(BF16)
            v_s[0, m, :, cols] = (made[:, 2 * GROUP :] + bias[1:2, cols]).astype(BF16)
            return unused

        def others(m, unused):
            made = dot_nn(other[m], weights[:, GROUP:])
            k_s[1, m, :, cols] = made[:, :GROUP].astype(BF16)
            v_s[1, m, :, cols] = (made[:, GROUP:] + bias[1:2, cols]).astype(BF16)
            return unused

        lax.fori_loop(0, 2, mine, 0)
        lax.fori_loop(0, 2, others, 0)
        for copy in written(g):
            copy.start()

        def one(j, unused):
            for n in range(4):

                @pl.when(j == n)
                def _():
                    gather.step(ready + 4 * g + n)

            if g + 1 < groups:

                @pl.when(j == 3)
                def _():
                    arrived(g + 1)

            m = j // 2
            p = 2 * g + j % 2
            lanes = pl.ds(pl.multiple_of(p * PAIR, PAIR), PAIR)
            keys = k_s[:, m, :, lanes].reshape(2 * length, PAIR)
            values = v_s[:, m, :, lanes].reshape(2 * length, PAIR)
            attended, logs = attend_pair(q_s[m, :, lanes], keys, values)
            att_ref[m, :, lanes] = attended
            lse_ref[m, p] = logs
            return unused

        lax.fori_loop(0, 4, one, 0)

    for n in range(ready + 4 * groups, gather.steps()):
        gather.step(n)
    for i in range(3 * groups + 1, len(chunks)):
        gather.across(i).wait_recv()
    for g in range(groups):
        for copy in written(g):
            copy.wait()
    rows.wait_send()
    gather.sent()


def forward_box(shards, own):
    micro, length, width = own.shape
    chunks = forward_chunks([a.shape for a in shards])
    any_spec = pl.BlockSpec(memory_space=pl.ANY)
    vmem_spec = pl.BlockSpec(memory_space=pltpu.VMEM)
    count = len(chunks)
    pairs = width // PAIR
    twice = (2, micro, length, width)
    outs = pl.pallas_call(
        functools.partial(forward_kernel, chunks),
        out_shape=[jax.ShapeDtypeStruct((2, 4, 2, 2) + a.shape, a.dtype) for a in shards]
        + [
            jax.ShapeDtypeStruct(own.shape, BF16),
            jax.ShapeDtypeStruct(twice, BF16),
            jax.ShapeDtypeStruct(twice, BF16),
            jax.ShapeDtypeStruct(own.shape, BF16),
            jax.ShapeDtypeStruct((micro, pairs, 2, length), F32),
        ],
        in_specs=[vmem_spec] * 8,
        out_specs=[any_spec] * 10 + [vmem_spec] * 2,
        scratch_shapes=[
            pltpu.VMEM(own.shape, BF16),
            pltpu.VMEM((2, 4, 2, 2, width // 32, 3 * GROUP), BF16),
            pltpu.VMEM((width, 3 * GROUP), BF16),
            pltpu.VMEM((2, 4, 2, 2, 16, LANES), BF16),
            pltpu.VMEM((8, width), F32),
            pltpu.VMEM(own.shape, BF16),
            pltpu.VMEM(twice, BF16),
            pltpu.VMEM(twice, BF16),
            pltpu.SemaphoreType.DMA((count,)),
            pltpu.SemaphoreType.DMA((count, 7)),
            pltpu.SemaphoreType.DMA((count, 7)),
            pltpu.SemaphoreType.DMA,
            pltpu.SemaphoreType.DMA,
            pltpu.SemaphoreType.DMA((4,)),
            pltpu.SemaphoreType.DMA((width // GROUP, 3)),
        ],
        compiler_params=pltpu.CompilerParams(
            collective_id=1, has_side_effects=True, vmem_limit_bytes=VMEM_LIMIT
        ),
        name="forward_attention",
    )(*shards, own)
    fulls = [full.reshape((-1, full.shape[-1])) for full in outs[1:7]]
    return [outs[0].reshape(32, 16, LANES)] + fulls, outs[7:]


def mean_rows(values):
    return jnp.mean(values, axis=-1, keepdims=True)


def rows_kernel(
    x_ref,
    att_ref,
    cot_ref,
    wo_ref,
    small_ref,
    win_in,
    wout_in,
    out_ref,
    hidden_ref,
    active_ref,
    inner_grad_ref,
    feed_ref,
    branch_ref,
    mixed_ref,
    first_ref,
    smallg_ref,
    vec,
    ib,
    slope,
    vecg,
    ibg,
    win_ref,
    wout_ref,
    load,
):
    step = pl.program_id(0)
    chunks = win_ref.shape[1] // CHUNK
    win_copy = pltpu.make_async_copy(win_in, win_ref, load.at[0])
    wout_copy = pltpu.make_async_copy(wout_in, wout_ref, load.at[1])

    @pl.when(step == 0)
    def _():
        win_copy.start()
        wout_copy.start()
        vec[...] = spread(small_ref[:, 0:8].astype(F32), vec.shape[1])
        ib[...] = spread(small_ref[:, 8:16].astype(F32), ib.shape[1])
        vecg[...] = jnp.zeros_like(vecg)
        ibg[...] = jnp.zeros_like(ibg)

    o_b, g1, s1, outer_b, g2, s2 = (vec[i : i + 1] for i in range(2, 8))
    first_sum = x_ref[...].astype(F32) + (dot_nn(att_ref[...], wo_ref[...]) + o_b)
    centred = first_sum - mean_rows(first_sum)
    r1 = lax.rsqrt(mean_rows(centred * centred) + EPS)
    n1 = centred * r1
    hidden = n1 * g1 + s1
    hidden_low = hidden.astype(BF16)
    hidden_ref[...] = hidden_low

    @pl.when(step == 0)
    def _():
        win_copy.wait()
        wout_copy.wait()

    total = hidden + outer_b
    ahead = dot_nn(hidden_low, win_ref[:, :CHUNK])
    for c in range(chunks):
        cols = slice(c * CHUNK, (c + 1) * CHUNK)
        v = ahead + ib[0:1, cols]
        if c + 1 < chunks:
            ahead = dot_nn(hidden_low, win_ref[:, (c + 1) * CHUNK : (c + 2) * CHUNK])
        square = v * v
        t = jnp.tanh(v * (GELU_C + (GELU_C * GELU_A) * square))
        half = 0.5 * (1.0 + t)
        gated = v * half
        active = gated.astype(BF16)
        active_ref[:, cols] = active
        slope[:, cols] = half + gated * (1.0 - half) * (
            (2.0 * GELU_C) + (6.0 * GELU_C * GELU_A) * square
        )
        total = total + dot_nn(active, wout_ref[cols, :])
    centred = total - mean_rows(total)
    r2 = lax.rsqrt(mean_rows(centred * centred) + EPS)
    n2 = centred * r2
    out_ref[...] = (n2 * g2 + s2).astype(BF16)
    e = cot_ref[...].astype(F32)
    m = e * g2
    second = (m - mean_rows(m) - n2 * mean_rows(m * n2)) * r2
    feed = second.astype(BF16)
    feed_ref[...] = feed
    vecg[6:7] += jnp.sum(e * n2, axis=0, keepdims=True)
    vecg[7:8] += jnp.sum(e, axis=0, keepdims=True)
    vecg[5:6] += jnp.sum(feed.astype(F32), axis=0, keepdims=True)
    e = second
    ahead = dot_nt(feed, wout_ref[:CHUNK, :])
    for c in range(chunks):
        cols = slice(c * CHUNK, (c + 1) * CHUNK)
        inner_grad = (ahead * slope[:, cols]).astype(BF16)
        if c + 1 < chunks:
            ahead = dot_nt(feed, wout_ref[(c + 1) * CHUNK : (c + 2) * CHUNK, :])
        inner_grad_ref[:, cols] = inner_grad
        ibg[0:1, cols] += jnp.sum(inner_grad.astype(F32), axis=0, keepdims=True)
        e = e + dot_nt(inner_grad, win_ref[:, cols])
    m = e * g1
    first = (m - mean_rows(m) - n1 * mean_rows(m * n1)) * r1
    first_ref[...] = first
    branch = first.astype(BF16)
    branch_ref[...] = branch
    vecg[3:4] += jnp.sum(e * n1, axis=0, keepdims=True)
    vecg[4:5] += jnp.sum(e, axis=0, keepdims=True)
    vecg[2:3] += jnp.sum(branch.astype(F32), axis=0, keepdims=True)
    mixed_ref[...] = dot_nt(branch, wo_ref[...]).astype(BF16)

    @pl.when(step == pl.num_programs(0) - 1)
    def _():
        devices = smallg_ref.shape[0]
        smallg_ref[:, 0:8] = collect(vecg[...], devices).astype(BF16)
        smallg_ref[:, 8:16] = collect(ibg[...], devices).astype(BF16)


def row_stage(x, attended, cotangent, wo, win, wout, small):
    rows, width = x.shape
    hidden_width = win.shape[1]
    block = min(ROWS, rows)
    whole = lambda a: pl.BlockSpec(
        a.shape, lambda i: (0,) * a.ndim, pipeline_mode=pl.Buffered(1)
    )
    narrow = pl.BlockSpec((block, width), lambda i: (i, 0))
    wide = pl.BlockSpec((block, hidden_width), lambda i: (i, 0))
    low = jax.ShapeDtypeStruct((rows, width), BF16)
    low_wide = jax.ShapeDtypeStruct((rows, hidden_width), BF16)
    return pl.pallas_call(
        rows_kernel,
        grid=(rows // block,),
        in_specs=[narrow] * 3
        + [whole(wo), whole(small)]
        + [pl.BlockSpec(memory_space=pl.ANY)] * 2,
        out_specs=[
            narrow,
            narrow,
            wide,
            wide,
            narrow,
            narrow,
            narrow,
            narrow,
            pl.BlockSpec(small.shape, lambda i: (0, 0, 0)),
        ],
        out_shape=[
            low,
            low,
            low_wide,
            low_wide,
            low,
            low,
            low,
            jax.ShapeDtypeStruct((rows, width), F32),
            jax.ShapeDtypeStruct(small.shape, BF16),
        ],
        scratch_shapes=[
            pltpu.VMEM((8, width), F32),
            pltpu.VMEM((8, hidden_width), F32),
            pltpu.VMEM((block, hidden_width), F32),
            pltpu.VMEM((8, width), F32),
            pltpu.VMEM((8, hidden_width), F32),
            pltpu.VMEM(win.shape, BF16),
            pltpu.VMEM(wout.shape, BF16),
            pltpu.SemaphoreType.DMA((2,)),
        ],
        compiler_params=pltpu.CompilerParams(vmem_limit_bytes=VMEM_LIMIT),
        name="row_stage",
    )(x, attended, cotangent, wo, small, win, wout)


def product_kernel(left_ref, right_ref, out_ref):
    out_ref[...] = dot_tn(left_ref[...], right_ref[...]).astype(BF16)


def product(left, right, block_m, block_n):
    depth, rows = left.shape
    cols = right.shape[1]
    return pl.pallas_call(
        product_kernel,
        grid=(rows // block_m, cols // block_n),
        in_specs=[
            pl.BlockSpec((depth, block_m), lambda i, j: (0, i)),
            pl.BlockSpec((depth, block_n), lambda i, j: (0, j)),
        ],
        out_specs=pl.BlockSpec((block_m, block_n), lambda i, j: (i, j)),
        out_shape=jax.ShapeDtypeStruct((rows, cols), BF16),
        compiler_params=pltpu.CompilerParams(vmem_limit_bytes=VMEM_LIMIT),
        name="weight_gradient",
    )(left, right)


def products_kernel(hidden, inner, active, feed_in, flat_in, branch_in, win, wo, wout, *scratch):
    feed, flat, branch, load = scratch
    step = pl.program_id(0)
    wide = pl.num_programs(0) // 2
    copies = [
        pltpu.make_async_copy(source, target, load.at[n])
        for n, (source, target) in enumerate(
            ((feed_in, feed), (flat_in, flat), (branch_in, branch))
        )
    ]

    @pl.when(step == 0)
    def _():
        for copy in copies:
            copy.start()

    @pl.when(step < wide)
    def _():
        win[...] = dot_tn(hidden[...], inner[...]).astype(BF16)

    @pl.when(step == wide - 1)
    def _():
        for copy in copies:
            copy.wait()

    @pl.when((step >= wide) & (step < 2 * wide))
    def _():
        wout[...] = dot_tn(active[...], feed[...]).astype(BF16)

    @pl.when(step == 2 * wide)
    def _():
        wo[...] = dot_tn(flat[...], branch[...]).astype(BF16)


def products(hidden, inner, active, feed, flat, branch):
    tokens, width = hidden.shape
    wide = inner.shape[1] // CHUNK
    low = lambda *shape: jax.ShapeDtypeStruct(shape, BF16)
    any_spec = pl.BlockSpec(memory_space=pl.ANY)
    return pl.pallas_call(
        products_kernel,
        grid=(2 * wide + 1,),
        in_specs=[
            pl.BlockSpec((tokens, width), lambda i: (0, 0), pipeline_mode=pl.Buffered(1)),
            pl.BlockSpec((tokens, CHUNK), lambda i: (0, jnp.clip(i, 0, wide - 1))),
            pl.BlockSpec((tokens, CHUNK), lambda i: (0, jnp.clip(i - wide, 0, wide - 1))),
            any_spec,
            any_spec,
            any_spec,
        ],
        out_specs=[
            pl.BlockSpec((width, CHUNK), lambda i: (0, jnp.clip(i, 0, wide - 1))),
            pl.BlockSpec((width, width), lambda i: (0, 0)),
            pl.BlockSpec((CHUNK, width), lambda i: (jnp.clip(i - wide, 0, wide - 1), 0)),
        ],
        out_shape=[
            low(width, inner.shape[1]),
            low(width, width),
            low(active.shape[1], width),
        ],
        scratch_shapes=[pltpu.VMEM((tokens, width), BF16)] * 3 + [pltpu.SemaphoreType.DMA((3,))],
        compiler_params=pltpu.CompilerParams(vmem_limit_bytes=VMEM_LIMIT),
        name="weight_gradients",
    )(hidden, inner, active, feed, flat, branch)


def input_kernel(first_ref, dq_ref, dk_ref, dv_ref, wq_ref, wk_ref, wv_ref, out_ref, vecg_ref, acc):
    step = pl.program_id(0)

    @pl.when(step == 0)
    def _():
        acc[...] = jnp.zeros_like(acc)

    out_ref[...] = (
        first_ref[...]
        + dot_nt(dq_ref[...], wq_ref[...])
        + dot_nt(dk_ref[...], wk_ref[...])
        + dot_nt(dv_ref[...], wv_ref[...])
    ).astype(BF16)
    acc[0:1] += jnp.sum(dq_ref[...].astype(F32), axis=0, keepdims=True)
    acc[1:2] += jnp.sum(dv_ref[...].astype(F32), axis=0, keepdims=True)

    @pl.when(step == pl.num_programs(0) - 1)
    def _():
        vecg_ref[:, 0:8] = collect(acc[...], vecg_ref.shape[0]).astype(BF16)
        vecg_ref[:, 8:16] = jnp.zeros((vecg_ref.shape[0], 8, LANES), BF16)


def input_stage(first, dq, dk, dv, wq, wk, wv, small_shape):
    rows, width = first.shape
    block = min(ROWS, rows)
    narrow = pl.BlockSpec((block, width), lambda i: (i, 0))
    whole = pl.BlockSpec((width, width), lambda i: (0, 0))
    return pl.pallas_call(
        input_kernel,
        grid=(rows // block,),
        in_specs=[narrow] * 4 + [whole] * 3,
        out_specs=[narrow, pl.BlockSpec(small_shape, lambda i: (0, 0, 0))],
        out_shape=[
            jax.ShapeDtypeStruct((rows, width), BF16),
            jax.ShapeDtypeStruct(small_shape, BF16),
        ],
        scratch_shapes=[pltpu.VMEM((8, width), F32)],
        compiler_params=pltpu.CompilerParams(vmem_limit_bytes=VMEM_LIMIT),
        name="input_stage",
    )(first, dq, dk, dv, wq, wk, wv)


PLAN_IN = ((1, 2, 5, 8, 11), (2, 3, 7, 10, 14), (3, 5, 9, 12, 15), (4, 7, 11, 13, 16),)
PLAN_OUT = ((9, 10, 13, 16, 19), (10, 12, 15, 17, 20), (12, 14, 17, 19, 22))
PLAN_O, PLAN_SMALL, PLAN_SMALL2 = (5, 9, 12, 15, 18), (5, 9, 12, 15, 18), (22, 23, 25, 27, 30)
PLAN_QKV = (
    (15, 16, 19, 21, 24),
    (19, 20, 22, 24, 27),
    (21, 22, 24, 26, 29),
    (22, 23, 25, 27, 30),
)
G_IN, G_OUT, G_O, G_SMALL, G_QKV, G_SMALL2 = 0, 1, 2, 3, 4, 8
UNITS = 12
FIRST = 9
STAGED = 5
BACK_STEPS = FIRST + UNITS + 5
BACK_PLAN = (
    [(G_IN, c * CHUNK, CHUNK, plan) for c, plan in enumerate(PLAN_IN)]
    + [(G_O, 0, CHUNK, PLAN_O), (G_SMALL, 0, LANES, PLAN_SMALL)]
    + [(G_OUT, c * GROUP, GROUP, plan) for c, plan in enumerate(PLAN_OUT)]
    + [(G_QKV + g, 0, 3 * w, plan) for g, (w, plan) in enumerate(zip((256, 256, 128, 128), PLAN_QKV))]
    + [(G_SMALL2, 0, LANES, PLAN_SMALL2)]
)
FETCHED = 6


def unit_of(step):
    u = jnp.clip(step - FIRST, 0, UNITS - 1)
    return u % 2, u // 2


def backward_kernel(sizes, *refs):
    hidden_in, inner_in, active_in, feed_in, flat_in, branch_in, small_in = refs[:7]
    (q_ref, k_ref, v_ref, o_ref, g_ref, lse_ref, x_in, wq_in, wk_in, wv_in, first_ref) = refs[7:18]
    outs, dx_ref = refs[18:27], refs[27]
    held1 = refs[28:32]
    broad, slim, small2, sums = refs[32:36]
    gots = got_levels(refs[36:72], 9)
    dq_all, dk_all, dv_all, away, far, x_t, x_v, wq_v, wk_v, wv_v, out_far = refs[72:83]
    load, send, recv, far_send, far_recv, bring, feed_sem = refs[83:]
    where = place()
    s, z, y, x = where
    step = pl.program_id(0)
    length = q_ref.shape[1]
    rows = dq_all.shape[0] * length
    chunks = [(a, 0, sizes[a][0], c, nc) for a, c, nc, _ in BACK_PLAN]

    def view(ref, cols=slice(None)):
        return lambda *at: ref.at[(*at, slice(None), cols)]

    terms = [view(broad.at[n % 2]) for n in range(STAGED)] + [view(small_in)]
    for _, c, nc, _ in BACK_PLAN[6:9]:
        terms.append(lambda s, *at, cols=slice(c, c + nc): out_far.at[(*at, slice(None), cols)])
    terms += [view(a.at[g]) for a in (broad, slim) for g in (0, 1)] + [view(small2)]
    held = list(held1) + [a.at[g, s] for a in (broad, slim) for g in (0, 1)] + [small2.at[s]]
    scatter = Scatter(terms, held, gots, outs, load, send, recv, chunks, where)
    copies = [
        pltpu.make_async_copy(a, b, bring.at[n])
        for n, (a, b) in enumerate(zip((x_in, wq_in, wk_in, wv_in), (x_v, wq_v, wk_v, wv_v)))
    ]

    operands = [
        pltpu.make_async_copy(a, b, feed_sem.at[n])
        for n, (a, b) in enumerate(
            ((hidden_in, dk_all), (feed_in, dv_all), (branch_in, dq_all), (flat_in, x_v))
        )
    ]

    def operand(n):
        source = inner_in if n < 4 else active_in
        cols = slice((n % 4) * CHUNK, (n % 4 + 1) * CHUNK)
        return pltpu.make_async_copy(source.at[:, :, cols], far.at[n % 2], feed_sem.at[4 + n % 2])

    def far_copies(u):
        m, p = unit_of(u + FIRST)
        lanes = pl.ds(pl.multiple_of(p * PAIR, PAIR), PAIR)
        target = device(1 - s, z, y, x)
        return [
            remote(
                away.at[u, n], far.at[n, m, :, lanes], far_send.at[u, n], far_recv.at[u, n], target
            )
            for n in (0, 1)
        ]

    @pl.when(step == 0)
    def _():
        operands[0].start()
        operand(0).start()
        operand(1).start()
        for copy in operands[1:] + copies[1:]:
            copy.start()
        greet(s, z, y, x)

    for n in range(BACK_STEPS):
        todo = [(t, i) for i, c in enumerate(BACK_PLAN) for t, at in enumerate(c[3]) if at == n]
        if todo or 2 <= n < 2 + STAGED:

            @pl.when(step == n)
            def _():
                if 2 <= n < 2 + STAGED:
                    scatter.release(n - 2)
                for t, i in sorted(todo, reverse=True):
                    scatter.stage(t, i)

    whole = lambda ref: ref[...].reshape(rows, CHUNK)
    for n in range(FIRST):

        @pl.when(step == n)
        def _():
            for at, which in ((0, 0), (4, 2), (4, 3), (5, 1)):
                if n == at:
                    operands[which].wait()
            if n != 4:
                operand(n - n // 5).wait()

    @pl.when(step < 4)
    def _():
        value = dot_tn(whole(dk_all), whole(far.at[step % 2])).astype(BF16)
        broad[step % 2] = value.reshape((2, 4, 2, 2) + sizes[G_O])

    @pl.when(step == 4)
    def _():
        value = dot_tn(x_v[...], whole(dq_all)).astype(BF16)
        broad[0] = value.reshape((2, 4, 2, 2) + sizes[G_O])
        copies[0].start()

    @pl.when((step > 4) & (step < FIRST))
    def _():
        c = step - 5
        value = dot_tn(whole(far.at[c % 2]), whole(dv_all)).astype(BF16)
        value = value.reshape((2, 2, 2) + sizes[G_OUT])
        half = pl.ds((c % 2) * 2, 2)

        @pl.when(s == c // 2)
        def _():
            held1[G_OUT][half] = value

        @pl.when(s != c // 2)
        def _():
            out_far[half] = value

    for n in range(FIRST):
        k = n - n // 5
        if n != 4 and k + 2 < 8:

            @pl.when(step == n)
            def _():
                operand(k + 2).start()

    @pl.when((step > FIRST) & (step < FIRST + UNITS))
    def _():
        for copy in far_copies(step - FIRST - 1):
            copy.start()

    @pl.when(step == FIRST)
    def _():
        copies[0].wait()
        x_t[...] = jnp.transpose(x_v[...])

    @pl.when((step >= FIRST) & (step < FIRST + UNITS))
    def _():
        m, p = unit_of(step)
        lanes = pl.ds(pl.multiple_of(p * PAIR, PAIR), PAIR)
        keys = k_ref[:, 0].reshape(-1, PAIR)
        values = v_ref[:, 0].reshape(-1, PAIR)
        dq, dk, dv = attend_pair_back(q_ref[0], keys, values, o_ref[0], g_ref[0], lse_ref[0, 0])
        dq_all[m, :, lanes] = dq
        dk_all[m, :, lanes] = dk[:length]
        dv_all[m, :, lanes] = dv[:length]
        away[step - FIRST, 0] = dk[length:]
        away[step - FIRST, 1] = dv[length:]

    @pl.when(step == FIRST + UNITS)
    def _():
        for copy in far_copies(UNITS - 1):
            copy.start()

    def products(to, g, unit, units, lane, lanes):
        for n in range(units):
            for copy in far_copies(unit + n):
                copy.wait_recv()
        cols = pl.ds(pl.multiple_of(lane, PAIR), lanes)
        for m in range(dq_all.shape[0]):
            for n, whole in enumerate((dk_all, dv_all)):
                whole[m, :, cols] = whole[m, :, cols] + far[n, m, :, cols]
        for n, whole in enumerate((dq_all, dk_all, dv_all)):
            value = dot_nn(x_t[...], whole[:, :, cols].reshape(rows, lanes)).astype(BF16)
            to[g, :, :, :, :, :, n * lanes : (n + 1) * lanes] = value.reshape(
                (2, 4, 2, 2) + (sizes[G_QKV][0], lanes)
            )

    @pl.when((step == FIRST + 5) | (step == FIRST + 9))
    def _():
        g = (step - FIRST - 5) // 4
        products(broad, g, 4 * g, 4, g * GROUP, GROUP)

    @pl.when((step == FIRST + 11) | (step == FIRST + 12))
    def _():
        g = step - FIRST - 11
        products(slim, g, 8 + 2 * g, 2, 2 * GROUP + g * PAIR, PAIR)

    @pl.when(step == FIRST + UNITS)
    def _():
        sums[...] = jnp.zeros_like(sums)
        for n, whole in enumerate((dq_all, dv_all)):
            total = jnp.sum(whole[...].astype(F32).reshape(rows, -1), axis=0, keepdims=True)
            sums[n : n + 1] = total
        small2[...] = jnp.zeros_like(small2)
        small2[:, :, :, :, 0:8] = (
            collect(sums[...], 32).astype(BF16).reshape((2, 4, 2, 2, 8, LANES))
        )
        for copy in copies[1:]:
            copy.wait()

    @pl.when(step > FIRST + UNITS)
    def _():
        block = first_ref.shape[0]
        r = step - FIRST - UNITS - 1
        per = length // block
        at = pl.ds(pl.multiple_of((r % per) * block, block), block)
        dx_ref[...] = (
            first_ref[...]
            + dot_nt(dq_all[r // per, at], wq_v[...])
            + dot_nt(dk_all[r // per, at], wk_v[...])
            + dot_nt(dv_all[r // per, at], wv_v[...])
        ).astype(BF16)

    @pl.when(step == BACK_STEPS - 1)
    def _():
        late = [(at, -t, i) for i, c in enumerate(BACK_PLAN) for t, at in enumerate(c[3])]
        for at, t, i in sorted(late):
            if at >= BACK_STEPS:
                scatter.stage(-t, i)
        for u in range(UNITS):
            for copy in far_copies(u):
                copy.wait_send()
        scatter.sent()


def backward_box(
    hidden, inner, active, feed, flat, branch, small, q, k, v, o, g, lse, tokens, wq, wk, wv, first
):
    micro, length, width = q.shape
    rows, hidden_width = inner.shape
    narrow, thin = (width // 32, width), (16, LANES)
    sizes = [(width // 32, hidden_width), (hidden_width // 32, width), narrow, thin]
    sizes += [(narrow[0], 3 * w) for w in (GROUP, GROUP, PAIR, PAIR)] + [thin]
    split = lambda a: a.reshape(micro, length, a.shape[1])
    given = [split(hidden), split(inner), split(active), split(feed), flat, split(branch)]
    given.append(small.reshape((2, 4, 2, 2) + thin))
    block = rows // 4

    def at(i):
        return unit_of(i)

    row = pl.BlockSpec((1, length, PAIR), lambda i: (at(i)[0], 0, at(i)[1]))
    col = pl.BlockSpec((2, 1, length, PAIR), lambda i: (0, at(i)[0], 0, at(i)[1]))
    log = pl.BlockSpec((1, 1, 2, length), lambda i: (at(i)[0], at(i)[1], 0, 0))
    flat = pl.BlockSpec((block, width), lambda i: (jnp.clip(i - FIRST - UNITS - 1, 0, 3), 0))
    any_spec = pl.BlockSpec(memory_space=pl.ANY)
    square = pltpu.VMEM((width, width), BF16)
    low = pltpu.VMEM((micro, length, width), BF16)
    outs = pl.pallas_call(
        functools.partial(backward_kernel, sizes),
        grid=(BACK_STEPS,),
        in_specs=[any_spec] * 7 + [row, col, col, row, row, log] + [any_spec] * 4 + [flat],
        out_specs=[pl.BlockSpec(size, lambda i: (0, 0)) for size in sizes] + [flat],
        out_shape=[jax.ShapeDtypeStruct(size, F32) for size in sizes]
        + [jax.ShapeDtypeStruct((rows, width), BF16)],
        scratch_shapes=[pltpu.VMEM((4, 2, 2) + size, BF16) for size in sizes[:4]]
        + [
            pltpu.VMEM((2, 2, 4, 2, 2) + sizes[G_QKV], BF16),
            pltpu.VMEM((2, 2, 4, 2, 2) + sizes[G_QKV + 2], BF16),
            pltpu.VMEM((2, 4, 2, 2) + thin, BF16),
            pltpu.VMEM((8, width), F32),
        ]
        + got_shapes(sizes)
        + [
            low,
            low,
            low,
            pltpu.VMEM((UNITS, 2, length, PAIR), BF16),
            pltpu.VMEM((2, micro, length, width), BF16),
            pltpu.VMEM((width, rows), BF16),
            pltpu.VMEM((rows, width), BF16),
            square,
            square,
            square,
            pltpu.VMEM((4, 2, 2) + sizes[G_OUT], BF16),
            pltpu.SemaphoreType.DMA((FETCHED,)),
            pltpu.SemaphoreType.DMA((len(BACK_PLAN), 7)),
            pltpu.SemaphoreType.DMA((len(BACK_PLAN), 7)),
            pltpu.SemaphoreType.DMA((UNITS, 2)),
            pltpu.SemaphoreType.DMA((UNITS, 2)),
            pltpu.SemaphoreType.DMA((4,)),
            pltpu.SemaphoreType.DMA((6,)),
        ],
        compiler_params=pltpu.CompilerParams(
            collective_id=2, has_side_effects=True, vmem_limit_bytes=VMEM_LIMIT
        ),
        name="backward_attention",
    )(*given, q, k, v, o, g, lse, tokens, wq, wk, wv, first)
    return outs[:9], outs[9]


def hand_out_kernel(*refs):
    (win, wout, wo, small) = refs[:4]
    qkv, small2, dx, dx_o, outs = refs[4:8], refs[8], refs[9], refs[10], refs[11:]
    dx_o[...] = dx[...]
    (wq_o, qb, wk_o, wv_o, vb, wo_o, ob, g1, s1, win_o, ib, wout_o, outb, g2, s2) = outs
    win_o[...] = win[...]
    wout_o[...] = wout[...]
    wo_o[...] = wo[...]
    first = 0
    for group in qkv:
        lanes = group.shape[1] // 3
        for n, target in enumerate((wq_o, wk_o, wv_o)):
            target[:, first : first + lanes] = group[:, n * lanes : (n + 1) * lanes]
        first += lanes
    piece = qb.shape[1]
    qb[...] = small2[0:1, :piece]
    vb[...] = small2[1:2, :piece]
    for row, target in zip(range(2, 8), (ob, g1, s1, outb, g2, s2)):
        target[...] = small[row : row + 1, :piece]
    ib[...] = small[8:9, : ib.shape[1]]


def hand_out(win, wout, wo, small, qkv, small2, dx, piece, wide):
    vmem_spec = pl.BlockSpec(memory_space=pltpu.VMEM)
    line = jax.ShapeDtypeStruct((1, piece), F32)
    like = lambda a: jax.ShapeDtypeStruct(a.shape, F32)
    shapes = [like(wo), line, like(wo), like(wo), line, like(wo), line, line, line, like(win)]
    shapes += [jax.ShapeDtypeStruct((1, wide), F32), like(wout), line, line, line]
    outs = pl.pallas_call(
        hand_out_kernel,
        in_specs=[vmem_spec] * 10,
        out_specs=[vmem_spec] * 16,
        out_shape=[jax.ShapeDtypeStruct(dx.shape, dx.dtype)] + shapes,
        compiler_params=pltpu.CompilerParams(vmem_limit_bytes=VMEM_LIMIT),
        name="hand_out",
    )(win, wout, wo, small, *qkv, small2, dx)
    return outs[0], [a.reshape(-1) if a.shape[0] == 1 else a for a in outs[1:]]


def body(
    inputs,
    cotangent,
    query_weight,
    query_bias,
    key_weight,
    value_weight,
    value_bias,
    output_weight,
    output_bias,
    first_gain,
    first_shift,
    inner_weight,
    inner_bias,
    outer_weight,
    outer_bias,
    second_gain,
    second_shift,
):
    micro, _, length, width = inputs.shape
    devices = lax.axis_size(("seq", "grp"))
    piece, wide = query_bias.shape[0], inner_bias.shape[0]
    boxed = lax.axis_size("seq") == 2 and lax.axis_size("grp") == 16 and piece % 8 == 0
    own = inputs[:, 0]
    tokens = own.reshape(-1, width)
    upstream = cotangent[:, 0].reshape(-1, width)
    small = jnp.zeros((16, LANES), BF16)
    for row, vector in enumerate(
        (
            query_bias,
            value_bias,
            output_bias,
            first_gain,
            first_shift,
            outer_bias,
            second_gain,
            second_shift,
            inner_bias,
        )
    ):
        small += jnp.pad(vector[None], ((row, 15 - row), (0, LANES - vector.shape[0])))
    shards = (
        small,
        query_weight,
        key_weight,
        value_weight,
        output_weight,
        inner_weight,
        outer_weight,
    )
    if boxed:
        fulls, made = forward_box(shards, own)
        small, wq, wk, wv, wo, win, wout = fulls
        queries, keys, values, attended, lse = made
    else:
        fulls = [lax.all_gather(a, ("seq", "grp"), axis=0, tiled=True) for a in shards]
        small, wq, wk, wv, wo, win, wout = fulls
        small = small.reshape(devices, 16, LANES)
        all_rows = lax.all_gather(own, "seq", axis=0)
        queries, keys, values = project(own, all_rows, wq, wk, wv, small)
        attended, lse = attend(queries, keys, values)
    flat = attended.reshape(-1, width)
    (
        layer_out,
        hidden_low,
        active,
        inner_grad,
        feed_grad,
        branch_grad,
        mixed_grad,
        first_grad,
        small_grad,
    ) = row_stage(tokens, flat, upstream, wo, win, wout, small)
    mixed_grad = mixed_grad.reshape(micro, length, width)
    if boxed:
        summed, input_grad = backward_box(
            hidden_low,
            inner_grad,
            active,
            feed_grad,
            flat,
            branch_grad,
            small_grad,
            queries,
            keys,
            values,
            attended,
            mixed_grad,
            lse,
            tokens,
            wq,
            wk,
            wv,
            first_grad,
        )
    else:
        win_grad, wo_grad, wout_grad = products(
            hidden_low, inner_grad, active, feed_grad, flat, branch_grad
        )
        dq, dk, dv = attend_back(queries, keys, values, attended, mixed_grad, lse)
        dk = lax.psum_scatter(dk, "seq", scatter_dimension=0)
        dv = lax.psum_scatter(dv, "seq", scatter_dimension=0)
        dq, dk, dv = (a.reshape(-1, width) for a in (dq, dk, dv))
        input_grad, small2_grad = input_stage(
            first_grad, dq, dk, dv, wq, wk, wv, (devices, 16, LANES)
        )
        groups = [
            jnp.concatenate([a[:, c : c + w] for a in (dq, dk, dv)], axis=1)
            for c, w in ((0, GROUP), (GROUP, GROUP), (2 * GROUP, PAIR), (2 * GROUP + PAIR, PAIR))
        ]
        terms = [win_grad, wout_grad, wo_grad, small_grad.reshape(-1, LANES)]
        terms += [product(tokens, a, 768, a.shape[1]) for a in groups]
        terms.append(small2_grad.reshape(-1, LANES))
        summed = [
            lax.psum_scatter(a.astype(F32), ("seq", "grp"), scatter_dimension=0, tiled=True)
            for a in terms
        ]
        summed = lax.optimization_barrier(summed)
    input_grad, grads = hand_out(*summed[:4], summed[4:8], summed[8], input_grad, piece, wide)
    return (layer_out.reshape(inputs.shape), input_grad.reshape(inputs.shape)) + tuple(grads)


def solution(mesh):
    rows = P(("seq", "grp"), None)
    line = P(("seq", "grp"))
    tokens = P(None, "grp", "seq", None)
    return jax.shard_map(
        body,
        mesh=mesh,
        in_specs=(
            tokens,
            tokens,
            rows,
            line,
            rows,
            rows,
            line,
            rows,
            line,
            line,
            line,
            rows,
            line,
            rows,
            line,
            line,
            line,
        ),
        out_specs=(
            tokens,
            tokens,
            rows,
            line,
            rows,
            rows,
            line,
            rows,
            line,
            line,
            line,
            rows,
            line,
            rows,
            line,
            line,
            line,
        ),
        check_vma=False,
    )
```
